128 devices in a mesh: gx: 8 (over y, core), gy: 16 (over z, x).
Axes of the slice: x: 4, y: 4, z: 4, core: 2. Of those that a mesh axis runs over, the one named last changes fastest.
Arguments:
- patches: bfloat16 [6144, 1408], P(('gx', 'gy')), may hold values from -6 to 6
- grids: int32 [16, 2], replicated, may hold values from 4 to 12, as said below
- text_ids: int32 [4096], P('gx'), may hold values from 0 to 31999
- positions: int32 [1536], replicated, may hold values from -1 to 2047, as said below
- lengths: int32 [8], replicated, may hold values from 1 to 3072, 4096 in all
- text_table: bfloat16 [32000, 1408], P('gy'), may hold values from -6 to 6
- vit_norm1: float32 [1408], replicated, may hold values from 0.5 to 1.5
- vit_qkv: bfloat16 [1408, 3, 1408], P('gx', None, 'gy'), may hold values from -0.15625 to 0.15625
- vit_out: bfloat16 [1408, 1408], P('gx', 'gy'), may hold values from -0.15625 to 0.15625
- vit_norm2: float32 [1408], replicated, may hold values from 0.5 to 1.5
- vit_fc1: bfloat16 [1408, 6144], P('gx', 'gy'), may hold values from -0.15625 to 0.15625
- vit_fc2: bfloat16 [1408, 6144], P('gx', 'gy'), may hold values from -0.078125 to 0.078125
- merge_norm: float32 [4, 1408], replicated, may hold values from 0.5 to 1.5
- merge_proj: bfloat16 [1408, 4, 1408], P('gx', None, 'gy'), may hold values from -0.078125 to 0.078125
- dec_norm1: float32 [1408], replicated, may hold values from 0.5 to 1.5
- dec_qkv: bfloat16 [1408, 3, 1408], P('gx', None, 'gy'), may hold values from -0.15625 to 0.15625
- dec_out: bfloat16 [1408, 1408], P('gx', 'gy'), may hold values from -0.15625 to 0.15625
- dec_norm2: float32 [1408], replicated, may hold values from 0.5 to 1.5
- dec_fc1: bfloat16 [1408, 6144], P('gx', 'gy'), may hold values from -0.15625 to 0.15625
- dec_fc2: bfloat16 [1408, 6144], P('gx', 'gy'), may hold values from -0.078125 to 0.078125
- next_norm: float32 [1408], replicated, may hold values from 0.5 to 1.5
- next_qkv: bfloat16 [1408, 3, 1408], P('gx', None, 'gy'), may hold values from -0.15625 to 0.15625
Outputs:
- next_triple: bfloat16 [4096, 3, 1408], P(('gx', 'gy'))
The draws below stay inside these ranges and needn't reach their ends.
Inputs may be any that keep to these rules, and one draw needn't show every extreme that they name: `grids`: row i gives image i's merged grid (rows from (9) // 2 to 8, columns from (13) // 2 to 12); images i * 2 to i * 2 + 1 belong to index i of gx; in every draw all images of some index of gx have 8 x 12, filling its 768 patch slots. Each index of gx's merged slots that belong to images come first; they hold distinct prompt positions that rise with the slot's global index; the other slots hold -1.
All inputs are finite; a program needn't handle non-finite values.
Results may differ from the reference program's by a relative error of at most 0.023.
Values may be sent and summed in bfloat16 or wider, within the bound.
No kernel may reach another device: no remote copies, remote signals or barrier semaphores. Data moves between devices by JAX's collectives and lax.ppermute only.
A program may use at most 64 MiB of HBM per device.

```python
import math
import jax
import jax.numpy as jnp
import numpy as np
from jax import lax

D = 1408
HEADS = 16
HEAD_DIM = 88
FF = 6144
VOCAB = 32000
MGRID_H = 8
MGRID_W = 12
REQS = 8
IMG_GX = 2
PATCH_GX = 768
MERGE_GX = 192
IMAGES = 16
PATCHES = 6144
MERGE_TOTAL = 1536
SEQ = 4096
N_GX = 8


def grid_table(key):
    grid_key = jax.random.fold_in(key, 11)
    key_rows, key_cols, key_full = jax.random.split(grid_key, 3)
    grid_rows = jax.random.randint(key_rows, (IMAGES,), (MGRID_H + 1) // 2, MGRID_H + 1)
    grid_cols = jax.random.randint(key_cols, (IMAGES,), (MGRID_W + 1) // 2, MGRID_W + 1)
    full_index = jax.random.randint(key_full, (), 0, IMAGES // IMG_GX)
    owner = jnp.arange(IMAGES) // IMG_GX
    grid_rows = jnp.where(owner == full_index, MGRID_H, grid_rows)
    grid_cols = jnp.where(owner == full_index, MGRID_W, grid_cols)
    return jnp.stack([grid_rows, grid_cols], axis=1).astype(jnp.int32)


def draw_grids(key, part):
    return grid_table(key)


def draw_positions(key, part):
    table = grid_table(key)
    counts = (table[:, 0] * table[:, 1]).reshape(IMAGES // IMG_GX, IMG_GX)
    live_total = jnp.sum(counts, axis=1)
    slot_index = jnp.arange(MERGE_GX)
    is_live = (slot_index[None, :] < live_total[:, None]).reshape(MERGE_TOTAL)
    chosen = jnp.sort(jax.random.permutation(jax.random.fold_in(key, 23), SEQ // 2)[:MERGE_TOTAL])
    global_slot = jnp.arange(MERGE_TOTAL)
    last_live = jnp.max(jnp.where(is_live, global_slot, -1))
    chosen = jnp.where(global_slot == last_live, SEQ // 2 - 1, chosen)
    return jnp.where(is_live, chosen, -1).astype(jnp.int32)


def touch_ends(values, own_key, least, top_value):
    longest = values.shape.index(max(values.shape))
    spots = []
    for shift in (0, 1):
        where = [jax.random.randint(jax.random.fold_in(own_key, axis), (), 0, length) for axis, length in enumerate(values.shape)]
        where[longest] = (where[longest] + shift) % values.shape[longest]
        spots.append(tuple(where))
    return values.at[spots[0]].set(least).at[spots[1]].set(top_value)


def block_levels(stream_key, extent, cuts, low, top_value):
    def one(axis_at, blocks):
        heights = jax.random.uniform(jax.random.fold_in(jax.random.fold_in(stream_key, 6), axis_at), (blocks,), jnp.float32, low / len(cuts), top_value / len(cuts))
        return jnp.repeat(jnp.exp(heights), extent[axis_at] // blocks).reshape((-1,) + (1,) * (len(extent) - axis_at - 1))

    gain = one(*cuts[0])
    for cut in cuts[1:]:
        gain = gain * one(*cut)
    return gain


def rank_table(amount, lean):
    weights = [(1 << 20) // math.isqrt(grade ** lean) + 1 for grade in range(1, amount + 1)]
    scale = 1 + sum(weights) // (1 << 30)
    return np.cumsum(np.array([max(1, weight // scale) for weight in weights]))


def ranked_ids(own_key, dims, number_of, skew):
    grid = rank_table(number_of, skew)
    pick = jax.random.randint(jax.random.fold_in(own_key, 1), dims, 0, int(grid[number_of - 1]))
    rank = jnp.searchsorted(jnp.asarray(grid, jnp.int32), pick, side="right")
    return jax.random.permutation(jax.random.fold_in(own_key, 2), number_of)[rank].astype(jnp.int32)


def split_up(amount, total, most, lean):
    portions = [(1 << 20) // math.isqrt(rank ** lean) + 1 for rank in range(2, amount + 1)]
    surplus, holding = total - most - (amount - 1), [1] * (amount - 1)
    while surplus > 0:
        movable = [i for i in range(amount - 1) if holding[i] < most]
        whole, budget = sum([portions[i] for i in movable]), surplus
        for i in movable:
            more = min(most - holding[i], max(1, budget * portions[i] // whole), surplus)
            holding[i] = holding[i] + more
            surplus = surplus - more
    return np.array([most] + holding)


def ragged(key, number_of, total, limit, lean):
    if number_of == 2:
        one = jax.random.randint(key, (), max(1, total - limit), min(limit, total - 1) + 1)
        return jnp.stack([one, total - one])
    tallies = jnp.asarray(split_up(number_of, total, limit, lean), jnp.int32)
    couples = (number_of - 1) // 2
    source_of, sink = tallies[1:1 + 2 * couples:2], tallies[2:2 + 2 * couples:2]
    margin = jnp.minimum(source_of - 1, limit - sink)
    moved = jax.random.randint(jax.random.fold_in(key, 1), (couples,), 0, 1 << 20) % (margin + 1)
    tallies = tallies.at[1:1 + 2 * couples:2].set(source_of - moved).at[2:2 + 2 * couples:2].set(sink + moved)
    return tallies[jax.random.permutation(jax.random.fold_in(key, 2), number_of)]


def bell_draw(stream_key, dims, scale, reach, pieces=(), kind=jnp.bfloat16):
    loudness = block_levels(stream_key, dims, pieces, -0.22, 0.18) if pieces else 1.0
    result = jax.random.normal(stream_key, dims, jnp.float32) * scale * loudness
    return jnp.minimum(jnp.maximum(result, -reach), reach).astype(kind)


def setup_inputs(seed: int = 0) -> dict:
    streams_of = jax.random.split(jax.random.key(seed), 23)
    patches = bell_draw(streams_of[0], (PATCHES, D), 1.0, 6.0, ((0, 128),))
    grids = draw_grids(jax.random.fold_in(streams_of[22], 71), 0)
    text_ids = touch_ends(ranked_ids(streams_of[2], (SEQ,), VOCAB, 2), jax.random.fold_in(streams_of[2], 3), 0, VOCAB - 1).astype(jnp.int32)
    positions = draw_positions(jax.random.fold_in(streams_of[22], 71), 0)
    lengths = ragged(streams_of[4], REQS, SEQ, 3 * SEQ // 4, 2).astype(jnp.int32)
    text_table = bell_draw(streams_of[5], (VOCAB, D), 1.0, 6.0, ((0, 16),))
    vit_norm1 = jnp.clip(1.0 + 0.1 * jax.random.normal(streams_of[6], (D,), jnp.float32), 0.5, 1.5)
    vit_qkv = bell_draw(streams_of[7], (D, 3, D), D ** -0.5, 0.15625, ((0, 8), (2, 16)))
    vit_out = bell_draw(streams_of[8], (D, D), D ** -0.5, 0.15625, ((0, 8), (1, 16)))
    vit_norm2 = jnp.clip(1.0 + 0.1 * jax.random.normal(streams_of[9], (D,), jnp.float32), 0.5, 1.5)
    vit_fc1 = bell_draw(streams_of[10], (D, FF), D ** -0.5, 0.15625, ((0, 8), (1, 16)))
    vit_fc2 = bell_draw(streams_of[11], (D, FF), FF ** -0.5, 0.078125, ((0, 8), (1, 16)))
    merge_norm = jnp.clip(1.0 + 0.1 * jax.random.normal(streams_of[12], (4, D), jnp.float32), 0.5, 1.5)
    merge_proj = bell_draw(streams_of[13], (D, 4, D), (4 * D) ** -0.5, 0.078125, ((0, 8), (2, 16)))
    dec_norm1 = jnp.clip(1.0 + 0.1 * jax.random.normal(streams_of[14], (D,), jnp.float32), 0.5, 1.5)
    dec_qkv = bell_draw(streams_of[15], (D, 3, D), D ** -0.5, 0.15625, ((0, 8), (2, 16)))
    dec_out = bell_draw(streams_of[16], (D, D), D ** -0.5, 0.15625, ((0, 8), (1, 16)))
    dec_norm2 = jnp.clip(1.0 + 0.1 * jax.random.normal(streams_of[17], (D,), jnp.float32), 0.5, 1.5)
    dec_fc1 = bell_draw(streams_of[18], (D, FF), D ** -0.5, 0.15625, ((0, 8), (1, 16)))
    dec_fc2 = bell_draw(streams_of[19], (D, FF), FF ** -0.5, 0.078125, ((0, 8), (1, 16)))
    next_norm = jnp.clip(1.0 + 0.1 * jax.random.normal(streams_of[20], (D,), jnp.float32), 0.5, 1.5)
    next_qkv = bell_draw(streams_of[21], (D, 3, D), D ** -0.5, 0.15625, ((0, 8), (2, 16)))
    return dict(patches=patches, grids=grids, text_ids=text_ids, positions=positions, lengths=lengths, text_table=text_table, vit_norm1=vit_norm1, vit_qkv=vit_qkv, vit_out=vit_out, vit_norm2=vit_norm2, vit_fc1=vit_fc1, vit_fc2=vit_fc2, merge_norm=merge_norm, merge_proj=merge_proj, dec_norm1=dec_norm1, dec_qkv=dec_qkv, dec_out=dec_out, dec_norm2=dec_norm2, dec_fc1=dec_fc1, dec_fc2=dec_fc2, next_norm=next_norm, next_qkv=next_qkv)


norm_eps = 1e-06
masked_score = -1e+30

def layer_norm(values, gain_row):
    values = values.astype(jnp.float32)
    centre = values - lax.optimization_barrier(jnp.mean(values, axis=-1, keepdims=True))
    spread = lax.optimization_barrier(jnp.mean(centre * centre, axis=-1, keepdims=True))
    return (centre * lax.rsqrt(spread + norm_eps) * gain_row).astype(jnp.bfloat16)

def rms_norm(values, gain_row):
    values = values.astype(jnp.float32)
    square = lax.optimization_barrier(jnp.mean(values * values, axis=-1, keepdims=True))
    return (values * lax.rsqrt(square + norm_eps) * gain_row).astype(jnp.bfloat16)

def image_bounds(grid_rows):
    merged_count = grid_rows[:, 0] * grid_rows[:, 1]
    merged_end = jnp.cumsum(merged_count).astype(jnp.int32)
    return (merged_count.astype(jnp.int32), merged_end)

def patch_images(grid_rows, patch_slots):
    merged_count, merged_end = image_bounds(grid_rows)
    slot_index = jnp.arange(patch_slots, dtype=jnp.int32)
    return lax.optimization_barrier(jnp.sum((slot_index[:, None] >= 4 * merged_end[None, :]).astype(jnp.int32), axis=1))

def merge_sources(grid_rows, merge_slots):
    image_count = grid_rows.shape[0]
    merged_count, merged_end = image_bounds(grid_rows)
    merged_start = merged_end - merged_count
    slot_index = jnp.arange(merge_slots, dtype=jnp.int32)
    image_of = lax.optimization_barrier(jnp.sum((slot_index[:, None] >= merged_end[None, :]).astype(jnp.int32), axis=1))
    is_live = image_of < image_count
    picked = (jnp.minimum(image_of, image_count - 1)[:, None] == jnp.arange(image_count, dtype=jnp.int32)[None, :]).astype(jnp.int32)
    col_count = lax.optimization_barrier(jnp.sum(picked * grid_rows[None, :, 1], axis=1))
    first_slot = lax.optimization_barrier(jnp.sum(picked * merged_start[None, :], axis=1))
    local_slot = slot_index - first_slot
    grid_row = local_slot // col_count
    grid_col = local_slot % col_count
    base_row = 4 * first_slot + 4 * grid_row * col_count + 2 * grid_col
    offsets = jnp.stack([jnp.zeros_like(col_count), jnp.ones_like(col_count), 2 * col_count, 2 * col_count + 1], axis=1)
    return jnp.where(is_live[:, None], base_row[:, None] + offsets, 0).astype(jnp.int32)

def head_attention(queries, key_rows, value_rows, allowed):
    scores = jnp.dot(queries, key_rows.T, preferred_element_type=jnp.float32) * HEAD_DIM ** (-0.5)
    exp_scores = jnp.where(allowed, jnp.exp(scores), 0.0)
    denominator = lax.optimization_barrier(jnp.sum(exp_scores, axis=1, keepdims=True))
    weighted = jnp.dot(exp_scores.astype(jnp.bfloat16), value_rows, preferred_element_type=jnp.float32)
    return (weighted / denominator).astype(jnp.bfloat16)

def many_heads(queries, key_rows, value_rows, allowed):

    def one_head(triple_in):
        return head_attention(triple_in[0], triple_in[1], triple_in[2], allowed)
    outputs = lax.map(one_head, (queries.transpose(1, 0, 2), key_rows.transpose(1, 0, 2), value_rows.transpose(1, 0, 2)))
    return outputs.transpose(1, 0, 2).reshape(queries.shape[0], -1)

def feed_forward(stream, gain_row, fc_in, fc_back, norm_fn):
    hidden = jax.nn.gelu(jnp.dot(norm_fn(stream, gain_row), fc_in, preferred_element_type=jnp.float32), approximate=False).astype(jnp.bfloat16)
    back = lax.dot_general(hidden, fc_back, (((1,), (1,)), ((), ())), preferred_element_type=jnp.float32)
    return (stream.astype(jnp.float32) + back).astype(jnp.bfloat16)

def reference(patches, grids, text_ids, positions, lengths, text_table, vit_norm1, vit_qkv, vit_out, vit_norm2, vit_fc1, vit_fc2, merge_norm, merge_proj, dec_norm1, dec_qkv, dec_out, dec_norm2, dec_fc1, dec_fc2, next_norm, next_qkv):
    grid_groups = grids.reshape(N_GX, IMG_GX, 2)
    normed = layer_norm(patches, vit_norm1)
    triple = jnp.dot(normed, vit_qkv.reshape(D, 3 * D), preferred_element_type=jnp.float32).astype(jnp.bfloat16)
    triple = triple.reshape(N_GX, PATCH_GX, 3, HEADS, HEAD_DIM)

    def patch_ids(grid_rows):
        return patch_images(grid_rows, PATCH_GX)
    image_ids = jax.vmap(patch_ids)(grid_groups)

    def group_attention(inputs):
        block, class_ids = inputs
        allowed = class_ids[:, None] == class_ids[None, :]
        return many_heads(block[:, 0], block[:, 1], block[:, 2], allowed)
    attended = lax.map(group_attention, (triple, image_ids)).reshape(PATCHES, D)
    vit_mid = (patches.astype(jnp.float32) + jnp.dot(attended, vit_out, preferred_element_type=jnp.float32)).astype(jnp.bfloat16)
    vit_final = feed_forward(vit_mid, vit_norm2, vit_fc1, vit_fc2, layer_norm)

    def merge_ids(grid_rows):
        return merge_sources(grid_rows, MERGE_GX)
    sources = jax.vmap(merge_ids)(grid_groups)
    sources = (sources + PATCH_GX * jnp.arange(N_GX, dtype=jnp.int32)[:, None, None]).reshape(MERGE_TOTAL * 4)
    merged = jnp.take(vit_final, sources, axis=0).reshape(MERGE_TOTAL, 4 * D)
    merged_normed = layer_norm(merged, merge_norm.reshape(4 * D))
    proj_flat = merge_proj.transpose(1, 0, 2).reshape(4 * D, D)
    projected = jnp.dot(merged_normed, proj_flat, preferred_element_type=jnp.float32).astype(jnp.bfloat16)
    seq_index = jnp.arange(SEQ, dtype=jnp.int32)
    matches = positions[None, :] == seq_index[:, None]
    is_image = jnp.any(matches, axis=1)
    slot_index = jnp.arange(MERGE_TOTAL, dtype=jnp.int32)
    source_slot = lax.optimization_barrier(jnp.sum(jnp.where(matches, slot_index[None, :], 0), axis=1)).astype(jnp.int32)
    embedded = jnp.where(is_image[:, None], jnp.take(projected, source_slot, axis=0), jnp.take(text_table, text_ids, axis=0))
    dec_triple = jnp.dot(rms_norm(embedded, dec_norm1), dec_qkv.reshape(D, 3 * D), preferred_element_type=jnp.float32).astype(jnp.bfloat16)
    dec_triple = dec_triple.reshape(SEQ, 3, HEADS, HEAD_DIM)
    bounds = jnp.cumsum(lengths).astype(jnp.int32)
    request = lax.optimization_barrier(jnp.sum((seq_index[:, None] >= bounds[None, :]).astype(jnp.int32), axis=1))
    allowed = (request[:, None] == request[None, :]) & (seq_index[None, :] <= seq_index[:, None])
    dec_attended = many_heads(dec_triple[:, 0], dec_triple[:, 1], dec_triple[:, 2], allowed)
    dec_mid = (embedded.astype(jnp.float32) + jnp.dot(dec_attended, dec_out, preferred_element_type=jnp.float32)).astype(jnp.bfloat16)
    dec_final = feed_forward(dec_mid, dec_norm2, dec_fc1, dec_fc2, rms_norm)
    next_triple = jnp.dot(rms_norm(dec_final, next_norm), next_qkv.reshape(D, 3 * D), preferred_element_type=jnp.float32).astype(jnp.bfloat16)
    return next_triple.reshape(SEQ, 3, D)
```

```python
import functools
import math

import jax
import jax.numpy as jnp
from jax import lax
from jax.experimental import pallas as pl
from jax.experimental.pallas import tpu as pltpu
from jax.sharding import Mesh, PartitionSpec as P

HEAD_DIM = 88
LANES = 128
SUB = 4
NORM_EPS = 1e-06
F32 = jnp.float32
BF16 = jnp.bfloat16
VMEM_LIMIT = 50 * 1024 * 1024


def merge_sources(grid_rows, merge_slots):
    image_count = grid_rows.shape[0]
    merged_count = grid_rows[:, 0] * grid_rows[:, 1]
    merged_end = jnp.cumsum(merged_count)
    merged_start = merged_end - merged_count
    slot_index = jnp.arange(merge_slots, dtype=jnp.int32)
    image_of = jnp.sum((slot_index[:, None] >= merged_end[None, :]).astype(jnp.int32), axis=1)
    is_live = image_of < image_count
    picked = (
        jnp.minimum(image_of, image_count - 1)[:, None]
        == jnp.arange(image_count, dtype=jnp.int32)[None, :]
    ).astype(jnp.int32)
    col_count = jnp.sum(picked * grid_rows[None, :, 1], axis=1)
    first_slot = jnp.sum(picked * merged_start[None, :], axis=1)
    local_slot = slot_index - first_slot
    grid_row = local_slot // col_count
    grid_col = local_slot % col_count
    base_row = 4 * first_slot + 4 * grid_row * col_count + 2 * grid_col
    offsets = jnp.stack(
        [jnp.zeros_like(col_count), jnp.ones_like(col_count), 2 * col_count, 2 * col_count + 1],
        axis=1,
    )
    sources = jnp.where(is_live[:, None], base_row[:, None] + offsets, 0)
    return sources, image_of, is_live


def shift_in(axis, values, step):
    return lax.ppermute(values, axis, [(i, (i + step) % SUB) for i in range(SUB)])


def gather_four(axis, values):
    return [values] + [shift_in(axis, values, k) for k in range(1, SUB)]


def exchange_four(axis, pieces):
    return [pieces[0]] + [shift_in(axis, pieces[k], k) for k in range(1, SUB)]


SMEM = pl.BlockSpec(memory_space=pltpu.SMEM)
VMEM = pl.BlockSpec(memory_space=pltpu.VMEM)


def shape(*dims, dtype=BF16):
    return jax.ShapeDtypeStruct(dims, dtype)


def call(body, outs, args, specs=None, grid=None, out_specs=None, scratch=(), flops=0, name=None):
    if specs is None:
        specs = [VMEM] * len(args)
    if out_specs is None:
        out_specs = jax.tree.map(lambda _: VMEM, outs)
    moved = sum(math.prod(a.shape) * a.dtype.itemsize for a in args)
    kwargs = {} if grid is None else {"grid": grid}
    return pl.pallas_call(
        body,
        out_shape=outs,
        in_specs=specs,
        out_specs=out_specs,
        scratch_shapes=list(scratch),
        cost_estimate=pl.CostEstimate(flops=flops, bytes_accessed=moved, transcendentals=0),
        compiler_params=pltpu.CompilerParams(vmem_limit_bytes=VMEM_LIMIT),
        name=name,
        **kwargs,
    )(*args)


def back(own, step):
    return lax.rem(own + (SUB - step), SUB)


def ahead(own, step):
    return lax.rem(own + step, SUB)


def dot(left, right):
    return jnp.dot(left, right, preferred_element_type=F32)


def layer_norm_rows(values, gain):
    centre = values - jnp.mean(values, axis=-1, keepdims=True)
    spread = jnp.mean(centre * centre, axis=-1, keepdims=True)
    return (centre * lax.rsqrt(spread + NORM_EPS) * gain).astype(BF16)


def rms_norm_rows(values, gain):
    square = jnp.mean(values * values, axis=-1, keepdims=True)
    return (values * lax.rsqrt(square + NORM_EPS) * gain).astype(BF16)


def gelu(values):
    return 0.5 * values * (1.0 + lax.erf(values * (2.0**-0.5)))


def vit_attention_body(place, rows, weight, gain, source, query_class, key_class, *rest):
    outs, (triple, attended) = rest[:SUB], rest[SUB:]
    own_z = place[1]
    slots = rows.shape[0]
    step = slots // 4
    for at in range(0, slots, step):
        normed = layer_norm_rows(rows[at : at + step, :].astype(F32), gain[...])
        triple[at : at + step, :] = dot(normed, weight[...]).astype(BF16)
    for at in range(0, slots, step):
        chosen = (
            source[at : at + step, :] == lax.broadcasted_iota(jnp.int32, (step, slots), 1)
        ).astype(BF16)
        attended[at : at + step, :] = dot(chosen, triple[...]).astype(BF16)
    keys = attended[:, LANES : 2 * LANES]
    values = attended[:, 2 * LANES :]
    for at in range(0, slots, step):
        scores = lax.dot_general(
            attended[at : at + step, :LANES],
            keys,
            (((1,), (1,)), ((), ())),
            preferred_element_type=F32,
        ) * HEAD_DIM ** (-0.5)
        allowed = query_class[at : at + step, :] == key_class[...]
        exp_scores = jnp.where(allowed, jnp.exp(scores), 0.0)
        denominator = jnp.sum(exp_scores, axis=1, keepdims=True)
        weighted = dot(exp_scores.astype(BF16), values)
        triple[at : at + step, :LANES] = (weighted / denominator).astype(BF16)
    share = slots // SUB
    for k in range(SUB):
        start = pl.multiple_of(ahead(own_z, k) * share, share)
        outs[k][...] = triple[pl.ds(start, share), :LANES]


def pick_rows_body(source, rows, out):
    chosen = (source[...] == lax.broadcasted_iota(jnp.int32, (source.shape[0], rows.shape[0]), 1)).astype(BF16)
    out[...] = dot(chosen, rows[...]).astype(BF16)


def join_heads(blocks):
    return jnp.concatenate([block[:, :HEAD_DIM] for block in blocks], axis=1)


def out_projection_body(place, a0, a1, a2, a3, weight, out, heads, left):
    own_z, own_q = place[1], place[2]
    step = pl.program_id(0)

    @pl.when(step == 0)
    def _():
        for k, ref in enumerate((a0, a1, a2, a3)):
            for m in range(SUB):
                heads[back(own_z, m) * SUB + back(own_q, k)] = ref[:, m * LANES : (m + 1) * LANES]
        left[...] = join_heads([heads[h] for h in range(SUB * SUB)])

    out[...] = dot(left[...], weight[0]).astype(BF16)


def feed_forward_body(norm, parts, share, place, o0, o1, o2, o3, stream, gain, weight, *rest):
    outs, mid_out, (heads, mid, normed, total) = rest[:SUB], rest[SUB], rest[SUB + 1 :]
    own_q = place[2]
    step = pl.program_id(0)
    rows = stream.shape[0]
    hidden_width = weight.shape[2] // 2

    @pl.when(step == 0)
    def _():
        for k, ref in enumerate((o0, o1, o2, o3)):
            for z in range(SUB):
                heads[z * SUB + back(own_q, k)] = ref[:, z * LANES : (z + 1) * LANES]
        for at in range(0, rows, parts):
            added = join_heads([heads[h, at : at + parts, :] for h in range(SUB * SUB)])
            summed = (stream[at : at + parts, :].astype(F32) + added.astype(F32)).astype(BF16)
            mid[at : at + parts, :] = summed
            normed[at : at + parts, :] = norm(summed.astype(F32), gain[...])

    hidden = gelu(dot(normed[...], weight[0, :, :hidden_width])).astype(BF16)
    down = lax.dot_general(
        hidden,
        weight[0, :, hidden_width:],
        (((1,), (1,)), ((), ())),
        preferred_element_type=F32,
    )

    @pl.when(step == 0)
    def _():
        total[...] = down

    @pl.when(step > 0)
    def _():
        total[...] += down

    @pl.when(step == SUB - 1)
    def _():
        for k in range(SUB):
            start = pl.multiple_of(ahead(own_q, k) * share, share)
            outs[k][...] = total[pl.ds(start, share), :].astype(BF16)
        mid_out[...] = mid[pl.ds(pl.multiple_of(own_q * share, share), share), :]


def merge_norm_body(p0, p1, p2, p3, mid, gain, out):
    rows, width = mid.shape
    summed = p0[...].astype(F32) + p1[...].astype(F32) + p2[...].astype(F32) + p3[...].astype(F32)
    final = (mid[...].astype(F32) + summed).astype(BF16).astype(F32)
    row = lax.broadcasted_iota(jnp.int32, (rows, rows), 0)
    col = lax.broadcasted_iota(jnp.int32, (rows, rows), 1)
    same_group = row // 4 == col // 4

    def group_mean(column):
        across = jnp.sum(jnp.where(same_group, column, 0.0), axis=0, keepdims=True)
        down = jnp.sum(jnp.where(row == col, across, 0.0), axis=1, keepdims=True)
        return down / (4 * width)

    centre = final - group_mean(jnp.sum(final, axis=1, keepdims=True))
    spread = group_mean(jnp.sum(centre * centre, axis=1, keepdims=True))
    normed = (centre * lax.rsqrt(spread + NORM_EPS) * gain[...]).astype(BF16)
    padded = out.shape[0]
    slots = padded // 4
    new_row = lax.broadcasted_iota(jnp.int32, (padded, rows), 0)
    old_row = lax.broadcasted_iota(jnp.int32, (padded, rows), 1)
    in_group = new_row % slots
    chosen = ((in_group * 4 + new_row // slots == old_row) & (in_group < rows // 4)).astype(BF16)
    out[...] = dot(chosen, normed).astype(BF16)


def merge_projection_body(place, g0, g1, g2, g3, w0, w1, w2, w3, *rest):
    outs, (left, done) = rest[:SUB], rest[SUB:]
    own_z, own_q = place[1], place[2]
    step = pl.program_id(0)
    slots = g0.shape[0] // 4

    @pl.when(step == 0)
    def _():
        for k, ref in enumerate((g0, g1, g2, g3)):
            start = pl.multiple_of(back(own_q, k) * slots, slots)
            for patch in range(4):
                left[patch, pl.ds(start, slots), :] = ref[patch * slots : (patch + 1) * slots, :]

    total = dot(left[0], w0[0]) + dot(left[1], w1[0]) + dot(left[2], w2[0]) + dot(left[3], w3[0])
    done[step] = total.astype(BF16)

    @pl.when(step == SUB - 1)
    def _():
        for k in range(SUB):
            outs[k][...] = done[ahead(own_z, k)]


def place_body(place, seq, slot_position, projected, *rest):
    outs, (placed,) = rest[:SUB], rest[SUB:]
    own_z = place[1]
    tokens, slots = seq.shape[0], slot_position.shape[1]
    chosen = (seq[...] == slot_position[...]).astype(BF16)
    placed[...] = dot(chosen, projected[...]).astype(BF16)
    share = tokens // SUB
    for k in range(SUB):
        start = pl.multiple_of(ahead(own_z, k) * share, share)
        outs[k][...] = placed[pl.ds(start, share), :]


def dec_qkv_body(place, g0, g1, g2, g3, t0, t1, t2, t3, is_image, gain, weight, *rest):
    outs, embedded_out, (heads, text, normed, done) = rest[:SUB], rest[SUB], rest[SUB + 1 :]
    own_z, own_q = place[1], place[2]
    step = pl.program_id(0)

    @pl.when(step == 0)
    def _():
        share = t0.shape[0]
        for k, ref in enumerate((g0, g1, g2, g3)):
            for m in range(SUB):
                heads[back(own_z, m) * SUB + back(own_q, k)] = ref[:, m * LANES : (m + 1) * LANES]
        for k, ref in enumerate((t0, t1, t2, t3)):
            text[pl.ds(pl.multiple_of(back(own_q, k) * share, share), share), :] = ref[...]
        image = join_heads([heads[h] for h in range(SUB * SUB)])
        embedded = jnp.where(is_image[...] > 0, image.astype(F32), text[...].astype(F32))
        embedded_out[...] = embedded.astype(BF16)
        normed[...] = rms_norm_rows(embedded, gain[...])

    done[step] = dot(normed[...], weight[0]).astype(BF16)

    @pl.when(step == SUB - 1)
    def _():
        for k in range(SUB):
            outs[k][...] = done[ahead(own_z, k)]


def dec_attention_body(place, queries, query_request, query_position, request, position, *rest):
    blocks, outs, (weighted, denominator) = rest[: 2 * SUB], rest[2 * SUB : 3 * SUB], rest[3 * SUB :]
    own_gx = place[0]
    tokens = queries.shape[0]
    part = tokens // 2
    weighted[...] = jnp.zeros_like(weighted)
    denominator[...] = jnp.zeros_like(denominator)
    for at_block, block in enumerate(blocks):
        k, other = at_block % SUB, at_block // SUB
        chip = back(lax.div(own_gx, 2), k)
        core = lax.rem(own_gx + other, 2)
        owner = 2 * chip + core

        @pl.when(owner <= own_gx)
        def _():
            key_request = request[pl.ds(owner, 1), :]
            key_position = position[...] + owner * tokens
            for at in range(0, tokens, part):
                scores = lax.dot_general(
                    queries[at : at + part, :],
                    block[:, :LANES],
                    (((1,), (1,)), ((), ())),
                    preferred_element_type=F32,
                ) * HEAD_DIM ** (-0.5)
                allowed = (key_request == query_request[at : at + part, :]) & (
                    key_position <= query_position[at : at + part, :]
                )
                exp_scores = jnp.where(allowed, jnp.exp(scores), 0.0)
                denominator[at : at + part, :] += jnp.sum(exp_scores, axis=1, keepdims=True)
                weighted[at : at + part, :] += dot(exp_scores.astype(BF16), block[:, LANES:])

    share = tokens // SUB
    for k in range(SUB):
        at = share * ((SUB - k) % SUB)
        outs[k][...] = (weighted[at : at + share, :] / denominator[at : at + share, :]).astype(BF16)


def dec_final_body(p0, p1, p2, p3, mid, gain, out):
    summed = p0[...].astype(F32) + p1[...].astype(F32) + p2[...].astype(F32) + p3[...].astype(F32)
    final = (mid[...].astype(F32) + summed).astype(BF16).astype(F32)
    out[...] = rms_norm_rows(final, gain[...])


def next_qkv_body(place, g0, g1, g2, g3, weight, *rest):
    outs, (left, done) = rest[:SUB], rest[SUB:]
    own_q = place[2]
    step = pl.program_id(0)
    share = g0.shape[0]

    @pl.when(step == 0)
    def _():
        for k, ref in enumerate((g0, g1, g2, g3)):
            left[pl.ds(pl.multiple_of(back(own_q, k) * share, share), share), :] = ref[...]

    done[step] = dot(left[...], weight[0]).astype(BF16)

    @pl.when(step == SUB - 1)
    def _():
        for k in range(SUB):
            start = pl.multiple_of(ahead(own_q, k) * share, share)
            for z in range(SUB):
                outs[k][:, 3 * LANES * z : 3 * LANES * (z + 1)] = done[z, pl.ds(start, share), :]


def finish_body(place, r0, r1, r2, r3, out, held):
    own_q = place[2]
    for k, ref in enumerate((r0, r1, r2, r3)):
        held[back(own_q, k)] = ref[...]
    for t in range(3):
        out[t] = join_heads(
            [
                held[q, :, 3 * LANES * z + LANES * t : 3 * LANES * z + LANES * (t + 1)]
                for z in range(SUB)
                for q in range(SUB)
            ]
        )


def pad_lanes(values):
    width = values.shape[-1]
    return jnp.pad(values, [(0, 0)] * (values.ndim - 1) + [(0, LANES - width)])


def pad_flat(values):
    padded = pad_lanes(values)
    return padded.reshape(padded.shape[0], -1)


def block_spec(rows, width, at):
    return pl.BlockSpec((1, rows, width), lambda z: (z, 0, at))


def whole(values):
    rank = values.ndim
    return pl.BlockSpec(values.shape, lambda z: (0,) * rank)


def fixed(struct):
    rank = len(struct.shape)
    return pl.BlockSpec(struct.shape, lambda z: (0,) * rank)


def per_device(
    patches,
    grids,
    text_ids,
    positions,
    lengths,
    text_table,
    vit_norm1,
    vit_qkv,
    vit_out,
    vit_norm2,
    vit_fc1,
    vit_fc2,
    merge_norm,
    merge_proj,
    dec_norm1,
    dec_qkv,
    dec_out,
    dec_norm2,
    dec_fc1,
    dec_fc2,
    next_norm,
    next_qkv,
):
    gx_count = lax.axis_size("gx")
    own_gx, own_z, own_q = lax.axis_index("gx"), lax.axis_index("gz"), lax.axis_index("gq")
    place = jnp.stack([own_gx, own_z, own_q]).astype(jnp.int32)
    width = patches.shape[1]
    share = patches.shape[0]
    slots = share * SUB * SUB

    def gather_weights(parts):
        local = jnp.concatenate(parts, axis=1)
        full = lax.all_gather(local, ("gz", "gx"), axis=0, tiled=True)
        return full.reshape(SUB, width, local.shape[1])

    vit_weights = gather_weights([vit_fc1, vit_fc2, pad_lanes(vit_out)])
    mid_weights = gather_weights([pad_flat(dec_qkv), pad_flat(merge_proj)])
    dec_weights = gather_weights([dec_fc1, dec_fc2, pad_flat(next_qkv), pad_lanes(dec_out)])
    qkv_weight = lax.all_gather(vit_qkv, "gx", axis=0, tiled=True)
    qkv_weight = pad_flat(qkv_weight)

    spread = lax.all_to_all(
        jnp.broadcast_to(patches, (SUB * SUB,) + patches.shape), ("gz", "gq"), 0, 0
    )
    patches_full = spread.reshape(slots, width)

    per_group = grids.shape[0] // gx_count
    own_grids = lax.dynamic_slice_in_dim(grids, own_gx * per_group, per_group, 0)
    merge_slots = positions.shape[0] // gx_count
    sources, image_of, is_live = merge_sources(own_grids, merge_slots)
    source_column = sources.reshape(slots, 1)
    query_class = jnp.repeat(jnp.where(is_live, image_of, 0), 4).reshape(slots, 1)
    key_class = jnp.repeat(image_of, 4).reshape(1, slots)

    row = lambda gain: gain.reshape(1, -1)
    attended = call(
        vit_attention_body,
        [shape(slots // SUB, LANES)] * SUB,
        (place, patches_full, qkv_weight, row(vit_norm1), source_column, query_class, key_class),
        specs=[SMEM] + [VMEM] * 6,
        scratch=[pltpu.VMEM((slots, 3 * LANES), BF16), pltpu.VMEM((slots, 3 * LANES), BF16)],
        flops=2 * slots * (width * 3 * LANES + slots * 5 * LANES),
        name="vit_attention",
    )
    group_rows = slots // SUB
    own_sources = lax.dynamic_slice_in_dim(source_column, own_z * group_rows, group_rows, 0)
    stream = call(
        pick_rows_body,
        shape(group_rows, width),
        (own_sources, patches_full),
        flops=2 * slots * group_rows * width,
        name="pick_rows",
    )

    def attention_output(pieces, weights, at, name):
        rows = pieces[0].shape[0]
        stacked = jnp.concatenate(exchange_four("gz", pieces), axis=1)
        gathered = gather_four("gq", stacked)
        out = shape(rows, SUB * LANES)
        return call(
            out_projection_body,
            out,
            (place, *gathered, weights),
            specs=[SMEM] + [whole(g) for g in gathered] + [block_spec(width, LANES, at)],
            grid=(SUB,),
            out_specs=pl.BlockSpec((rows, LANES), lambda z: (0, z)),
            scratch=[
                pltpu.VMEM((SUB * SUB, rows, LANES), BF16),
                pltpu.VMEM((rows, width), BF16),
            ],
            flops=2 * rows * width * SUB * LANES,
            name=name,
        )

    def feed_forward(projected, stream, gain, weights, norm, name):
        rows = stream.shape[0]
        own = rows // SUB
        gathered = gather_four("gq", projected)
        hidden_width = vit_fc1.shape[1]
        outs = [shape(own, width)] * (SUB + 1)
        *pieces, mid = call(
            functools.partial(feed_forward_body, norm, own, own),
            outs,
            (place, *gathered, stream, gain, weights),
            specs=[SMEM]
            + [whole(g) for g in gathered]
            + [whole(stream), whole(gain), block_spec(width, 2 * hidden_width, 0)],
            grid=(SUB,),
            out_specs=[fixed(o) for o in outs],
            scratch=[
                pltpu.VMEM((SUB * SUB, rows, LANES), BF16),
                pltpu.VMEM((rows, width), BF16),
                pltpu.VMEM((rows, width), BF16),
                pltpu.VMEM((rows, width), F32),
            ],
            flops=4 * rows * width * SUB * hidden_width,
            name=name,
        )
        return exchange_four("gq", pieces), mid

    projected = attention_output(attended, vit_weights, 6, "vit_output")
    partials, mid = feed_forward(
        projected, stream, row(vit_norm2), vit_weights, layer_norm_rows, "vit_feed_forward"
    )

    gain_rows = jnp.tile(merge_norm, (share // 4, 1))
    merged = call(merge_norm_body, shape(64, width), (*partials, mid, gain_rows), name="merge_norm")
    gathered = gather_four("gq", merged)
    outs = [shape(64, LANES)] * SUB
    pieces = call(
        merge_projection_body,
        outs,
        (place, *gathered, mid_weights, mid_weights, mid_weights, mid_weights),
        specs=[SMEM]
        + [whole(g) for g in gathered]
        + [block_spec(width, LANES, 3 + patch) for patch in range(4)],
        grid=(SUB,),
        out_specs=[fixed(o) for o in outs],
        scratch=[pltpu.VMEM((4, 64, width), BF16), pltpu.VMEM((SUB, 64, LANES), BF16)],
        flops=2 * 64 * 4 * width * SUB * LANES,
        name="merge_projection",
    )
    own_columns = jnp.concatenate(exchange_four("gz", pieces), axis=0)
    all_projected = lax.all_gather(own_columns, "gx", axis=0, tiled=True)

    tokens = text_ids.shape[0]
    part = tokens // SUB
    relative = lax.rem(own_z + SUB - jnp.arange(SUB, dtype=jnp.int32), SUB)
    local_order = (relative[:, None] * part + jnp.arange(part, dtype=jnp.int32)[None, :]).reshape(-1)
    seq_natural = own_gx * tokens + jnp.arange(tokens, dtype=jnp.int32)
    by_slot = jnp.pad(
        positions.reshape(gx_count, SUB, SUB, merge_slots // (SUB * SUB)),
        ((0, 0), (0, 0), (0, 0), (0, 4)),
        constant_values=-1,
    )
    slot_position = jnp.take(by_slot, relative, axis=1).reshape(1, -1)
    placed = call(
        place_body,
        [shape(part, LANES)] * SUB,
        (place, seq_natural.reshape(tokens, 1), slot_position, all_projected),
        specs=[SMEM] + [VMEM] * 3,
        scratch=[pltpu.VMEM((tokens, LANES), BF16)],
        flops=2 * tokens * slot_position.shape[1] * LANES,
        name="place_rows",
    )
    image_rows = gather_four("gq", jnp.concatenate(exchange_four("gz", placed), axis=1))

    vocab_rows = text_table.shape[0]
    shifted_ids = text_ids - (own_z * SUB + own_q) * vocab_rows
    chosen = (shifted_ids[:, None] == jnp.arange(vocab_rows, dtype=jnp.int32)[None, :]).astype(BF16)
    table_rows = jnp.dot(chosen, text_table, preferred_element_type=F32).astype(BF16)
    text_parts = lax.all_to_all(
        table_rows.reshape(SUB * SUB, tokens // (SUB * SUB), width), ("gz", "gq"), 0, 0
    )
    own_text = jnp.sum(text_parts.astype(F32), axis=0).astype(BF16)
    text_rows = gather_four("gq", own_text)

    group_seq = own_gx * tokens + own_z * part + jnp.arange(part, dtype=jnp.int32)
    is_image = jnp.any(positions[None, :] == group_seq[:, None], axis=1).astype(F32).reshape(part, 1)

    outs = [shape(part, 3 * LANES)] * SUB + [shape(part, width)]
    *pieces, embedded = call(
        dec_qkv_body,
        outs,
        (place, *image_rows, *text_rows, is_image, row(dec_norm1), mid_weights),
        specs=[SMEM]
        + [whole(a) for a in (*image_rows, *text_rows, is_image, row(dec_norm1))]
        + [block_spec(width, 3 * LANES, 0)],
        grid=(SUB,),
        out_specs=[fixed(o) for o in outs],
        scratch=[
            pltpu.VMEM((SUB * SUB, part, LANES), BF16),
            pltpu.VMEM((part, width), BF16),
            pltpu.VMEM((part, width), BF16),
            pltpu.VMEM((SUB, part, 3 * LANES), BF16),
        ],
        flops=2 * part * width * SUB * 3 * LANES,
        name="dec_qkv",
    )
    triple = jnp.concatenate(exchange_four("gz", pieces), axis=0)
    key_values = triple[:, LANES:]
    same_core = [key_values] + [
        lax.ppermute(
            key_values,
            "gx",
            [(2 * y + c, 2 * ((y + k) % SUB) + c) for y in range(SUB) for c in range(2)],
        )
        for k in range(1, SUB)
    ]
    other_core = [lax.ppermute(b, "gx", [(i, i ^ 1) for i in range(gx_count)]) for b in same_core]
    bounds = jnp.cumsum(lengths)
    all_index = (
        jnp.arange(gx_count, dtype=jnp.int32)[:, None] * tokens + local_order[None, :]
    )
    request = jnp.sum((all_index[:, :, None] >= bounds).astype(jnp.int32), axis=2)
    own_index = own_gx * tokens + local_order
    own_request = jnp.sum((own_index[:, None] >= bounds).astype(jnp.int32), axis=1)
    attended = call(
        dec_attention_body,
        [shape(part, LANES)] * SUB,
        (
            place,
            triple[:, :LANES],
            own_request.reshape(tokens, 1),
            own_index.reshape(tokens, 1),
            request,
            local_order.reshape(1, tokens),
            *same_core,
            *other_core,
        ),
        specs=[SMEM] + [VMEM] * (5 + 2 * SUB),
        scratch=[pltpu.VMEM((tokens, LANES), F32), pltpu.VMEM((tokens, 1), F32)],
        flops=4 * tokens * tokens * gx_count * LANES,
        name="dec_attention",
    )
    projected = attention_output(attended, dec_weights, 9, "dec_output")
    partials, mid = feed_forward(
        projected, embedded, row(dec_norm2), dec_weights, rms_norm_rows, "dec_feed_forward"
    )
    own_tokens = mid.shape[0]
    normed = call(
        dec_final_body, shape(own_tokens, width), (*partials, mid, row(next_norm)), name="dec_final"
    )

    gathered = gather_four("gq", normed)
    outs = [shape(own_tokens, SUB * 3 * LANES)] * SUB
    pieces = call(
        next_qkv_body,
        outs,
        (place, *gathered, dec_weights),
        specs=[SMEM] + [whole(g) for g in gathered] + [block_spec(width, 3 * LANES, 2)],
        grid=(SUB,),
        out_specs=[fixed(o) for o in outs],
        scratch=[
            pltpu.VMEM((part, width), BF16),
            pltpu.VMEM((SUB, part, 3 * LANES), BF16),
        ],
        flops=2 * part * width * SUB * 3 * LANES,
        name="next_qkv",
    )
    received = exchange_four("gq", pieces)
    finished = call(
        finish_body,
        shape(3, own_tokens, width),
        (place, *received),
        specs=[SMEM] + [VMEM] * SUB,
        scratch=[pltpu.VMEM((SUB, own_tokens, SUB * 3 * LANES), BF16)],
        name="finish",
    )
    return finished.transpose(1, 0, 2)


def solution(mesh):
    gx_size = mesh.shape["gx"]
    cut = Mesh(mesh.devices.reshape(gx_size, SUB, SUB), ("gx", "gz", "gq"))
    gy = ("gz", "gq")
    flat = P("gx", gy)
    deep = P("gx", None, gy)
    placed = (
        P(("gx", *gy), None),
        P(),
        P("gx"),
        P(),
        P(),
        P(gy, None),
        P(),
        deep,
        flat,
        P(),
        flat,
        flat,
        P(),
        deep,
        P(),
        deep,
        flat,
        P(),
        flat,
        flat,
        P(),
        deep,
    )
    return jax.shard_map(
        per_device,
        mesh=cut,
        in_specs=placed,
        out_specs=P(("gx", *gy), None, None),
        check_vma=False,
    )
```

```python
import functools
import math

import jax
import jax.numpy as jnp
from jax import lax
from jax.experimental import pallas as pl
from jax.experimental.pallas import tpu as pltpu
from jax.sharding import Mesh, PartitionSpec as P

HEAD_DIM = 88
LANES = 128
SUB = 4
NORM_EPS = 1e-06
F32 = jnp.float32
BF16 = jnp.bfloat16
VMEM_LIMIT = 50 * 1024 * 1024


def merge_sources(grid_rows, merge_slots):
    image_count = grid_rows.shape[0]
    merged_count = grid_rows[:, 0] * grid_rows[:, 1]
    merged_end = jnp.cumsum(merged_count)
    merged_start = merged_end - merged_count
    slot_index = jnp.arange(merge_slots, dtype=jnp.int32)
    image_of = jnp.sum((slot_index[:, None] >= merged_end[None, :]).astype(jnp.int32), axis=1)
    is_live = image_of < image_count
    picked = (
        jnp.minimum(image_of, image_count - 1)[:, None]
        == jnp.arange(image_count, dtype=jnp.int32)[None, :]
    ).astype(jnp.int32)
    col_count = jnp.sum(picked * grid_rows[None, :, 1], axis=1)
    first_slot = jnp.sum(picked * merged_start[None, :], axis=1)
    local_slot = slot_index - first_slot
    grid_row = local_slot // col_count
    grid_col = local_slot % col_count
    base_row = 4 * first_slot + 4 * grid_row * col_count + 2 * grid_col
    offsets = jnp.stack(
        [jnp.zeros_like(col_count), jnp.ones_like(col_count), 2 * col_count, 2 * col_count + 1],
        axis=1,
    )
    sources = jnp.where(is_live[:, None], base_row[:, None] + offsets, 0)
    return sources, image_of, is_live


def shift_in(axis, values, step):
    return lax.ppermute(values, axis, [(i, (i + step) % SUB) for i in range(SUB)])


def gather_four(axis, values):
    return [values] + [shift_in(axis, values, k) for k in range(1, SUB)]


def exchange(axis, pieces):
    return lax.all_to_all(pieces, axis, 0, 0)


SMEM = pl.BlockSpec(memory_space=pltpu.SMEM)
VMEM = pl.BlockSpec(memory_space=pltpu.VMEM)


def shape(*dims, dtype=BF16):
    return jax.ShapeDtypeStruct(dims, dtype)


def call(body, outs, args, specs=None, grid=None, out_specs=None, scratch=(), flops=0, name=None):
    if specs is None:
        specs = [VMEM] * len(args)
    if out_specs is None:
        out_specs = jax.tree.map(lambda _: VMEM, outs)
    moved = sum(math.prod(a.shape) * a.dtype.itemsize for a in args)
    kwargs = {} if grid is None else {"grid": grid}
    return pl.pallas_call(
        body,
        out_shape=outs,
        in_specs=specs,
        out_specs=out_specs,
        scratch_shapes=list(scratch),
        cost_estimate=pl.CostEstimate(flops=flops, bytes_accessed=moved, transcendentals=0),
        compiler_params=pltpu.CompilerParams(vmem_limit_bytes=VMEM_LIMIT),
        name=name,
        **kwargs,
    )(*args)


def back(own, step):
    return lax.rem(own + (SUB - step), SUB)


def ahead(own, step):
    return lax.rem(own + step, SUB)


def dot(left, right):
    return jnp.dot(left, right, preferred_element_type=F32)


def layer_norm_rows(values, gain):
    centre = values - jnp.mean(values, axis=-1, keepdims=True)
    spread = jnp.mean(centre * centre, axis=-1, keepdims=True)
    return (centre * lax.rsqrt(spread + NORM_EPS) * gain).astype(BF16)


def rms_norm_rows(values, gain):
    square = jnp.mean(values * values, axis=-1, keepdims=True)
    return (values * lax.rsqrt(square + NORM_EPS) * gain).astype(BF16)


def gelu(values):
    return 0.5 * values * (1.0 + lax.erf(values * (2.0**-0.5)))


def pad_heads(values):
    empty = jnp.zeros((values.shape[0], LANES - HEAD_DIM), values.dtype)
    parts = []
    for t in range(3):
        parts += [values[:, t * HEAD_DIM : (t + 1) * HEAD_DIM], empty]
    return jnp.concatenate(parts, axis=1)


def vit_attention_body(patches, weight, gain, source, query_class, key_class, out, triple, merged):
    slots = triple.shape[0]
    count = patches.shape[1]
    step = slots // SUB

    def project(i, _):
        rows = patches[pl.ds(i, 1)].reshape(count, patches.shape[2])
        normed = layer_norm_rows(rows.astype(F32), gain[...])
        at = pl.multiple_of(i * count, count)
        triple[pl.ds(at, count), :] = pad_heads(dot(normed, weight[...]).astype(BF16))
        return 0

    lax.fori_loop(0, patches.shape[0], project, 0)

    def reorder(i, _):
        at = pl.multiple_of(i * step, step)
        chosen = (
            source[pl.ds(at, step), :] == lax.broadcasted_iota(jnp.int32, (step, slots), 1)
        ).astype(BF16)
        merged[pl.ds(at, step), :] = dot(chosen, triple[...]).astype(BF16)
        return 0

    lax.fori_loop(0, SUB, reorder, 0)

    def attend(i, _):
        at = pl.multiple_of(i * step, step)
        scores = lax.dot_general(
            merged[pl.ds(at, step), :LANES],
            merged[:, LANES : 2 * LANES],
            (((1,), (1,)), ((), ())),
            preferred_element_type=F32,
        ) * HEAD_DIM ** (-0.5)
        allowed = query_class[pl.ds(at, step), :] == key_class[...]
        exp_scores = jnp.where(allowed, jnp.exp(scores), 0.0)
        denominator = jnp.sum(exp_scores, axis=1, keepdims=True)
        weighted = dot(exp_scores.astype(BF16), merged[:, 2 * LANES :])
        result = (weighted / denominator).astype(BF16)
        for q in range(SUB):
            out[i * SUB + q] = result
        return 0

    lax.fori_loop(0, SUB, attend, 0)


def pick_rows_body(source, patches, out):
    slots = patches.shape[0] * patches.shape[1]
    rows = patches[...].reshape(slots, patches.shape[2])
    chosen = (source[...] == lax.broadcasted_iota(jnp.int32, (source.shape[0], slots), 1)).astype(BF16)
    out[...] = dot(chosen, rows).astype(BF16)


def join_heads(blocks):
    return jnp.concatenate([block[:, :HEAD_DIM] for block in blocks], axis=1)


def out_projection_body(heads, weight, out, left):
    @pl.when(pl.program_id(0) == 0)
    def _():
        left[...] = join_heads([heads[h] for h in range(SUB * SUB)])

    out[...] = dot(left[...], weight[0]).astype(BF16)


def hold_blocks(refs, own_q, heads):
    for k, ref in enumerate(refs):
        for z in range(SUB):
            heads[z * SUB + back(own_q, k)] = ref[:, z * LANES : (z + 1) * LANES]


def feed_forward_body(norm, place, o0, o1, o2, o3, stream, gain, weight, out, mid_out, heads, mid, normed, total):
    own_q = place[2]
    step = pl.program_id(0)
    rows = stream.shape[0]
    share = rows // SUB
    hidden_width = weight.shape[2] // 2

    @pl.when(step == 0)
    def _():
        hold_blocks((o0, o1, o2, o3), own_q, heads)

        def prepare(i, _):
            part = pl.ds(pl.multiple_of(i * share, share), share)
            added = join_heads([heads[h, part, :] for h in range(SUB * SUB)])
            summed = (stream[part, :].astype(F32) + added.astype(F32)).astype(BF16)
            mid[part, :] = summed
            normed[part, :] = norm(summed.astype(F32), gain[...])
            return 0

        lax.fori_loop(0, SUB, prepare, 0)

    hidden = gelu(dot(normed[...], weight[0, :, :hidden_width])).astype(BF16)
    down = lax.dot_general(
        hidden,
        weight[0, :, hidden_width:],
        (((1,), (1,)), ((), ())),
        preferred_element_type=F32,
    )

    @pl.when(step == 0)
    def _():
        total[...] = down

    @pl.when((step > 0) & (step < SUB - 1))
    def _():
        total[...] += down

    @pl.when(step == SUB - 1)
    def _():
        out[...] = (total[...] + down).astype(BF16)
        mid_out[...] = mid[pl.ds(pl.multiple_of(own_q * share, share), share), :]


def summed_stream(partials, mid):
    summed = partials[0].astype(F32)
    for i in range(1, SUB):
        summed += partials[i].astype(F32)
    return (mid[...].astype(F32) + summed).astype(BF16).astype(F32)


def merge_norm_body(partials, mid, gain, out):
    rows, width = mid.shape
    final = summed_stream(partials, mid)
    row = lax.broadcasted_iota(jnp.int32, (rows, rows), 0)
    col = lax.broadcasted_iota(jnp.int32, (rows, rows), 1)
    same_group = row // 4 == col // 4

    def group_mean(column):
        across = jnp.sum(jnp.where(same_group, column, 0.0), axis=0, keepdims=True)
        down = jnp.sum(jnp.where(row == col, across, 0.0), axis=1, keepdims=True)
        return down / (4 * width)

    centre = final - group_mean(jnp.sum(final, axis=1, keepdims=True))
    spread = group_mean(jnp.sum(centre * centre, axis=1, keepdims=True))
    normed = (centre * lax.rsqrt(spread + NORM_EPS) * gain[...]).astype(BF16)
    padded = out.shape[0]
    slots = padded // 4
    new_row = lax.broadcasted_iota(jnp.int32, (padded, rows), 0)
    old_row = lax.broadcasted_iota(jnp.int32, (padded, rows), 1)
    in_group = new_row % slots
    chosen = ((in_group * 4 + new_row // slots == old_row) & (in_group < rows // 4)).astype(BF16)
    out[...] = dot(chosen, normed).astype(BF16)


def merge_projection_body(place, g0, g1, g2, g3, weight, out, left):
    own_q = place[2]
    slots = g0.shape[0] // 4

    @pl.when(pl.program_id(0) == 0)
    def _():
        for k, ref in enumerate((g0, g1, g2, g3)):
            start = pl.multiple_of(back(own_q, k) * slots, slots)
            for patch in range(4):
                left[patch, pl.ds(start, slots), :] = ref[patch * slots : (patch + 1) * slots, :]

    total = dot(left[0], weight[0, :, :HEAD_DIM])
    for patch in range(1, 4):
        total += dot(left[patch], weight[0, :, patch * HEAD_DIM : (patch + 1) * HEAD_DIM])
    empty = jnp.zeros((total.shape[0], LANES - HEAD_DIM), F32)
    out[...] = jnp.concatenate([total, empty], axis=1).astype(BF16)


def text_rows_body(place, ids, table, *outs):
    own_q = place[2]
    first = (place[1] * SUB + own_q) * table.shape[0]
    tokens = ids.shape[0]
    chosen = (
        ids[...] - first == lax.broadcasted_iota(jnp.int32, (tokens, table.shape[0]), 1)
    ).astype(BF16)
    rows = dot(chosen, table[...]).astype(BF16)
    empty = jnp.zeros((tokens, LANES - HEAD_DIM), BF16)
    held = outs[SUB]
    for z in range(SUB):
        for q in range(SUB):
            at = (z * SUB + q) * HEAD_DIM
            held[q, :, z * LANES : (z + 1) * LANES] = jnp.concatenate(
                [rows[:, at : at + HEAD_DIM], empty], axis=1
            )
    for k in range(SUB):
        outs[k][...] = held[ahead(own_q, k)]


def place_body(seq, is_image, slot_position, projected, t0, t1, t2, t3, out):
    chosen = (seq[...] == slot_position[...]).astype(BF16)
    placed = dot(chosen, projected[...])
    text = t0[...].astype(F32) + t1[...].astype(F32) + t2[...].astype(F32) + t3[...].astype(F32)
    out[...] = jnp.where(is_image[...] > 0, placed, text).astype(BF16)


def dec_qkv_body(place, g0, g1, g2, g3, gain, weight, out, embedded_out, heads, normed):
    @pl.when(pl.program_id(0) == 0)
    def _():
        hold_blocks((g0, g1, g2, g3), place[2], heads)
        embedded = join_heads([heads[h] for h in range(SUB * SUB)])
        embedded_out[...] = embedded
        normed[...] = rms_norm_rows(embedded.astype(F32), gain[...])

    first = weight.shape[2] - 3 * HEAD_DIM - 24
    result = dot(normed[...], weight[0, :, first - first % LANES :])
    at = first % LANES
    out[0] = pad_heads(result[:, at : at + 3 * HEAD_DIM].astype(BF16))


def dec_attention_body(place, triple, query_request, query_position, request, near, far, out, weighted, denominator):
    own_gx = place[0]
    tokens = triple.shape[0]
    part = tokens // 2
    weighted[...] = jnp.zeros_like(weighted)
    denominator[...] = jnp.zeros_like(denominator)

    def attend(k, blocks, core):
        owner = 2 * lax.rem(lax.div(own_gx, 2) + (SUB - k), SUB) + core

        @pl.when(owner <= own_gx)
        def _():
            key_request = request[pl.ds(owner, 1), :]
            key_position = lax.broadcasted_iota(jnp.int32, (1, tokens), 1) + owner * tokens

            def half(i, _):
                rows = pl.ds(pl.multiple_of(i * part, part), part)
                scores = lax.dot_general(
                    triple[rows, :LANES],
                    blocks[k, :, :LANES],
                    (((1,), (1,)), ((), ())),
                    preferred_element_type=F32,
                ) * HEAD_DIM ** (-0.5)
                allowed = (key_request == query_request[rows, :]) & (
                    key_position <= query_position[rows, :]
                )
                exp_scores = jnp.where(allowed, jnp.exp(scores), 0.0)
                denominator[rows, :] += jnp.sum(exp_scores, axis=1, keepdims=True)
                weighted[rows, :] += dot(exp_scores.astype(BF16), blocks[k, :, LANES:])
                return 0

            lax.fori_loop(0, 2, half, 0)

    def both(k, _):
        attend(k, near, lax.rem(own_gx, 2))
        attend(k, far, lax.rem(own_gx + 1, 2))
        return 0

    lax.fori_loop(0, SUB, both, 0)
    share = tokens // SUB
    for z in range(SUB):
        rows = slice(z * share, (z + 1) * share)
        result = (weighted[rows, :] / denominator[rows, :]).astype(BF16)
        for q in range(SUB):
            out[z * SUB + q] = result


def dec_final_body(partials, mid, gain, out):
    out[...] = rms_norm_rows(summed_stream(partials, mid), gain[...])


def next_qkv_body(place, g0, g1, g2, g3, weight, out, left):
    own_q = place[2]
    share = g0.shape[0]

    @pl.when(pl.program_id(0) == 0)
    def _():
        for k, ref in enumerate((g0, g1, g2, g3)):
            left[pl.ds(pl.multiple_of(back(own_q, k) * share, share), share), :] = ref[...]

    result = dot(left[...], weight[0])
    out[...] = pad_heads(result[:, HEAD_DIM : 4 * HEAD_DIM].astype(BF16))


def finish_body(received, out):
    for t in range(3):
        at = LANES * t
        out[t] = join_heads(
            [
                received[q, :, 3 * LANES * z + at : 3 * LANES * z + at + LANES]
                for z in range(SUB)
                for q in range(SUB)
            ]
        )


def pad_to(values, width):
    return jnp.pad(values, ((0, 0), (0, width - values.shape[1])))


def flat_rows(values):
    return values.reshape(values.shape[0], -1)


def block_spec(rows, width, at):
    return pl.BlockSpec((1, rows, width), lambda z: (z, 0, at))


def whole(values):
    rank = values.ndim
    return pl.BlockSpec(values.shape, lambda z: (0,) * rank)


def fixed(struct):
    rank = len(struct.shape)
    return pl.BlockSpec(struct.shape, lambda z: (0,) * rank)


def per_device(
    patches,
    grids,
    text_ids,
    positions,
    lengths,
    text_table,
    vit_norm1,
    vit_qkv,
    vit_out,
    vit_norm2,
    vit_fc1,
    vit_fc2,
    merge_norm,
    merge_proj,
    dec_norm1,
    dec_qkv,
    dec_out,
    dec_norm2,
    dec_fc1,
    dec_fc2,
    next_norm,
    next_qkv,
):
    gx_count = lax.axis_size("gx")
    own_gx, own_z, own_q = lax.axis_index("gx"), lax.axis_index("gz"), lax.axis_index("gq")
    place = jnp.stack([own_gx, own_z, own_q]).astype(jnp.int32)
    width = patches.shape[1]
    share = patches.shape[0]
    slots = share * SUB * SUB

    def gather_weights(parts, lanes):
        local = pad_to(jnp.concatenate([flat_rows(p) for p in parts], axis=1), lanes)
        full = lax.all_gather(local, ("gz", "gx"), axis=0, tiled=True)
        return full.reshape(SUB, width, lanes)

    vit_weights = gather_weights([vit_fc1, vit_fc2, vit_out], 896)
    mid_weights = gather_weights([merge_proj, dec_qkv], 640)
    dec_weights = gather_weights([dec_fc1, dec_fc2, dec_out, next_qkv], 1152)

    of_column = jnp.stack(gather_four("gz", patches))
    relative_z = lax.rem(own_z + SUB - jnp.arange(SUB, dtype=jnp.int32), SUB)
    relative_q = lax.rem(own_q + SUB - jnp.arange(SUB, dtype=jnp.int32), SUB)
    own_qkv, of_column = lax.optimization_barrier((flat_rows(vit_qkv), of_column))
    patches_full = jnp.concatenate(gather_four("gq", of_column), axis=0)
    qkv_weight = lax.all_gather(own_qkv, "gx", axis=0, tiled=True)

    per_group = grids.shape[0] // gx_count
    own_grids = lax.dynamic_slice_in_dim(grids, own_gx * per_group, per_group, 0)
    merge_slots = positions.shape[0] // gx_count
    sources, image_of, is_live = merge_sources(own_grids, merge_slots)
    holder = sources // share
    block = lax.rem(own_q + SUB - lax.rem(holder, SUB), SUB) * SUB + lax.rem(
        own_z + SUB - holder // SUB, SUB
    )
    source_column = (block * share + lax.rem(sources, share)).reshape(slots, 1)
    query_class = jnp.repeat(jnp.where(is_live, image_of, 0), 4).reshape(slots, 1)
    key_class = jnp.repeat(image_of, 4).reshape(1, slots)

    row = lambda gain: gain.reshape(1, -1)
    group_rows = slots // SUB
    attended = call(
        vit_attention_body,
        shape(SUB * SUB, group_rows, LANES),
        (patches_full, qkv_weight, row(vit_norm1), source_column, query_class, key_class),
        scratch=[pltpu.VMEM((slots, 3 * LANES), BF16), pltpu.VMEM((slots, 3 * LANES), BF16)],
        flops=2 * slots * (width * 3 * LANES + slots * 5 * LANES),
        name="vit_attention",
    )
    own_sources = lax.dynamic_slice_in_dim(source_column, own_z * group_rows, group_rows, 0)
    stream = call(
        pick_rows_body,
        shape(group_rows, width),
        (own_sources, patches_full),
        flops=2 * slots * group_rows * width,
        name="pick_rows",
    )

    def attention_output(attended, weights, name):
        heads = exchange(("gz", "gq"), attended)
        rows = heads.shape[1]
        return call(
            out_projection_body,
            shape(rows, SUB * LANES),
            (heads, weights),
            specs=[whole(heads), block_spec(width, LANES, 6)],
            grid=(SUB,),
            out_specs=pl.BlockSpec((rows, LANES), lambda z: (0, z)),
            scratch=[pltpu.VMEM((rows, width), BF16)],
            flops=2 * rows * width * SUB * LANES,
            name=name,
        )

    def feed_forward(projected, stream, gain, weights, norm, name):
        rows = stream.shape[0]
        own = rows // SUB
        gathered = gather_four("gq", projected)
        hidden_width = vit_fc1.shape[1]
        outs = [shape(rows, width), shape(own, width)]
        partial, mid = call(
            functools.partial(feed_forward_body, norm),
            outs,
            (place, *gathered, stream, gain, weights),
            specs=[SMEM]
            + [whole(g) for g in gathered]
            + [whole(stream), whole(gain), block_spec(width, 2 * hidden_width, 0)],
            grid=(SUB,),
            out_specs=[fixed(o) for o in outs],
            scratch=[
                pltpu.VMEM((SUB * SUB, rows, LANES), BF16),
                pltpu.VMEM((rows, width), BF16),
                pltpu.VMEM((rows, width), BF16),
                pltpu.VMEM((rows, width), F32),
            ],
            flops=4 * rows * width * SUB * hidden_width,
            name=name,
        )
        return exchange("gq", partial.reshape(SUB, own, width)), mid

    projected = attention_output(attended, vit_weights, "vit_output")
    partials, mid = feed_forward(
        projected, stream, row(vit_norm2), vit_weights, layer_norm_rows, "vit_feed_forward"
    )

    own_slots = 16
    gain_rows = jnp.tile(merge_norm, (share // 4, 1))
    merged = call(
        merge_norm_body, shape(4 * own_slots, width), (partials, mid, gain_rows), name="merge_norm"
    )
    gathered = gather_four("gq", merged)
    group_slots = SUB * own_slots
    projected = call(
        merge_projection_body,
        shape(group_slots, SUB * LANES),
        (place, *gathered, mid_weights),
        specs=[SMEM] + [whole(g) for g in gathered] + [block_spec(width, 384, 0)],
        grid=(SUB,),
        out_specs=pl.BlockSpec((group_slots, LANES), lambda z: (0, z)),
        scratch=[pltpu.VMEM((4, group_slots, width), BF16)],
        flops=2 * group_slots * 4 * width * SUB * LANES,
        name="merge_projection",
    )
    all_projected = lax.all_gather(projected, "gx", axis=0, tiled=True)

    tokens = text_ids.shape[0]
    part = tokens // SUB
    text_blocks = call(
        text_rows_body,
        [shape(tokens, SUB * LANES)] * SUB,
        (place, text_ids.reshape(tokens, 1), text_table),
        specs=[SMEM, VMEM, VMEM],
        scratch=[pltpu.VMEM((SUB, tokens, SUB * LANES), BF16)],
        flops=2 * tokens * text_table.shape[0] * width,
        name="text_rows",
    )
    text_rows = [text_blocks[0]] + [shift_in("gq", text_blocks[k], k) for k in range(1, SUB)]
    own_index = own_gx * tokens + jnp.arange(tokens, dtype=jnp.int32)
    is_image = jnp.any(positions[None, :] == own_index[:, None], axis=1).astype(F32)
    live_slots = merge_slots // (SUB * SUB)
    by_slot = jnp.pad(
        lax.dynamic_index_in_dim(
            positions.reshape(gx_count, SUB, SUB, live_slots), own_z, 1, keepdims=False
        ),
        ((0, 0), (0, 0), (0, own_slots - live_slots)),
        constant_values=-1,
    )
    placed = call(
        place_body,
        shape(tokens, SUB * LANES),
        (
            own_index.reshape(tokens, 1),
            is_image.reshape(tokens, 1),
            by_slot.reshape(1, -1),
            all_projected,
            *text_rows,
        ),
        flops=2 * tokens * by_slot.size * SUB * LANES,
        name="place_rows",
    )
    own_rows = jnp.sum(
        exchange("gz", placed.reshape(SUB, part, SUB * LANES)).astype(F32), axis=0
    ).astype(BF16)
    gathered = gather_four("gq", own_rows)

    outs = [shape(SUB, part, 3 * LANES), shape(part, width)]
    triple, embedded = call(
        dec_qkv_body,
        outs,
        (place, *gathered, row(dec_norm1), mid_weights),
        specs=[SMEM]
        + [whole(a) for a in (*gathered, row(dec_norm1))]
        + [block_spec(width, 640, 0)],
        grid=(SUB,),
        out_specs=[pl.BlockSpec((1, part, 3 * LANES), lambda z: (z, 0, 0)), fixed(outs[1])],
        scratch=[pltpu.VMEM((SUB * SUB, part, LANES), BF16), pltpu.VMEM((part, width), BF16)],
        flops=2 * part * width * SUB * 3 * LANES,
        name="dec_qkv",
    )
    triple = exchange("gz", triple).reshape(tokens, 3 * LANES)
    key_values = triple[:, LANES:]
    near = jnp.stack(
        [key_values]
        + [
            lax.ppermute(
                key_values,
                "gx",
                [(2 * y + c, 2 * ((y + k) % SUB) + c) for y in range(SUB) for c in range(2)],
            )
            for k in range(1, SUB)
        ]
    )
    far = lax.ppermute(near, "gx", [(i, i ^ 1) for i in range(gx_count)])
    bounds = jnp.cumsum(lengths)
    all_index = jnp.arange(gx_count * tokens, dtype=jnp.int32).reshape(gx_count, tokens)
    request = jnp.sum((all_index[:, :, None] >= bounds).astype(jnp.int32), axis=2)
    own_request = jnp.sum((own_index[:, None] >= bounds).astype(jnp.int32), axis=1)
    attended = call(
        dec_attention_body,
        shape(SUB * SUB, part, LANES),
        (
            place,
            triple,
            own_request.reshape(tokens, 1),
            own_index.reshape(tokens, 1),
            request,
            near,
            far,
        ),
        specs=[SMEM] + [VMEM] * 6,
        scratch=[pltpu.VMEM((tokens, LANES), F32), pltpu.VMEM((tokens, 1), F32)],
        flops=4 * tokens * tokens * gx_count * LANES,
        name="dec_attention",
    )
    projected = attention_output(attended, dec_weights, "dec_output")
    partials, mid = feed_forward(
        projected, embedded, row(dec_norm2), dec_weights, rms_norm_rows, "dec_feed_forward"
    )
    own_tokens = mid.shape[0]
    normed = call(
        dec_final_body, shape(own_tokens, width), (partials, mid, row(next_norm)), name="dec_final"
    )

    gathered = gather_four("gq", normed)
    triple = call(
        next_qkv_body,
        shape(part, SUB * 3 * LANES),
        (place, *gathered, dec_weights),
        specs=[SMEM] + [whole(g) for g in gathered] + [block_spec(width, 3 * LANES, 2)],
        grid=(SUB,),
        out_specs=pl.BlockSpec((part, 3 * LANES), lambda z: (0, z)),
        scratch=[pltpu.VMEM((part, width), BF16)],
        flops=2 * part * width * SUB * 3 * LANES,
        name="next_qkv",
    )
    received = exchange("gq", triple.reshape(SUB, own_tokens, SUB * 3 * LANES))
    finished = call(finish_body, shape(3, own_tokens, width), (received,), name="finish")
    return finished.transpose(1, 0, 2)


def solution(mesh):
    gx_size = mesh.shape["gx"]
    cut = Mesh(mesh.devices.reshape(gx_size, SUB, SUB), ("gx", "gz", "gq"))
    gy = ("gz", "gq")
    flat = P("gx", gy)
    deep = P("gx", None, gy)
    placed = (
        P(("gx", *gy), None),
        P(),
        P("gx"),
        P(),
        P(),
        P(gy, None),
        P(),
        deep,
        flat,
        P(),
        flat,
        flat,
        P(),
        deep,
        P(),
        deep,
        flat,
        P(),
        flat,
        flat,
        P(),
        deep,
    )
    return jax.shard_map(
        per_device,
        mesh=cut,
        in_specs=placed,
        out_specs=P(("gx", *gy), None, None),
        check_vma=False,
    )
```

```python
import functools
import math

import jax
import jax.numpy as jnp
from jax import lax
from jax.experimental import pallas as pl
from jax.experimental.pallas import tpu as pltpu
from jax.sharding import Mesh, PartitionSpec as P

HEAD_DIM = 88
LANES = 128
SUB = 4
NORM_EPS = 1e-06
F32 = jnp.float32
BF16 = jnp.bfloat16
VMEM_LIMIT = 50 * 1024 * 1024


def merge_sources(grid_rows, merge_slots):
    image_count = grid_rows.shape[0]
    merged_count = grid_rows[:, 0] * grid_rows[:, 1]
    merged_end = jnp.cumsum(merged_count)
    merged_start = merged_end - merged_count
    slot_index = jnp.arange(merge_slots, dtype=jnp.int32)
    image_of = jnp.sum((slot_index[:, None] >= merged_end[None, :]).astype(jnp.int32), axis=1)
    is_live = image_of < image_count
    picked = (
        jnp.minimum(image_of, image_count - 1)[:, None]
        == jnp.arange(image_count, dtype=jnp.int32)[None, :]
    ).astype(jnp.int32)
    col_count = jnp.sum(picked * grid_rows[None, :, 1], axis=1)
    first_slot = jnp.sum(picked * merged_start[None, :], axis=1)
    local_slot = slot_index - first_slot
    grid_row = local_slot // col_count
    grid_col = local_slot % col_count
    base_row = 4 * first_slot + 4 * grid_row * col_count + 2 * grid_col
    offsets = jnp.stack(
        [jnp.zeros_like(col_count), jnp.ones_like(col_count), 2 * col_count, 2 * col_count + 1],
        axis=1,
    )
    sources = jnp.where(is_live[:, None], base_row[:, None] + offsets, 0)
    return sources, image_of, is_live


def shift_in(axis, values, step):
    return lax.ppermute(values, axis, [(i, (i + step) % SUB) for i in range(SUB)])


def gather_four(axis, values):
    return [values] + [shift_in(axis, values, k) for k in range(1, SUB)]


def exchange(axis, pieces):
    return lax.all_to_all(pieces, axis, 0, 0)


SMEM = pl.BlockSpec(memory_space=pltpu.SMEM)
VMEM = pl.BlockSpec(memory_space=pltpu.VMEM)


def shape(*dims, dtype=BF16):
    return jax.ShapeDtypeStruct(dims, dtype)


def call(body, outs, args, specs=None, grid=None, out_specs=None, scratch=(), flops=0, name=None):
    if specs is None:
        specs = [VMEM] * len(args)
    if out_specs is None:
        out_specs = jax.tree.map(lambda _: VMEM, outs)
    moved = sum(math.prod(a.shape) * a.dtype.itemsize for a in args)
    kwargs = {} if grid is None else {"grid": grid}
    return pl.pallas_call(
        body,
        out_shape=outs,
        in_specs=specs,
        out_specs=out_specs,
        scratch_shapes=list(scratch),
        cost_estimate=pl.CostEstimate(
            flops=flops, bytes_accessed=moved if flops else 0, transcendentals=0
        ),
        compiler_params=pltpu.CompilerParams(vmem_limit_bytes=VMEM_LIMIT),
        name=name,
        **kwargs,
    )(*args)


def back(own, step):
    return lax.rem(own + (SUB - step), SUB)


def ahead(own, step):
    return lax.rem(own + step, SUB)


def dot(left, right):
    return jnp.dot(left, right, preferred_element_type=F32)


def layer_norm_rows(values, gain):
    centre = values - jnp.mean(values, axis=-1, keepdims=True)
    spread = jnp.mean(centre * centre, axis=-1, keepdims=True)
    return (centre * lax.rsqrt(spread + NORM_EPS) * gain).astype(BF16)


def rms_norm_rows(values, gain):
    square = jnp.mean(values * values, axis=-1, keepdims=True)
    return (values * lax.rsqrt(square + NORM_EPS) * gain).astype(BF16)


def gelu(values):
    return 0.5 * values * (1.0 + lax.erf(values * (2.0**-0.5)))


def pad_heads(values):
    empty = jnp.zeros((values.shape[0], LANES - HEAD_DIM), values.dtype)
    parts = []
    for t in range(3):
        parts += [values[:, t * HEAD_DIM : (t + 1) * HEAD_DIM], empty]
    return jnp.concatenate(parts, axis=1)


def vit_attention_body(r0, r1, r2, r3, weight, gain, source, query_class, key_class, out, triple, merged, normed):
    slots = triple.shape[0]
    step = slots // SUB
    share = step // SUB
    for i, rows in enumerate((r0, r1, r2, r3)):

        def normalize(j, _):
            part = pl.ds(pl.multiple_of(j * share, share), share)
            to = pl.ds(pl.multiple_of(i * step + j * share, share), share)
            normed[to, :] = layer_norm_rows(rows[part, :].astype(F32), gain[...])
            return 0

        lax.fori_loop(0, SUB, normalize, 0)

    def project(i, _):
        part = pl.ds(pl.multiple_of(i * step, step), step)
        triple[part, :] = pad_heads(dot(normed[part, :], weight[...]).astype(BF16))
        return 0

    lax.fori_loop(0, SUB, project, 0)

    def reorder(i, _):
        at = pl.multiple_of(i * step, step)
        chosen = (
            source[pl.ds(at, step), :] == lax.broadcasted_iota(jnp.int32, (step, slots), 1)
        ).astype(BF16)
        merged[pl.ds(at, step), :] = dot(chosen, triple[...]).astype(BF16)
        return 0

    lax.fori_loop(0, SUB, reorder, 0)

    def attend(i, _):
        at = pl.multiple_of(i * step, step)
        scores = lax.dot_general(
            merged[pl.ds(at, step), :LANES],
            merged[:, LANES : 2 * LANES],
            (((1,), (1,)), ((), ())),
            preferred_element_type=F32,
        ) * HEAD_DIM ** (-0.5)
        allowed = query_class[pl.ds(at, step), :] == key_class[...]
        exp_scores = jnp.where(allowed, jnp.exp(scores), 0.0)
        denominator = jnp.sum(exp_scores, axis=1, keepdims=True)
        weighted = dot(exp_scores.astype(BF16), merged[:, 2 * LANES :])
        result = (weighted / denominator).astype(BF16)
        for q in range(SUB):
            out[i * SUB + q] = result
        return 0

    lax.fori_loop(0, SUB, attend, 0)


def pick_rows_body(source, r0, r1, r2, r3, out):
    rows = r0.shape[0]
    total = None
    for i, ref in enumerate((r0, r1, r2, r3)):
        at = lax.broadcasted_iota(jnp.int32, (source.shape[0], rows), 1) + i * rows
        term = dot((source[...] == at).astype(BF16), ref[...])
        total = term if total is None else total + term
    out[...] = total.astype(BF16)


def join_heads(blocks):
    return jnp.concatenate([block[:, :HEAD_DIM] for block in blocks], axis=1)


def out_projection_body(heads, weight, out, left, done):
    step = pl.program_id(0)

    @pl.when(step == 0)
    def _():
        left[...] = join_heads([heads[h] for h in range(SUB * SUB)])

    done[step] = dot(left[...], weight[0]).astype(BF16)

    @pl.when(step == SUB - 1)
    def _():
        out[:, : SUB * HEAD_DIM] = join_heads([done[z] for z in range(SUB)])


def hold_blocks(refs, own_q, held):
    for k, ref in enumerate(refs):
        held[back(own_q, k)] = ref[...]


def in_order(held, rows=slice(None)):
    return jnp.concatenate(
        [
            held[q, rows, z * HEAD_DIM : (z + 1) * HEAD_DIM]
            for z in range(SUB)
            for q in range(SUB)
        ],
        axis=1,
    )


def feed_forward_body(norm, place, o0, o1, o2, o3, stream, gain, weight, out, mid_out, held, mid, normed, total):
    own_q = place[2]
    step = pl.program_id(0)
    rows = stream.shape[0]
    share = rows // SUB
    hidden_width = weight.shape[2] // 2

    @pl.when(step == 0)
    def _():
        hold_blocks((o0, o1, o2, o3), own_q, held)

        def prepare(i, _):
            part = pl.ds(pl.multiple_of(i * share, share), share)
            added = in_order(held, part).astype(F32)
            summed = (stream[part, :].astype(F32) + added).astype(BF16)
            mid[part, :] = summed
            normed[part, :] = norm(summed.astype(F32), gain[...])
            return 0

        lax.fori_loop(0, SUB, prepare, 0)

    hidden = gelu(dot(normed[...], weight[0, :, :hidden_width])).astype(BF16)
    down = lax.dot_general(
        hidden,
        weight[0, :, hidden_width:],
        (((1,), (1,)), ((), ())),
        preferred_element_type=F32,
    )

    @pl.when(step == 0)
    def _():
        total[...] = down

    @pl.when((step > 0) & (step < SUB - 1))
    def _():
        total[...] += down

    @pl.when(step == SUB - 1)
    def _():
        out[...] = (total[...] + down).astype(BF16)
        mid_out[...] = mid[pl.ds(pl.multiple_of(own_q * share, share), share), :]


def summed_stream(partials, mid):
    summed = partials[0].astype(F32)
    for i in range(1, SUB):
        summed += partials[i].astype(F32)
    return (mid[...].astype(F32) + summed).astype(BF16).astype(F32)


def merge_norm_body(partials, mid, gain, out):
    rows, width = mid.shape
    final = summed_stream(partials, mid)
    row = lax.broadcasted_iota(jnp.int32, (rows, rows), 0)
    col = lax.broadcasted_iota(jnp.int32, (rows, rows), 1)
    same_group = row // 4 == col // 4

    def group_mean(column):
        across = jnp.sum(jnp.where(same_group, column, 0.0), axis=0, keepdims=True)
        down = jnp.sum(jnp.where(row == col, across, 0.0), axis=1, keepdims=True)
        return down / (4 * width)

    centre = final - group_mean(jnp.sum(final, axis=1, keepdims=True))
    spread = group_mean(jnp.sum(centre * centre, axis=1, keepdims=True))
    out[...] = (centre * lax.rsqrt(spread + NORM_EPS) * gain[...]).astype(BF16)


def merge_projection_body(place, g0, g1, g2, g3, weight, out, rows, left, done):
    own_q = place[2]
    step = pl.program_id(0)
    share = g0.shape[0]
    count = rows.shape[0]
    slots = count // 4

    @pl.when(step == 0)
    def _():
        for k, ref in enumerate((g0, g1, g2, g3)):
            rows[pl.ds(pl.multiple_of(back(own_q, k) * share, share), share), :] = ref[...]
        new_row = lax.broadcasted_iota(jnp.int32, (count, count), 0)
        old_row = lax.broadcasted_iota(jnp.int32, (count, count), 1)
        chosen = ((new_row % slots) * 4 + new_row // slots == old_row).astype(BF16)
        left[...] = dot(chosen, rows[...]).astype(BF16)

    total = dot(left[:slots, :], weight[0, :, :HEAD_DIM])
    for patch in range(1, 4):
        total += dot(
            left[patch * slots : (patch + 1) * slots, :],
            weight[0, :, patch * HEAD_DIM : (patch + 1) * HEAD_DIM],
        )
    done[step, :, :HEAD_DIM] = total.astype(BF16)

    @pl.when(step == SUB - 1)
    def _():
        projected = join_heads([done[z] for z in range(SUB)])
        for g in range(out.shape[0]):
            out[g, :, : SUB * HEAD_DIM] = projected


def text_rows_body(place, ids, table, *rest):
    outs, (total,) = rest[:SUB], rest[SUB:]
    own_q = place[2]
    step = pl.program_id(0)
    last = pl.num_programs(0) - 1
    count = table.shape[0]
    share = ids.shape[0] // SUB
    first = (place[1] * SUB + place[2]) * count * pl.num_programs(0) + step * count

    def add(i, _):
        rows = pl.ds(pl.multiple_of(i * share, share), share)
        chosen = (
            ids[rows, :] - first == lax.broadcasted_iota(jnp.int32, (share, count), 1)
        ).astype(BF16)
        found = dot(chosen, table[...])

        @pl.when(step == 0)
        def _():
            total[rows, :] = found

        @pl.when(step > 0)
        def _():
            total[rows, :] += found

        @pl.when(step == last)
        def _():
            for q in range(SUB):
                blocks = [
                    total[rows, at : at + HEAD_DIM]
                    for at in range(q * HEAD_DIM, total.shape[1], SUB * HEAD_DIM)
                ]
                columns = jnp.concatenate(blocks, axis=1).astype(BF16)
                for k in range(SUB):

                    @pl.when(ahead(own_q, k) == q)
                    def _():
                        outs[k][rows, : SUB * HEAD_DIM] = columns

        return 0

    lax.fori_loop(0, SUB, add, 0)


def place_body(seq, is_image, slot_position, projected, t0, t1, t2, t3, out):
    chosen = (seq[...] == slot_position[...]).astype(BF16)
    placed = dot(chosen, projected[...])
    text = t0[...].astype(F32) + t1[...].astype(F32) + t2[...].astype(F32) + t3[...].astype(F32)
    width = SUB * HEAD_DIM
    out[:, :width] = jnp.where(is_image[...] > 0, placed, text)[:, :width].astype(BF16)


def dec_qkv_body(place, g0, g1, g2, g3, gain, w0, w1, w2, out, embedded_out, held, normed):
    @pl.when(pl.program_id(0) == 0)
    def _():
        hold_blocks((g0, g1, g2, g3), place[2], held)
        embedded = in_order(held)
        embedded_out[...] = embedded
        normed[...] = rms_norm_rows(embedded.astype(F32), gain[...])

    result = jnp.concatenate([dot(normed[...], w[0]) for w in (w0, w1, w2)], axis=1)
    at = 4 * HEAD_DIM - 2 * LANES
    out[0] = pad_heads(result[:, at : at + 3 * HEAD_DIM].astype(BF16))


def dec_attention_body(place, triple, query_request, query_position, request, near, far, out, weighted, denominator):
    own_gx = place[0]
    tokens = triple.shape[0]
    part = tokens // 2
    weighted[...] = jnp.zeros_like(weighted)
    denominator[...] = jnp.zeros_like(denominator)

    def attend(k, blocks, core):
        owner = 2 * lax.rem(lax.div(own_gx, 2) + (SUB - k), SUB) + core

        @pl.when(owner <= own_gx)
        def _():
            key_request = request[pl.ds(owner, 1), :]
            key_position = lax.broadcasted_iota(jnp.int32, (1, tokens), 1) + owner * tokens

            def half(i, _):
                rows = pl.ds(pl.multiple_of(i * part, part), part)
                scores = lax.dot_general(
                    triple[rows, :LANES],
                    blocks[k, :, :LANES],
                    (((1,), (1,)), ((), ())),
                    preferred_element_type=F32,
                ) * HEAD_DIM ** (-0.5)
                allowed = (key_request == query_request[rows, :]) & (
                    key_position <= query_position[rows, :]
                )
                exp_scores = jnp.where(allowed, jnp.exp(scores), 0.0)
                denominator[rows, :] += jnp.sum(exp_scores, axis=1, keepdims=True)
                weighted[rows, :] += dot(exp_scores.astype(BF16), blocks[k, :, LANES:])
                return 0

            lax.fori_loop(0, 2, half, 0)

    def both(k, _):
        attend(k, near, lax.rem(own_gx, 2))
        attend(k, far, lax.rem(own_gx + 1, 2))
        return 0

    lax.fori_loop(0, SUB, both, 0)
    share = tokens // SUB
    for z in range(SUB):
        rows = slice(z * share, (z + 1) * share)
        result = (weighted[rows, :] / denominator[rows, :]).astype(BF16)
        for q in range(SUB):
            out[z * SUB + q] = result


def dec_final_body(partials, mid, gain, out):
    out[...] = rms_norm_rows(summed_stream(partials, mid), gain[...])


def next_qkv_body(place, g0, g1, g2, g3, weight, out, left, done):
    own_q = place[2]
    step = pl.program_id(0)
    share = g0.shape[0]

    @pl.when(step == 0)
    def _():
        for k, ref in enumerate((g0, g1, g2, g3)):
            left[pl.ds(pl.multiple_of(back(own_q, k) * share, share), share), :] = ref[...]

    done[step] = dot(left[...], weight[0]).astype(BF16)

    @pl.when(step == SUB - 1)
    def _():
        out[:, : 3 * SUB * HEAD_DIM] = jnp.concatenate(
            [done[z, :, HEAD_DIM : 4 * HEAD_DIM] for z in range(SUB)], axis=1
        )


def finish_body(received, out):
    for t in range(3):
        parts = []
        for z in range(SUB):
            at = (3 * z + t) * HEAD_DIM
            parts += [received[q, :, at : at + HEAD_DIM] for q in range(SUB)]
        out[t] = jnp.concatenate(parts, axis=1)


def pad_to(values, width):
    return jnp.pad(values, ((0, 0), (0, width - values.shape[1])))


def flat_rows(values):
    return values.reshape(values.shape[0], -1)


def block_spec(rows, width, at):
    return pl.BlockSpec((1, rows, width), lambda z: (z, 0, at))


def whole(values):
    rank = values.ndim
    return pl.BlockSpec(values.shape, lambda z: (0,) * rank)


def fixed(struct):
    rank = len(struct.shape)
    return pl.BlockSpec(struct.shape, lambda z: (0,) * rank)


def per_device(
    patches,
    grids,
    text_ids,
    positions,
    lengths,
    text_table,
    vit_norm1,
    vit_qkv,
    vit_out,
    vit_norm2,
    vit_fc1,
    vit_fc2,
    merge_norm,
    merge_proj,
    dec_norm1,
    dec_qkv,
    dec_out,
    dec_norm2,
    dec_fc1,
    dec_fc2,
    next_norm,
    next_qkv,
):
    gx_count = lax.axis_size("gx")
    own_gx, own_z, own_q = lax.axis_index("gx"), lax.axis_index("gz"), lax.axis_index("gq")
    place = jnp.stack([own_gx, own_z, own_q]).astype(jnp.int32)
    width = patches.shape[1]
    share = patches.shape[0]
    slots = share * SUB * SUB

    def gather_weights(parts, lanes):
        columns = []
        for p in parts:
            columns += [p] if p.ndim == 2 else [p[:, t] for t in range(p.shape[1])]
        used = sum(c.shape[1] for c in columns)
        columns.append(jnp.zeros((columns[0].shape[0], lanes - used), BF16))
        local = jnp.concatenate([c for c in columns if c.shape[1]], axis=1)
        full = lax.all_gather(local, ("gz", "gx"), axis=0, tiled=True)
        return full.reshape(SUB, width, lanes)

    vit_weights = gather_weights([vit_fc1, vit_fc2, vit_out], 896)

    per_group = grids.shape[0] // gx_count
    own_grids = lax.dynamic_slice_in_dim(grids, own_gx * per_group, per_group, 0)
    merge_slots = positions.shape[0] // gx_count
    sources, image_of, is_live = merge_sources(own_grids, merge_slots)
    holder = sources // share
    block = lax.rem(own_q + SUB - lax.rem(holder, SUB), SUB) * SUB + lax.rem(
        own_z + SUB - holder // SUB, SUB
    )
    source_column = (block * share + lax.rem(sources, share)).reshape(slots, 1)
    query_class = jnp.repeat(jnp.where(is_live, image_of, 0), 4).reshape(slots, 1)
    key_class = jnp.repeat(image_of, 4).reshape(1, slots)

    of_column = jnp.stack(gather_four("gz", patches))
    of_column, source_column, query_class, key_class, own_qkv, ids = lax.optimization_barrier(
        (of_column, source_column, query_class, key_class, flat_rows(vit_qkv), text_ids)
    )
    patches_full = [
        rows.reshape(SUB * share, width) for rows in gather_four("gq", of_column)
    ]
    qkv_weight = lax.all_gather(own_qkv, "gx", axis=0, tiled=True)

    tokens = text_ids.shape[0]
    part = tokens // SUB
    block_width = SUB * HEAD_DIM
    block_lanes = 3 * LANES
    table_step = text_table.shape[0] // 5
    text_blocks = call(
        text_rows_body,
        [shape(tokens, block_lanes)] * SUB,
        (place, ids.reshape(tokens, 1), text_table),
        specs=[
            SMEM,
            pl.BlockSpec((tokens, 1), lambda i: (0, 0)),
            pl.BlockSpec((table_step, width), lambda i: (i, 0)),
        ],
        grid=(5,),
        out_specs=[pl.BlockSpec((tokens, block_lanes), lambda i: (0, 0))] * SUB,
        scratch=[pltpu.VMEM((tokens, width), F32)],
        name="text_rows",
    )
    qkv_weight, text_blocks, patches_full = lax.optimization_barrier(
        (qkv_weight, text_blocks, patches_full)
    )
    text_parts = [text_blocks[0], shift_in("gq", text_blocks[2], 2)]

    row = lambda gain: gain.reshape(1, -1)
    group_rows = slots // SUB
    attended = call(
        vit_attention_body,
        shape(SUB * SUB, group_rows, LANES),
        (*patches_full, qkv_weight, row(vit_norm1), source_column, query_class, key_class),
        scratch=[
            pltpu.VMEM((slots, 3 * LANES), BF16),
            pltpu.VMEM((slots, 3 * LANES), BF16),
            pltpu.VMEM((slots, width), BF16),
        ],
        flops=2 * slots * (width * 3 * LANES + slots * 5 * LANES),
        name="vit_attention",
    )
    attended, text_parts, mid_parts, dec_parts = lax.optimization_barrier(
        (attended, text_parts, [merge_proj, dec_qkv], [dec_fc1, dec_fc2, dec_out, next_qkv])
    )
    mid_weights = gather_weights(mid_parts, 640)
    dec_weights = gather_weights(dec_parts, 1152)
    own_sources = lax.dynamic_slice_in_dim(source_column, own_z * group_rows, group_rows, 0)
    stream = call(
        pick_rows_body,
        shape(group_rows, width),
        (own_sources, *patches_full),
        flops=2 * slots * group_rows * width,
        name="pick_rows",
    )

    def attention_output(attended, weights, name):
        heads = exchange(("gz", "gq"), attended)
        rows = heads.shape[1]
        return call(
            out_projection_body,
            shape(rows, block_lanes),
            (heads, weights),
            specs=[whole(heads), block_spec(width, LANES, 6)],
            grid=(SUB,),
            out_specs=pl.BlockSpec((rows, block_lanes), lambda z: (0, 0)),
            scratch=[pltpu.VMEM((rows, width), BF16), pltpu.VMEM((SUB, rows, LANES), BF16)],
            flops=2 * rows * width * SUB * LANES,
            name=name,
        )

    def feed_forward(projected, stream, gain, weights, norm, name, beside=()):
        rows = stream.shape[0]
        own = rows // SUB
        gathered = gather_four("gq", projected)
        gathered, travel = lax.optimization_barrier((gathered, [value for _, value in beside]))
        arrived = [shift_in("gq", value, k) for (k, _), value in zip(beside, travel)]
        hidden_width = vit_fc1.shape[1]
        outs = [shape(rows, width), shape(own, width)]
        partial, mid = call(
            functools.partial(feed_forward_body, norm),
            outs,
            (place, *gathered, stream, gain, weights),
            specs=[SMEM]
            + [whole(g) for g in gathered]
            + [whole(stream), whole(gain), block_spec(width, 2 * hidden_width, 0)],
            grid=(SUB,),
            out_specs=[fixed(o) for o in outs],
            scratch=[
                pltpu.VMEM((SUB, rows, block_lanes), BF16),
                pltpu.VMEM((rows, width), BF16),
                pltpu.VMEM((rows, width), BF16),
                pltpu.VMEM((rows, width), F32),
            ],
            flops=4 * rows * width * SUB * hidden_width,
            name=name,
        )
        partial, arrived = lax.optimization_barrier((partial, arrived))
        return exchange("gq", partial.reshape(SUB, own, width)), mid, arrived

    projected = attention_output(attended, vit_weights, "vit_output")
    partials, mid, arrived = feed_forward(
        projected,
        stream,
        row(vit_norm2),
        vit_weights,
        layer_norm_rows,
        "vit_feed_forward",
        [(1, text_blocks[1]), (3, text_blocks[3])],
    )
    text_parts += arrived

    gain_rows = jnp.tile(merge_norm, (share // 4, 1))
    merged = call(merge_norm_body, shape(share, width), (partials, mid, gain_rows), name="merge_norm")
    gathered = gather_four("gq", merged)
    group_slots = group_rows // 4
    outs = shape(gx_count, group_slots, block_lanes)
    projected = call(
        merge_projection_body,
        outs,
        (place, *gathered, mid_weights),
        specs=[SMEM] + [whole(g) for g in gathered] + [block_spec(width, 384, 0)],
        grid=(SUB,),
        out_specs=fixed(outs),
        scratch=[
            pltpu.VMEM((group_rows, width), BF16),
            pltpu.VMEM((group_rows, width), BF16),
            pltpu.VMEM((SUB, group_slots, LANES), BF16),
        ],
        flops=2 * group_rows * width * SUB * LANES,
        name="merge_projection",
    )
    all_projected = exchange("gx", projected).reshape(gx_count * group_slots, block_lanes)

    own_index = own_gx * tokens + jnp.arange(tokens, dtype=jnp.int32)
    is_image = jnp.any(positions[None, :] == own_index[:, None], axis=1).astype(F32)
    by_slot = lax.dynamic_index_in_dim(
        positions.reshape(gx_count, SUB, group_slots), own_z, 1, keepdims=False
    )
    placed = call(
        place_body,
        shape(tokens, block_lanes),
        (
            own_index.reshape(tokens, 1),
            is_image.reshape(tokens, 1),
            by_slot.reshape(1, -1),
            all_projected,
            *text_parts,
        ),
        flops=2 * tokens * by_slot.size * block_width,
        name="place_rows",
    )
    own_rows = jnp.sum(
        exchange("gz", placed.reshape(SUB, part, block_lanes)).astype(F32), axis=0
    ).astype(BF16)
    gathered = gather_four("gq", own_rows)

    outs = [shape(SUB, part, 3 * LANES), shape(part, width)]
    triple, embedded = call(
        dec_qkv_body,
        outs,
        (place, *gathered, row(dec_norm1), mid_weights, mid_weights, mid_weights),
        specs=[SMEM]
        + [whole(a) for a in (*gathered, row(dec_norm1))]
        + [block_spec(width, LANES, at) for at in (2, 3, 4)],
        grid=(SUB,),
        out_specs=[pl.BlockSpec((1, part, 3 * LANES), lambda z: (z, 0, 0)), fixed(outs[1])],
        scratch=[pltpu.VMEM((SUB, part, block_lanes), BF16), pltpu.VMEM((part, width), BF16)],
        flops=2 * part * width * SUB * 3 * LANES,
        name="dec_qkv",
    )
    triple = exchange("gz", triple).reshape(tokens, 3 * LANES)
    key_values = triple[:, LANES:]
    near = jnp.stack(
        [key_values]
        + [
            lax.ppermute(
                key_values,
                "gx",
                [(2 * y + c, 2 * ((y + k) % SUB) + c) for y in range(SUB) for c in range(2)],
            )
            for k in range(1, SUB)
        ]
    )
    far = lax.ppermute(near, "gx", [(i, i ^ 1) for i in range(gx_count)])
    bounds = jnp.cumsum(lengths)
    all_index = jnp.arange(gx_count * tokens, dtype=jnp.int32).reshape(gx_count, tokens)
    request = jnp.sum((all_index[:, :, None] >= bounds).astype(jnp.int32), axis=2)
    own_request = jnp.sum((own_index[:, None] >= bounds).astype(jnp.int32), axis=1)
    attended = call(
        dec_attention_body,
        shape(SUB * SUB, part, LANES),
        (
            place,
            triple,
            own_request.reshape(tokens, 1),
            own_index.reshape(tokens, 1),
            request,
            near,
            far,
        ),
        specs=[SMEM] + [VMEM] * 6,
        scratch=[pltpu.VMEM((tokens, LANES), F32), pltpu.VMEM((tokens, 1), F32)],
        flops=4 * tokens * tokens * gx_count * LANES,
        name="dec_attention",
    )
    projected = attention_output(attended, dec_weights, "dec_output")
    partials, mid, _ = feed_forward(
        projected, embedded, row(dec_norm2), dec_weights, rms_norm_rows, "dec_feed_forward"
    )
    own_tokens = mid.shape[0]
    normed = call(
        dec_final_body, shape(own_tokens, width), (partials, mid, row(next_norm)), name="dec_final"
    )

    gathered = gather_four("gq", normed)
    triple = call(
        next_qkv_body,
        shape(part, 3 * block_lanes),
        (place, *gathered, dec_weights),
        specs=[SMEM] + [whole(g) for g in gathered] + [block_spec(width, 3 * LANES, 2)],
        grid=(SUB,),
        out_specs=pl.BlockSpec((part, 3 * block_lanes), lambda z: (0, 0)),
        scratch=[pltpu.VMEM((part, width), BF16), pltpu.VMEM((SUB, part, 3 * LANES), BF16)],
        flops=2 * part * width * SUB * 3 * LANES,
        name="next_qkv",
    )
    received = exchange("gq", triple.reshape(SUB, own_tokens, 3 * block_lanes))
    finished = call(finish_body, shape(3, own_tokens, width), (received,), name="finish")
    return finished.transpose(1, 0, 2)


def solution(mesh):
    gx_size = mesh.shape["gx"]
    cut = Mesh(mesh.devices.reshape(gx_size, SUB, SUB), ("gx", "gz", "gq"))
    gy = ("gz", "gq")
    flat = P("gx", gy)
    deep = P("gx", None, gy)
    placed = (
        P(("gx", *gy), None),
        P(),
        P("gx"),
        P(),
        P(),
        P(gy, None),
        P(),
        deep,
        flat,
        P(),
        flat,
        flat,
        P(),
        deep,
        P(),
        deep,
        flat,
        P(),
        flat,
        flat,
        P(),
        deep,
    )
    return jax.shard_map(
        per_device,
        mesh=cut,
        in_specs=placed,
        out_specs=P(("gx", *gy), None, None),
        check_vma=False,
    )
```

```python
import functools
import math

import jax
import jax.numpy as jnp
from jax import lax
from jax.experimental import pallas as pl
from jax.experimental.pallas import tpu as pltpu
from jax.sharding import Mesh, PartitionSpec as P

HEAD_DIM = 88
LANES = 128
SUB = 4
NORM_EPS = 1e-06
F32 = jnp.float32
BF16 = jnp.bfloat16
VMEM_LIMIT = 50 * 1024 * 1024


def merge_sources(grid_rows, merge_slots):
    image_count = grid_rows.shape[0]
    merged_count = grid_rows[:, 0] * grid_rows[:, 1]
    merged_end = jnp.cumsum(merged_count)
    merged_start = merged_end - merged_count
    slot_index = jnp.arange(merge_slots, dtype=jnp.int32)
    image_of = jnp.sum((slot_index[:, None] >= merged_end[None, :]).astype(jnp.int32), axis=1)
    is_live = image_of < image_count
    picked = (
        jnp.minimum(image_of, image_count - 1)[:, None]
        == jnp.arange(image_count, dtype=jnp.int32)[None, :]
    ).astype(jnp.int32)
    col_count = jnp.sum(picked * grid_rows[None, :, 1], axis=1)
    first_slot = jnp.sum(picked * merged_start[None, :], axis=1)
    local_slot = slot_index - first_slot
    grid_row = local_slot // col_count
    grid_col = local_slot % col_count
    base_row = 4 * first_slot + 4 * grid_row * col_count + 2 * grid_col
    offsets = jnp.stack(
        [jnp.zeros_like(col_count), jnp.ones_like(col_count), 2 * col_count, 2 * col_count + 1],
        axis=1,
    )
    sources = jnp.where(is_live[:, None], base_row[:, None] + offsets, 0)
    return sources, image_of, is_live


def shift_in(axis, values, step):
    return lax.ppermute(values, axis, [(i, (i + step) % SUB) for i in range(SUB)])


def gather_four(axis, values):
    return [values] + [shift_in(axis, values, k) for k in range(1, SUB)]


def exchange(axis, pieces):
    return lax.all_to_all(pieces, axis, 0, 0)


def collect(axis, values, size):
    return exchange(axis, jnp.broadcast_to(values, (size,) + values.shape))


SMEM = pl.BlockSpec(memory_space=pltpu.SMEM)
VMEM = pl.BlockSpec(memory_space=pltpu.VMEM)


def shape(*dims, dtype=BF16):
    return jax.ShapeDtypeStruct(dims, dtype)


def call(body, outs, args, specs=None, grid=None, out_specs=None, scratch=(), flops=0, name=None):
    if specs is None:
        specs = [VMEM] * len(args)
    if out_specs is None:
        out_specs = jax.tree.map(lambda _: VMEM, outs)
    moved = sum(math.prod(a.shape) * a.dtype.itemsize for a in args)
    kwargs = {} if grid is None else {"grid": grid}
    return pl.pallas_call(
        body,
        out_shape=outs,
        in_specs=specs,
        out_specs=out_specs,
        scratch_shapes=list(scratch),
        cost_estimate=pl.CostEstimate(
            flops=flops, bytes_accessed=moved if flops else 0, transcendentals=0
        ),
        compiler_params=pltpu.CompilerParams(vmem_limit_bytes=VMEM_LIMIT),
        name=name,
        **kwargs,
    )(*args)


def back(own, step):
    return lax.rem(own + (SUB - step), SUB)


def ahead(own, step):
    return lax.rem(own + step, SUB)


def dot(left, right):
    return jnp.dot(left, right, preferred_element_type=F32)


def layer_norm_rows(values, gain):
    centre = values - jnp.mean(values, axis=-1, keepdims=True)
    spread = jnp.mean(centre * centre, axis=-1, keepdims=True)
    return (centre * lax.rsqrt(spread + NORM_EPS) * gain).astype(BF16)


def rms_norm_rows(values, gain):
    square = jnp.mean(values * values, axis=-1, keepdims=True)
    return (values * lax.rsqrt(square + NORM_EPS) * gain).astype(BF16)


def gelu(values):
    return 0.5 * values * (1.0 + lax.erf(values * (2.0**-0.5)))


def pad_heads(values):
    empty = jnp.zeros((values.shape[0], LANES - HEAD_DIM), values.dtype)
    parts = []
    for t in range(3):
        parts += [values[:, t * HEAD_DIM : (t + 1) * HEAD_DIM], empty]
    return jnp.concatenate(parts, axis=1)


def vit_attention_body(r0, r1, r2, r3, weight, gain, source, query_class, key_class, out, triple, merged):
    slots = triple.shape[0]
    step = slots // SUB
    for i, rows in enumerate((r0, r1, r2, r3)):
        normed = layer_norm_rows(rows[...].astype(F32), gain[...])
        triple[i * step : (i + 1) * step, :] = pad_heads(dot(normed, weight[...]).astype(BF16))

    def reorder(i, _):
        part = pl.ds(pl.multiple_of(i * step, step), step)
        chosen = (
            source[part, :] == lax.broadcasted_iota(jnp.int32, (step, slots), 1)
        ).astype(BF16)
        merged[part, :] = dot(chosen, triple[...]).astype(BF16)
        return 0

    lax.fori_loop(0, SUB, reorder, 0)
    for i in range(SUB):
        at = i * step
        scores = lax.dot_general(
            merged[at : at + step, :LANES],
            merged[:, LANES : 2 * LANES],
            (((1,), (1,)), ((), ())),
            preferred_element_type=F32,
        ) * HEAD_DIM ** (-0.5)
        allowed = query_class[at : at + step, :] == key_class[...]
        exp_scores = jnp.where(allowed, jnp.exp(scores), 0.0)
        denominator = jnp.sum(exp_scores, axis=1, keepdims=True)
        weighted = dot(exp_scores.astype(BF16), merged[:, 2 * LANES :])
        result = (weighted / denominator).astype(BF16)
        for q in range(SUB):
            out[i * SUB + q] = result


def pick_rows_body(source, r0, r1, r2, r3, out):
    rows = r0.shape[0]
    total = None
    for i, ref in enumerate((r0, r1, r2, r3)):
        at = lax.broadcasted_iota(jnp.int32, (source.shape[0], rows), 1) + i * rows
        term = dot((source[...] == at).astype(BF16), ref[...])
        total = term if total is None else total + term
    out[...] = total.astype(BF16)


def join_heads(blocks):
    return jnp.concatenate([block[:, :HEAD_DIM] for block in blocks], axis=1)


def out_projection_body(heads, weight, out, left, done):
    step = pl.program_id(0)

    @pl.when(step == 0)
    def _():
        left[...] = join_heads([heads[h] for h in range(SUB * SUB)])

    done[step] = dot(left[...], weight[0]).astype(BF16)

    @pl.when(step == SUB - 1)
    def _():
        out[:, : SUB * HEAD_DIM] = join_heads([done[z] for z in range(SUB)])


def hold_blocks(refs, own_q, held):
    for k, ref in enumerate(refs):
        held[back(own_q, k)] = ref[...]


def in_order(held, rows=slice(None)):
    return jnp.concatenate(
        [
            held[q, rows, z * HEAD_DIM : (z + 1) * HEAD_DIM]
            for z in range(SUB)
            for q in range(SUB)
        ],
        axis=1,
    )


def feed_forward_body(norm, place, o0, o1, o2, o3, stream, gain, weight, out, mid_out, held, mid, normed, total):
    own_q = place[2]
    step = pl.program_id(0)
    rows = stream.shape[0]
    share = rows // SUB
    hidden_width = weight.shape[2] // 2

    @pl.when(step == 0)
    def _():
        hold_blocks((o0, o1, o2, o3), own_q, held)

        def prepare(i, _):
            part = pl.ds(pl.multiple_of(i * 2 * share, 2 * share), 2 * share)
            added = in_order(held, part).astype(F32)
            summed = (stream[part, :].astype(F32) + added).astype(BF16)
            mid[part, :] = summed
            normed[part, :] = norm(summed.astype(F32), gain[...])
            return 0

        lax.fori_loop(0, SUB // 2, prepare, 0)

    hidden = gelu(dot(normed[...], weight[0, :, :hidden_width])).astype(BF16)
    down = lax.dot_general(
        hidden,
        weight[0, :, hidden_width:],
        (((1,), (1,)), ((), ())),
        preferred_element_type=F32,
    )

    @pl.when(step == 0)
    def _():
        total[...] = down

    @pl.when((step > 0) & (step < SUB - 1))
    def _():
        total[...] += down

    @pl.when(step == SUB - 1)
    def _():
        out[...] = (total[...] + down).astype(BF16)
        mid_out[...] = mid[pl.ds(pl.multiple_of(own_q * share, share), share), :]


def summed_stream(partials, mid):
    summed = partials[0].astype(F32)
    for i in range(1, SUB):
        summed += partials[i].astype(F32)
    return (mid[...].astype(F32) + summed).astype(BF16).astype(F32)


def merge_norm_body(partials, mid, gain, out):
    rows, width = mid.shape
    final = summed_stream(partials, mid)
    row = lax.broadcasted_iota(jnp.int32, (rows, rows), 0)
    col = lax.broadcasted_iota(jnp.int32, (rows, rows), 1)
    same_group = row // 4 == col // 4

    def group_mean(column):
        across = jnp.sum(jnp.where(same_group, column, 0.0), axis=0, keepdims=True)
        down = jnp.sum(jnp.where(row == col, across, 0.0), axis=1, keepdims=True)
        return down / (4 * width)

    centre = final - group_mean(jnp.sum(final, axis=1, keepdims=True))
    spread = group_mean(jnp.sum(centre * centre, axis=1, keepdims=True))
    out[...] = (centre * lax.rsqrt(spread + NORM_EPS) * gain[...]).astype(BF16)


def merge_projection_body(place, g0, g1, g2, g3, weight, out, rows, left, done):
    own_q = place[2]
    step = pl.program_id(0)
    share = g0.shape[0]
    count = rows.shape[0]
    slots = count // 4

    @pl.when(step == 0)
    def _():
        for k, ref in enumerate((g0, g1, g2, g3)):
            rows[pl.ds(pl.multiple_of(back(own_q, k) * share, share), share), :] = ref[...]
        new_row = lax.broadcasted_iota(jnp.int32, (count, count), 0)
        old_row = lax.broadcasted_iota(jnp.int32, (count, count), 1)
        chosen = ((new_row % slots) * 4 + new_row // slots == old_row).astype(BF16)
        left[...] = dot(chosen, rows[...]).astype(BF16)

    total = dot(left[:slots, :], weight[0, :, :HEAD_DIM])
    for patch in range(1, 4):
        total += dot(
            left[patch * slots : (patch + 1) * slots, :],
            weight[0, :, patch * HEAD_DIM : (patch + 1) * HEAD_DIM],
        )
    done[step, :, :HEAD_DIM] = total.astype(BF16)

    @pl.when(step == SUB - 1)
    def _():
        projected = join_heads([done[z] for z in range(SUB)])
        for g in range(out.shape[0]):
            out[g, :, : SUB * HEAD_DIM] = projected


def text_rows_body(place, ids, table, *rest):
    outs, (total,) = rest[:SUB], rest[SUB:]
    own_q = place[2]
    step = pl.program_id(0)
    last = pl.num_programs(0) - 1
    count = table.shape[0]
    tokens = ids.shape[0]
    share = tokens // SUB
    first = (place[1] * SUB + own_q) * count * pl.num_programs(0) + step * count
    chosen = (ids[...] - first == lax.broadcasted_iota(jnp.int32, (tokens, count), 1)).astype(BF16)
    found = dot(chosen, table[...])

    @pl.when(step == 0)
    def _():
        total[...] = found

    @pl.when(step > 0)
    def _():
        total[...] += found

    @pl.when(step == last)
    def _():
        def hand_out(i, _):
            rows = pl.ds(pl.multiple_of(i * share, share), share)
            for q in range(SUB):
                blocks = [
                    total[rows, at : at + HEAD_DIM]
                    for at in range(q * HEAD_DIM, total.shape[1], SUB * HEAD_DIM)
                ]
                columns = jnp.concatenate(blocks, axis=1).astype(BF16)
                for k in range(SUB):

                    @pl.when(ahead(own_q, k) == q)
                    def _():
                        outs[k][rows, : SUB * HEAD_DIM] = columns

            return 0

        lax.fori_loop(0, SUB, hand_out, 0)


def place_body(seq, is_image, slot_position, projected, t0, t1, t2, t3, out):
    chosen = (seq[...] == slot_position[...]).astype(BF16)
    placed = dot(chosen, projected[...])
    text = t0[...].astype(F32) + t1[...].astype(F32) + t2[...].astype(F32) + t3[...].astype(F32)
    width = SUB * HEAD_DIM
    out[:, :width] = jnp.where(is_image[...] > 0, placed, text)[:, :width].astype(BF16)


def dec_qkv_body(place, g0, g1, g2, g3, gain, w0, w1, w2, out, embedded_out, held, normed):
    @pl.when(pl.program_id(0) == 0)
    def _():
        hold_blocks((g0, g1, g2, g3), place[2], held)
        embedded = in_order(held)
        embedded_out[...] = embedded
        normed[...] = rms_norm_rows(embedded.astype(F32), gain[...])

    result = jnp.concatenate([dot(normed[...], w[0]) for w in (w0, w1, w2)], axis=1)
    at = 4 * HEAD_DIM - 2 * LANES
    out[0] = pad_heads(result[:, at : at + 3 * HEAD_DIM].astype(BF16))


def attend_blocks(own_gx, core, triple, query_request, query_position, request, blocks, weighted, denominator):
    tokens = triple.shape[0]
    part = tokens // 2

    def attend(k, _):
        owner = 2 * lax.rem(lax.div(own_gx, 2) + (SUB - k), SUB) + core

        @pl.when(owner <= own_gx)
        def _():
            key_request = request[pl.ds(owner, 1), :]
            key_position = lax.broadcasted_iota(jnp.int32, (1, tokens), 1) + owner * tokens
            for at in range(0, tokens, part):
                rows = slice(at, at + part)
                scores = lax.dot_general(
                    triple[rows, :LANES],
                    blocks[k, :, :LANES],
                    (((1,), (1,)), ((), ())),
                    preferred_element_type=F32,
                ) * HEAD_DIM ** (-0.5)
                allowed = (key_request == query_request[rows, :]) & (
                    key_position <= query_position[rows, :]
                )
                exp_scores = jnp.where(allowed, jnp.exp(scores), 0.0)
                denominator[rows, :] += jnp.sum(exp_scores, axis=1, keepdims=True)
                weighted[rows, :] += dot(exp_scores.astype(BF16), blocks[k, :, LANES:])

        return 0

    lax.fori_loop(0, SUB, attend, 0)


def near_attention_body(place, triple, query_request, query_position, request, near, weighted, denominator):
    weighted[...] = jnp.zeros_like(weighted)
    denominator[...] = jnp.zeros_like(denominator)
    attend_blocks(
        place[0], lax.rem(place[0], 2), triple, query_request, query_position, request, near, weighted, denominator
    )


def far_attention_body(
    place, triple, query_request, query_position, request, far, near_weighted, near_denominator, out, weighted, denominator
):
    weighted[...] = near_weighted[...]
    denominator[...] = near_denominator[...]
    attend_blocks(
        place[0], lax.rem(place[0] + 1, 2), triple, query_request, query_position, request, far, weighted, denominator
    )
    share = triple.shape[0] // SUB
    for z in range(SUB):
        rows = slice(z * share, (z + 1) * share)
        result = (weighted[rows, :] / denominator[rows, :]).astype(BF16)
        for q in range(SUB):
            out[z * SUB + q] = result


def dec_final_body(partials, mid, gain, out):
    out[...] = rms_norm_rows(summed_stream(partials, mid), gain[...])


def next_qkv_body(place, g0, g1, g2, g3, weight, out, left, done):
    own_q = place[2]
    step = pl.program_id(0)
    share = g0.shape[0]

    @pl.when(step == 0)
    def _():
        for k, ref in enumerate((g0, g1, g2, g3)):
            left[pl.ds(pl.multiple_of(back(own_q, k) * share, share), share), :] = ref[...]

    done[step] = dot(left[...], weight[0]).astype(BF16)

    @pl.when(step == SUB - 1)
    def _():
        out[:, : 3 * SUB * HEAD_DIM] = jnp.concatenate(
            [done[z, :, HEAD_DIM : 4 * HEAD_DIM] for z in range(SUB)], axis=1
        )


def finish_body(received, out):
    for t in range(3):
        parts = []
        for z in range(SUB):
            at = (3 * z + t) * HEAD_DIM
            parts += [received[q, :, at : at + HEAD_DIM] for q in range(SUB)]
        out[t] = jnp.concatenate(parts, axis=1)


def block_spec(rows, width, at):
    return pl.BlockSpec((1, rows, width), lambda z: (z, 0, at))


def whole(values):
    rank = values.ndim
    return pl.BlockSpec(values.shape, lambda z: (0,) * rank)


def fixed(struct):
    rank = len(struct.shape)
    return pl.BlockSpec(struct.shape, lambda z: (0,) * rank)


def per_device(
    patches,
    grids,
    text_ids,
    positions,
    lengths,
    text_table,
    vit_norm1,
    vit_qkv,
    vit_out,
    vit_norm2,
    vit_fc1,
    vit_fc2,
    merge_norm,
    merge_proj,
    dec_norm1,
    dec_qkv,
    dec_out,
    dec_norm2,
    dec_fc1,
    dec_fc2,
    next_norm,
    next_qkv,
):
    gx_count = lax.axis_size("gx")
    own_gx, own_z, own_q = lax.axis_index("gx"), lax.axis_index("gz"), lax.axis_index("gq")
    place = jnp.stack([own_gx, own_z, own_q]).astype(jnp.int32)
    width = patches.shape[1]
    share = patches.shape[0]
    slots = share * SUB * SUB

    def gather_weights(parts, lanes):
        columns = []
        for p in parts:
            columns += [p] if p.ndim == 2 else [p[:, t] for t in range(p.shape[1])]
        used = sum(c.shape[1] for c in columns)
        columns.append(jnp.zeros((columns[0].shape[0], lanes - used), BF16))
        local = jnp.concatenate([c for c in columns if c.shape[1]], axis=1)
        full = lax.all_gather(local, ("gz", "gx"), axis=0, tiled=True)
        return full.reshape(SUB, width, lanes)

    vit_weights = gather_weights([vit_fc1, vit_fc2, vit_out], 896)

    per_group = grids.shape[0] // gx_count
    own_grids = lax.dynamic_slice_in_dim(grids, own_gx * per_group, per_group, 0)
    merge_slots = positions.shape[0] // gx_count
    sources, image_of, is_live = merge_sources(own_grids, merge_slots)
    holder = sources // share
    block = lax.rem(own_q + SUB - lax.rem(holder, SUB), SUB) * SUB + lax.rem(
        own_z + SUB - holder // SUB, SUB
    )
    source_column = (block * share + lax.rem(sources, share)).reshape(slots, 1)
    query_class = jnp.repeat(jnp.where(is_live, image_of, 0), 4).reshape(slots, 1)
    key_class = jnp.repeat(image_of, 4).reshape(1, slots)

    of_column = jnp.stack(gather_four("gz", patches))
    of_column, source_column, query_class, key_class, qkv_parts, ids = lax.optimization_barrier(
        (of_column, source_column, query_class, key_class, vit_qkv, text_ids)
    )
    patches_full = [
        rows.reshape(SUB * share, width) for rows in gather_four("gq", of_column)
    ]
    own_qkv = jnp.concatenate([qkv_parts[:, t] for t in range(3)], axis=1)
    qkv_weight = collect("gx", own_qkv, gx_count).reshape(width, own_qkv.shape[1])

    tokens = text_ids.shape[0]
    part = tokens // SUB
    block_width = SUB * HEAD_DIM
    block_lanes = 3 * LANES
    table_step = text_table.shape[0] // 5
    text_blocks = call(
        text_rows_body,
        [shape(tokens, block_lanes)] * SUB,
        (place, ids.reshape(tokens, 1), text_table),
        specs=[
            SMEM,
            pl.BlockSpec((tokens, 1), lambda i: (0, 0)),
            pl.BlockSpec((table_step, width), lambda i: (i, 0)),
        ],
        grid=(5,),
        out_specs=[pl.BlockSpec((tokens, block_lanes), lambda i: (0, 0))] * SUB,
        scratch=[pltpu.VMEM((tokens, width), F32)],
        flops=2 * tokens * text_table.shape[0] * width,
        name="text_rows",
    )
    qkv_weight, text_blocks, patches_full = lax.optimization_barrier(
        (qkv_weight, text_blocks, patches_full)
    )
    text_parts = [text_blocks[0], shift_in("gq", text_blocks[2], 2)]

    row = lambda gain: gain.reshape(1, -1)
    group_rows = slots // SUB
    attended = call(
        vit_attention_body,
        shape(SUB * SUB, group_rows, LANES),
        (*patches_full, qkv_weight, row(vit_norm1), source_column, query_class, key_class),
        scratch=[
            pltpu.VMEM((slots, 3 * LANES), BF16),
            pltpu.VMEM((slots, 3 * LANES), BF16),
        ],
        flops=2 * slots * (width * 3 * LANES + slots * 5 * LANES),
        name="vit_attention",
    )
    attended, text_parts, mid_parts, dec_parts = lax.optimization_barrier(
        (attended, text_parts, [merge_proj, dec_qkv], [dec_fc1, dec_fc2, dec_out, next_qkv])
    )
    mid_weights = gather_weights(mid_parts, 640)
    dec_weights = gather_weights(dec_parts, 1152)
    own_sources = lax.dynamic_slice_in_dim(source_column, own_z * group_rows, group_rows, 0)
    stream = call(
        pick_rows_body,
        shape(group_rows, width),
        (own_sources, *patches_full),
        flops=2 * slots * group_rows * width,
        name="pick_rows",
    )

    def attention_output(attended, weights, name, beside=()):
        heads = exchange(("gz", "gq"), attended)
        heads, beside = lax.optimization_barrier((heads, beside))
        rows = heads.shape[1]
        return call(
            out_projection_body,
            shape(rows, block_lanes),
            (heads, weights),
            specs=[whole(heads), block_spec(width, LANES, 6)],
            grid=(SUB,),
            out_specs=pl.BlockSpec((rows, block_lanes), lambda z: (0, 0)),
            scratch=[pltpu.VMEM((rows, width), BF16), pltpu.VMEM((SUB, rows, LANES), BF16)],
            flops=2 * rows * width * SUB * LANES,
            name=name,
        ), beside

    def feed_forward(projected, stream, gain, weights, norm, name, beside=()):
        rows = stream.shape[0]
        own = rows // SUB
        gathered = gather_four("gq", projected)
        gathered, travel = lax.optimization_barrier((gathered, [value for _, value in beside]))
        arrived = [shift_in("gq", value, k) for (k, _), value in zip(beside, travel)]
        hidden_width = vit_fc1.shape[1]
        outs = [shape(rows, width), shape(own, width)]
        partial, mid = call(
            functools.partial(feed_forward_body, norm),
            outs,
            (place, *gathered, stream, gain, weights),
            specs=[SMEM]
            + [whole(g) for g in gathered]
            + [whole(stream), whole(gain), block_spec(width, 2 * hidden_width, 0)],
            grid=(SUB,),
            out_specs=[fixed(o) for o in outs],
            scratch=[
                pltpu.VMEM((SUB, rows, block_lanes), BF16),
                pltpu.VMEM((rows, width), BF16),
                pltpu.VMEM((rows, width), BF16),
                pltpu.VMEM((rows, width), F32),
            ],
            flops=4 * rows * width * SUB * hidden_width,
            name=name,
        )
        partial, arrived = lax.optimization_barrier((partial, arrived))
        return exchange("gq", partial.reshape(SUB, own, width)), mid, arrived

    projected, stream = attention_output(attended, vit_weights, "vit_output", stream)
    partials, mid, arrived = feed_forward(
        projected,
        stream,
        row(vit_norm2),
        vit_weights,
        layer_norm_rows,
        "vit_feed_forward",
        [(1, text_blocks[1]), (3, text_blocks[3])],
    )
    text_parts += arrived

    gain_rows = jnp.tile(merge_norm, (share // 4, 1))
    merged = call(merge_norm_body, shape(share, width), (partials, mid, gain_rows), name="merge_norm")
    gathered = gather_four("gq", merged)
    group_slots = group_rows // 4
    outs = shape(gx_count, group_slots, block_lanes)
    projected = call(
        merge_projection_body,
        outs,
        (place, *gathered, mid_weights),
        specs=[SMEM] + [whole(g) for g in gathered] + [block_spec(width, 384, 0)],
        grid=(SUB,),
        out_specs=fixed(outs),
        scratch=[
            pltpu.VMEM((group_rows, width), BF16),
            pltpu.VMEM((group_rows, width), BF16),
            pltpu.VMEM((SUB, group_slots, LANES), BF16),
        ],
        flops=2 * group_rows * width * SUB * LANES,
        name="merge_projection",
    )
    all_projected = exchange("gx", projected).reshape(gx_count * group_slots, block_lanes)

    own_index = own_gx * tokens + jnp.arange(tokens, dtype=jnp.int32)
    is_image = jnp.any(positions[None, :] == own_index[:, None], axis=1).astype(F32)
    by_slot = lax.dynamic_index_in_dim(
        positions.reshape(gx_count, SUB, group_slots), own_z, 1, keepdims=False
    )
    placed = call(
        place_body,
        shape(tokens, block_lanes),
        (
            own_index.reshape(tokens, 1),
            is_image.reshape(tokens, 1),
            by_slot.reshape(1, -1),
            all_projected,
            *text_parts,
        ),
        flops=2 * tokens * by_slot.size * block_width,
        name="place_rows",
    )
    own_rows = jnp.sum(
        exchange("gz", placed.reshape(SUB, part, block_lanes)).astype(F32), axis=0
    ).astype(BF16)
    gathered = gather_four("gq", own_rows)

    outs = [shape(SUB, part, 3 * LANES), shape(part, width)]
    triple, embedded = call(
        dec_qkv_body,
        outs,
        (place, *gathered, row(dec_norm1), mid_weights, mid_weights, mid_weights),
        specs=[SMEM]
        + [whole(a) for a in (*gathered, row(dec_norm1))]
        + [block_spec(width, LANES, at) for at in (2, 3, 4)],
        grid=(SUB,),
        out_specs=[pl.BlockSpec((1, part, 3 * LANES), lambda z: (z, 0, 0)), fixed(outs[1])],
        scratch=[pltpu.VMEM((SUB, part, block_lanes), BF16), pltpu.VMEM((part, width), BF16)],
        flops=2 * part * width * SUB * 3 * LANES,
        name="dec_qkv",
    )
    triple = exchange("gz", triple).reshape(tokens, 3 * LANES)
    key_values = triple[:, LANES:]
    near = jnp.stack(
        [key_values]
        + [
            lax.ppermute(
                key_values,
                "gx",
                [(2 * y + c, 2 * ((y + k) % SUB) + c) for y in range(SUB) for c in range(2)],
            )
            for k in range(1, SUB)
        ]
    )
    far = lax.ppermute(near, "gx", [(i, i ^ 1) for i in range(gx_count)])
    bounds = jnp.cumsum(lengths)
    all_index = jnp.arange(gx_count * tokens, dtype=jnp.int32).reshape(gx_count, tokens)
    request = jnp.sum((all_index[:, :, None] >= bounds).astype(jnp.int32), axis=2)
    own_request = jnp.sum((own_index[:, None] >= bounds).astype(jnp.int32), axis=1)
    tables = (place, triple, own_request.reshape(tokens, 1), own_index.reshape(tokens, 1), request)
    sums = [shape(tokens, LANES, dtype=F32), shape(tokens, 1, dtype=F32)]
    weighted, denominator = call(
        near_attention_body,
        sums,
        (*tables, near),
        specs=[SMEM] + [VMEM] * 5,
        flops=2 * tokens * tokens * gx_count * LANES,
        name="near_attention",
    )
    attended = call(
        far_attention_body,
        shape(SUB * SUB, part, LANES),
        (*tables, far, weighted, denominator),
        specs=[SMEM] + [VMEM] * 7,
        scratch=[pltpu.VMEM(sums[0].shape, F32), pltpu.VMEM(sums[1].shape, F32)],
        flops=2 * tokens * tokens * gx_count * LANES,
        name="far_attention",
    )
    projected, _ = attention_output(attended, dec_weights, "dec_output")
    partials, mid, _ = feed_forward(
        projected, embedded, row(dec_norm2), dec_weights, rms_norm_rows, "dec_feed_forward"
    )
    own_tokens = mid.shape[0]
    normed = call(
        dec_final_body, shape(own_tokens, width), (partials, mid, row(next_norm)), name="dec_final"
    )

    gathered = gather_four("gq", normed)
    triple = call(
        next_qkv_body,
        shape(part, 3 * block_lanes),
        (place, *gathered, dec_weights),
        specs=[SMEM] + [whole(g) for g in gathered] + [block_spec(width, 3 * LANES, 2)],
        grid=(SUB,),
        out_specs=pl.BlockSpec((part, 3 * block_lanes), lambda z: (0, 0)),
        scratch=[pltpu.VMEM((part, width), BF16), pltpu.VMEM((SUB, part, 3 * LANES), BF16)],
        flops=2 * part * width * SUB * 3 * LANES,
        name="next_qkv",
    )
    received = exchange("gq", triple.reshape(SUB, own_tokens, 3 * block_lanes))
    finished = call(finish_body, shape(3, own_tokens, width), (received,), name="finish")
    return finished.transpose(1, 0, 2)


def solution(mesh):
    gx_size = mesh.shape["gx"]
    cut = Mesh(mesh.devices.reshape(gx_size, SUB, SUB), ("gx", "gz", "gq"))
    gy = ("gz", "gq")
    flat = P("gx", gy)
    deep = P("gx", None, gy)
    placed = (
        P(("gx", *gy), None),
        P(),
        P("gx"),
        P(),
        P(),
        P(gy, None),
        P(),
        deep,
        flat,
        P(),
        flat,
        flat,
        P(),
        deep,
        P(),
        deep,
        flat,
        P(),
        flat,
        flat,
        P(),
        deep,
    )
    return jax.shard_map(
        per_device,
        mesh=cut,
        in_specs=placed,
        out_specs=P(("gx", *gy), None, None),
        check_vma=False,
    )
```

```python
import functools
import math

import jax
import jax.numpy as jnp
from jax import lax
from jax.experimental import pallas as pl
from jax.experimental.pallas import tpu as pltpu
from jax.sharding import Mesh, PartitionSpec as P

HEAD_DIM = 88
LANES = 128
SUB = 4
NORM_EPS = 1e-06
F32 = jnp.float32
BF16 = jnp.bfloat16
VMEM_LIMIT = 50 * 1024 * 1024


def merge_sources(grid_rows, merge_slots):
    image_count = grid_rows.shape[0]
    merged_count = grid_rows[:, 0] * grid_rows[:, 1]
    merged_end = jnp.cumsum(merged_count)
    merged_start = merged_end - merged_count
    slot_index = jnp.arange(merge_slots, dtype=jnp.int32)
    image_of = jnp.sum((slot_index[:, None] >= merged_end[None, :]).astype(jnp.int32), axis=1)
    is_live = image_of < image_count
    picked = (
        jnp.minimum(image_of, image_count - 1)[:, None]
        == jnp.arange(image_count, dtype=jnp.int32)[None, :]
    ).astype(jnp.int32)
    col_count = jnp.sum(picked * grid_rows[None, :, 1], axis=1)
    first_slot = jnp.sum(picked * merged_start[None, :], axis=1)
    local_slot = slot_index - first_slot
    grid_row = local_slot // col_count
    grid_col = local_slot % col_count
    base_row = 4 * first_slot + 4 * grid_row * col_count + 2 * grid_col
    offsets = jnp.stack(
        [jnp.zeros_like(col_count), jnp.ones_like(col_count), 2 * col_count, 2 * col_count + 1],
        axis=1,
    )
    sources = jnp.where(is_live[:, None], base_row[:, None] + offsets, 0)
    return sources, image_of, is_live


def shift_in(axis, values, step):
    return lax.ppermute(values, axis, [(i, (i + step) % SUB) for i in range(SUB)])


def gather_four(axis, values):
    return [values] + [shift_in(axis, values, k) for k in range(1, SUB)]


def exchange(axis, pieces):
    return lax.all_to_all(pieces, axis, 0, 0)


def collect(axis, values, size):
    return exchange(axis, jnp.broadcast_to(values, (size,) + values.shape))


SMEM = pl.BlockSpec(memory_space=pltpu.SMEM)
VMEM = pl.BlockSpec(memory_space=pltpu.VMEM)


def shape(*dims, dtype=BF16):
    return jax.ShapeDtypeStruct(dims, dtype)


def call(body, outs, args, specs=None, grid=None, out_specs=None, scratch=(), flops=0, name=None):
    if specs is None:
        specs = [VMEM] * len(args)
    if out_specs is None:
        out_specs = jax.tree.map(lambda _: VMEM, outs)
    moved = sum(math.prod(a.shape) * a.dtype.itemsize for a in args)
    kwargs = {} if grid is None else {"grid": grid}
    return pl.pallas_call(
        body,
        out_shape=outs,
        in_specs=specs,
        out_specs=out_specs,
        scratch_shapes=list(scratch),
        cost_estimate=pl.CostEstimate(
            flops=flops, bytes_accessed=moved if flops else 0, transcendentals=0
        ),
        compiler_params=pltpu.CompilerParams(vmem_limit_bytes=VMEM_LIMIT),
        name=name,
        **kwargs,
    )(*args)


def back(own, step):
    return lax.rem(own + (SUB - step), SUB)


def ahead(own, step):
    return lax.rem(own + step, SUB)


def dot(left, right):
    return jnp.dot(left, right, preferred_element_type=F32)


def layer_norm_rows(values, gain):
    centre = values - jnp.mean(values, axis=-1, keepdims=True)
    spread = jnp.mean(centre * centre, axis=-1, keepdims=True)
    return (centre * lax.rsqrt(spread + NORM_EPS) * gain).astype(BF16)


def rms_norm_rows(values, gain):
    square = jnp.mean(values * values, axis=-1, keepdims=True)
    return (values * lax.rsqrt(square + NORM_EPS) * gain).astype(BF16)


def gelu(values):
    return 0.5 * values * (1.0 + lax.erf(values * (2.0**-0.5)))


def pad_heads(values):
    empty = jnp.zeros((values.shape[0], LANES - HEAD_DIM), values.dtype)
    parts = []
    for t in range(3):
        parts += [values[:, t * HEAD_DIM : (t + 1) * HEAD_DIM], empty]
    return jnp.concatenate(parts, axis=1)


def vit_attention_body(r0, r1, r2, r3, weight, gain, source, query_class, key_class, out, triple, merged):
    slots = triple.shape[0]
    step = slots // SUB
    for i, rows in enumerate((r0, r1, r2, r3)):
        normed = layer_norm_rows(rows[...].astype(F32), gain[...])
        triple[i * step : (i + 1) * step, :] = pad_heads(dot(normed, weight[...]).astype(BF16))

    def reorder(i, _):
        part = pl.ds(pl.multiple_of(i * step, step), step)
        chosen = (
            source[part, :] == lax.broadcasted_iota(jnp.int32, (step, slots), 1)
        ).astype(BF16)
        merged[part, :] = dot(chosen, triple[...]).astype(BF16)
        return 0

    lax.fori_loop(0, SUB, reorder, 0)
    for i in range(SUB):
        at = i * step
        scores = lax.dot_general(
            merged[at : at + step, :LANES],
            merged[:, LANES : 2 * LANES],
            (((1,), (1,)), ((), ())),
            preferred_element_type=F32,
        ) * HEAD_DIM ** (-0.5)
        allowed = query_class[at : at + step, :] == key_class[...]
        exp_scores = jnp.where(allowed, jnp.exp(scores), 0.0)
        denominator = jnp.sum(exp_scores, axis=1, keepdims=True)
        weighted = dot(exp_scores.astype(BF16), merged[:, 2 * LANES :])
        result = (weighted / denominator).astype(BF16)
        for q in range(SUB):
            out[i * SUB + q] = result


def pick_rows_body(source, r0, r1, r2, r3, out):
    rows = r0.shape[0]
    total = None
    for i, ref in enumerate((r0, r1, r2, r3)):
        at = lax.broadcasted_iota(jnp.int32, (source.shape[0], rows), 1) + i * rows
        term = dot((source[...] == at).astype(BF16), ref[...])
        total = term if total is None else total + term
    out[...] = total.astype(BF16)


def join_heads(blocks):
    return jnp.concatenate([block[:, :HEAD_DIM] for block in blocks], axis=1)


def out_projection_body(heads, weight, out, left, done):
    step = pl.program_id(0)

    @pl.when(step == 0)
    def _():
        left[...] = join_heads([heads[h] for h in range(SUB * SUB)])

    done[step] = dot(left[...], weight[0]).astype(BF16)

    @pl.when(step == SUB - 1)
    def _():
        out[:, : SUB * HEAD_DIM] = join_heads([done[z] for z in range(SUB)])


def hold_blocks(refs, own_q, held):
    for k, ref in enumerate(refs):
        held[back(own_q, k)] = ref[...]


def in_order(held, rows=slice(None)):
    return jnp.concatenate(
        [
            held[q, rows, z * HEAD_DIM : (z + 1) * HEAD_DIM]
            for z in range(SUB)
            for q in range(SUB)
        ],
        axis=1,
    )


def feed_forward_body(norm, place, o0, o1, o2, o3, stream, gain, weight, out, mid_out, held, mid, normed, total):
    own_q = place[2]
    step = pl.program_id(0)
    rows = stream.shape[0]
    share = rows // SUB
    hidden_width = weight.shape[2] // 2

    @pl.when(step == 0)
    def _():
        hold_blocks((o0, o1, o2, o3), own_q, held)

        def prepare(i, _):
            part = pl.ds(pl.multiple_of(i * 2 * share, 2 * share), 2 * share)
            added = in_order(held, part).astype(F32)
            summed = (stream[part, :].astype(F32) + added).astype(BF16)
            mid[part, :] = summed
            normed[part, :] = norm(summed.astype(F32), gain[...])
            return 0

        lax.fori_loop(0, SUB // 2, prepare, 0)

    hidden = gelu(dot(normed[...], weight[0, :, :hidden_width])).astype(BF16)
    down = lax.dot_general(
        hidden,
        weight[0, :, hidden_width:],
        (((1,), (1,)), ((), ())),
        preferred_element_type=F32,
    )

    @pl.when(step == 0)
    def _():
        total[...] = down

    @pl.when((step > 0) & (step < SUB - 1))
    def _():
        total[...] += down

    @pl.when(step == SUB - 1)
    def _():
        out[...] = (total[...] + down).astype(BF16)
        mid_out[...] = mid[pl.ds(pl.multiple_of(own_q * share, share), share), :]


def summed_stream(partials, mid):
    summed = partials[0].astype(F32)
    for i in range(1, SUB):
        summed += partials[i].astype(F32)
    return (mid[...].astype(F32) + summed).astype(BF16).astype(F32)


def merge_norm_body(partials, mid, gain, out):
    rows, width = mid.shape
    final = summed_stream(partials, mid)
    row = lax.broadcasted_iota(jnp.int32, (rows, rows), 0)
    col = lax.broadcasted_iota(jnp.int32, (rows, rows), 1)
    same_group = row // 4 == col // 4

    def group_mean(column):
        across = jnp.sum(jnp.where(same_group, column, 0.0), axis=0, keepdims=True)
        down = jnp.sum(jnp.where(row == col, across, 0.0), axis=1, keepdims=True)
        return down / (4 * width)

    centre = final - group_mean(jnp.sum(final, axis=1, keepdims=True))
    spread = group_mean(jnp.sum(centre * centre, axis=1, keepdims=True))
    out[...] = (centre * lax.rsqrt(spread + NORM_EPS) * gain[...]).astype(BF16)


def merge_projection_body(place, g0, g1, g2, g3, weight, out, rows, left, done):
    own_q = place[2]
    step = pl.program_id(0)
    share = g0.shape[0]
    count = rows.shape[0]
    slots = count // 4

    @pl.when(step == 0)
    def _():
        for k, ref in enumerate((g0, g1, g2, g3)):
            rows[pl.ds(pl.multiple_of(back(own_q, k) * share, share), share), :] = ref[...]
        new_row = lax.broadcasted_iota(jnp.int32, (count, count), 0)
        old_row = lax.broadcasted_iota(jnp.int32, (count, count), 1)
        chosen = ((new_row % slots) * 4 + new_row // slots == old_row).astype(BF16)
        left[...] = dot(chosen, rows[...]).astype(BF16)

    total = dot(left[:slots, :], weight[0, :, :HEAD_DIM])
    for patch in range(1, 4):
        total += dot(
            left[patch * slots : (patch + 1) * slots, :],
            weight[0, :, patch * HEAD_DIM : (patch + 1) * HEAD_DIM],
        )
    done[step, :, :HEAD_DIM] = total.astype(BF16)

    @pl.when(step == SUB - 1)
    def _():
        projected = join_heads([done[z] for z in range(SUB)])
        for g in range(out.shape[0]):
            out[g, :, : SUB * HEAD_DIM] = projected


def text_rows_body(place, ids, table, *rest):
    outs, (total,) = rest[:SUB], rest[SUB:]
    own_q = place[2]
    step = pl.program_id(0)
    last = pl.num_programs(0) - 1
    count = table.shape[0]
    tokens = ids.shape[0]
    share = tokens // SUB
    first = (place[1] * SUB + own_q) * count * pl.num_programs(0) + step * count
    chosen = (ids[...] - first == lax.broadcasted_iota(jnp.int32, (tokens, count), 1)).astype(BF16)
    found = dot(chosen, table[...])

    @pl.when(step == 0)
    def _():
        total[...] = found

    @pl.when(step > 0)
    def _():
        total[...] += found

    @pl.when(step == last)
    def _():
        def hand_out(i, _):
            rows = pl.ds(pl.multiple_of(i * share, share), share)
            for q in range(SUB):
                blocks = [
                    total[rows, at : at + HEAD_DIM]
                    for at in range(q * HEAD_DIM, total.shape[1], SUB * HEAD_DIM)
                ]
                columns = jnp.concatenate(blocks, axis=1).astype(BF16)
                for k in range(SUB):

                    @pl.when(ahead(own_q, k) == q)
                    def _():
                        outs[k][rows, : SUB * HEAD_DIM] = columns

            return 0

        lax.fori_loop(0, SUB, hand_out, 0)


def place_body(seq, is_image, slot_position, projected, t0, t1, t2, t3, out):
    chosen = (seq[...] == slot_position[...]).astype(BF16)
    placed = dot(chosen, projected[...])
    text = t0[...].astype(F32) + t1[...].astype(F32) + t2[...].astype(F32) + t3[...].astype(F32)
    width = SUB * HEAD_DIM
    out[:, :width] = jnp.where(is_image[...] > 0, placed, text)[:, :width].astype(BF16)


def dec_qkv_body(place, g0, g1, g2, g3, gain, w0, w1, w2, out, embedded_out, held, normed):
    @pl.when(pl.program_id(0) == 0)
    def _():
        hold_blocks((g0, g1, g2, g3), place[2], held)
        embedded = in_order(held)
        embedded_out[...] = embedded
        normed[...] = rms_norm_rows(embedded.astype(F32), gain[...])

    result = jnp.concatenate([dot(normed[...], w[0]) for w in (w0, w1, w2)], axis=1)
    at = 4 * HEAD_DIM - 2 * LANES
    out[0] = pad_heads(result[:, at : at + 3 * HEAD_DIM].astype(BF16))


def attend_blocks(own_gx, core, triple, query_request, query_position, request, blocks, weighted, denominator):
    tokens = triple.shape[0]
    part = tokens // 2

    def attend(k, _):
        owner = 2 * lax.rem(lax.div(own_gx, 2) + (SUB - k), SUB) + core

        @pl.when(owner <= own_gx)
        def _():
            key_request = request[pl.ds(owner, 1), :]
            key_position = lax.broadcasted_iota(jnp.int32, (1, tokens), 1) + owner * tokens
            for at in range(0, tokens, part):
                rows = slice(at, at + part)
                scores = lax.dot_general(
                    triple[rows, :LANES],
                    blocks[k, :, :LANES],
                    (((1,), (1,)), ((), ())),
                    preferred_element_type=F32,
                ) * HEAD_DIM ** (-0.5)
                allowed = (key_request == query_request[rows, :]) & (
                    key_position <= query_position[rows, :]
                )
                exp_scores = jnp.where(allowed, jnp.exp(scores), 0.0)
                denominator[rows, :] += jnp.sum(exp_scores, axis=1, keepdims=True)
                weighted[rows, :] += dot(exp_scores.astype(BF16), blocks[k, :, LANES:])

        return 0

    lax.fori_loop(0, SUB, attend, 0)


def near_attention_body(place, triple, query_request, query_position, request, near, weighted, denominator):
    weighted[...] = jnp.zeros_like(weighted)
    denominator[...] = jnp.zeros_like(denominator)
    attend_blocks(
        place[0], lax.rem(place[0], 2), triple, query_request, query_position, request, near, weighted, denominator
    )


def far_attention_body(
    place, triple, query_request, query_position, request, far, near_weighted, near_denominator, out, weighted, denominator
):
    weighted[...] = near_weighted[...]
    denominator[...] = near_denominator[...]
    attend_blocks(
        place[0], lax.rem(place[0] + 1, 2), triple, query_request, query_position, request, far, weighted, denominator
    )
    share = triple.shape[0] // SUB
    for z in range(SUB):
        rows = slice(z * share, (z + 1) * share)
        result = (weighted[rows, :] / denominator[rows, :]).astype(BF16)
        for q in range(SUB):
            out[z * SUB + q] = result


def dec_final_body(partials, mid, gain, out):
    out[...] = rms_norm_rows(summed_stream(partials, mid), gain[...])


def next_qkv_body(place, g0, g1, g2, g3, weight, out, left, done):
    own_q = place[2]
    step = pl.program_id(0)
    share = g0.shape[0]

    @pl.when(step == 0)
    def _():
        for k, ref in enumerate((g0, g1, g2, g3)):
            left[pl.ds(pl.multiple_of(back(own_q, k) * share, share), share), :] = ref[...]

    done[step] = dot(left[...], weight[0]).astype(BF16)

    @pl.when(step == SUB - 1)
    def _():
        out[:, : 3 * SUB * HEAD_DIM] = jnp.concatenate(
            [done[z, :, HEAD_DIM : 4 * HEAD_DIM] for z in range(SUB)], axis=1
        )


def finish_body(received, out):
    for t in range(3):
        parts = []
        for z in range(SUB):
            at = (3 * z + t) * HEAD_DIM
            parts += [received[q, :, at : at + HEAD_DIM] for q in range(SUB)]
        out[t] = jnp.concatenate(parts, axis=1)


def block_spec(rows, width, at):
    return pl.BlockSpec((1, rows, width), lambda z: (z, 0, at))


def whole(values):
    rank = values.ndim
    return pl.BlockSpec(values.shape, lambda z: (0,) * rank)


def fixed(struct):
    rank = len(struct.shape)
    return pl.BlockSpec(struct.shape, lambda z: (0,) * rank)


def per_device(
    patches,
    grids,
    text_ids,
    positions,
    lengths,
    text_table,
    vit_norm1,
    vit_qkv,
    vit_out,
    vit_norm2,
    vit_fc1,
    vit_fc2,
    merge_norm,
    merge_proj,
    dec_norm1,
    dec_qkv,
    dec_out,
    dec_norm2,
    dec_fc1,
    dec_fc2,
    next_norm,
    next_qkv,
):
    gx_count = lax.axis_size("gx")
    own_gx, own_z, own_q = lax.axis_index("gx"), lax.axis_index("gz"), lax.axis_index("gq")
    place = jnp.stack([own_gx, own_z, own_q]).astype(jnp.int32)
    width = patches.shape[1]
    share = patches.shape[0]
    slots = share * SUB * SUB

    def join_weights(parts, lanes):
        columns = []
        for p in parts:
            columns += [p] if p.ndim == 2 else [p[:, t] for t in range(p.shape[1])]
        used = sum(c.shape[1] for c in columns)
        columns.append(jnp.zeros((columns[0].shape[0], lanes - used), BF16))
        return jnp.concatenate([c for c in columns if c.shape[1]], axis=1)

    def gather_weights(local):
        full = lax.all_gather(local, ("gz", "gx"), axis=0, tiled=True)
        return full.reshape(SUB, width, local.shape[1])

    vit_weights = gather_weights(join_weights([vit_fc1, vit_fc2, vit_out], 896))

    per_group = grids.shape[0] // gx_count
    own_grids = lax.dynamic_slice_in_dim(grids, own_gx * per_group, per_group, 0)
    merge_slots = positions.shape[0] // gx_count
    sources, image_of, is_live = merge_sources(own_grids, merge_slots)
    holder = sources // share
    block = lax.rem(own_q + SUB - lax.rem(holder, SUB), SUB) * SUB + lax.rem(
        own_z + SUB - holder // SUB, SUB
    )
    source_column = (block * share + lax.rem(sources, share)).reshape(slots, 1)
    query_class = jnp.repeat(jnp.where(is_live, image_of, 0), 4).reshape(slots, 1)
    key_class = jnp.repeat(image_of, 4).reshape(1, slots)

    of_column = jnp.stack(gather_four("gz", patches))
    mid_local = join_weights([merge_proj, dec_qkv], 640)
    dec_local = join_weights([dec_fc1, dec_fc2, dec_out, next_qkv], 1152)
    of_column, mid_local, dec_local, source_column, query_class, key_class, qkv_parts = (
        lax.optimization_barrier(
            (of_column, mid_local, dec_local, source_column, query_class, key_class, vit_qkv)
        )
    )
    patches_full = [
        rows.reshape(SUB * share, width) for rows in gather_four("gq", of_column)
    ]
    mid_weights = gather_weights(mid_local)
    dec_weights = gather_weights(dec_local)
    own_qkv = jnp.concatenate([qkv_parts[:, t] for t in range(3)], axis=1)
    qkv_weight = lax.all_gather(own_qkv, "gx", axis=0, tiled=True)

    row = lambda gain: gain.reshape(1, -1)
    group_rows = slots // SUB
    attended = call(
        vit_attention_body,
        shape(SUB * SUB, group_rows, LANES),
        (*patches_full, qkv_weight, row(vit_norm1), source_column, query_class, key_class),
        scratch=[
            pltpu.VMEM((slots, 3 * LANES), BF16),
            pltpu.VMEM((slots, 3 * LANES), BF16),
        ],
        flops=2 * slots * (width * 3 * LANES + slots * 5 * LANES),
        name="vit_attention",
    )
    attended, ids = lax.optimization_barrier((attended, text_ids))

    tokens = text_ids.shape[0]
    part = tokens // SUB
    block_width = SUB * HEAD_DIM
    block_lanes = 3 * LANES
    table_step = text_table.shape[0] // 5
    text_blocks = call(
        text_rows_body,
        [shape(tokens, block_lanes)] * SUB,
        (place, ids.reshape(tokens, 1), text_table),
        specs=[
            SMEM,
            pl.BlockSpec((tokens, 1), lambda i: (0, 0)),
            pl.BlockSpec((table_step, width), lambda i: (i, 0)),
        ],
        grid=(5,),
        out_specs=[pl.BlockSpec((tokens, block_lanes), lambda i: (0, 0))] * SUB,
        scratch=[pltpu.VMEM((tokens, width), F32)],
        flops=2 * tokens * text_table.shape[0] * width,
        name="text_rows",
    )
    own_sources = lax.dynamic_slice_in_dim(source_column, own_z * group_rows, group_rows, 0)
    stream = call(
        pick_rows_body,
        shape(group_rows, width),
        (own_sources, *patches_full),
        flops=2 * slots * group_rows * width,
        name="pick_rows",
    )

    def attention_output(attended, weights, name, beside=()):
        heads = exchange(("gz", "gq"), attended)
        heads, beside = lax.optimization_barrier((heads, beside))
        rows = heads.shape[1]
        return call(
            out_projection_body,
            shape(rows, block_lanes),
            (heads, weights),
            specs=[whole(heads), block_spec(width, LANES, 6)],
            grid=(SUB,),
            out_specs=pl.BlockSpec((rows, block_lanes), lambda z: (0, 0)),
            scratch=[pltpu.VMEM((rows, width), BF16), pltpu.VMEM((SUB, rows, LANES), BF16)],
            flops=2 * rows * width * SUB * LANES,
            name=name,
        ), beside

    def feed_forward(projected, stream, gain, weights, norm, name, beside=()):
        rows = stream.shape[0]
        own = rows // SUB
        gathered = gather_four("gq", projected)
        gathered, travel = lax.optimization_barrier((gathered, [value for _, value in beside]))
        arrived = [shift_in("gq", value, k) for (k, _), value in zip(beside, travel)]
        hidden_width = vit_fc1.shape[1]
        outs = [shape(rows, width), shape(own, width)]
        partial, mid = call(
            functools.partial(feed_forward_body, norm),
            outs,
            (place, *gathered, stream, gain, weights),
            specs=[SMEM]
            + [whole(g) for g in gathered]
            + [whole(stream), whole(gain), block_spec(width, 2 * hidden_width, 0)],
            grid=(SUB,),
            out_specs=[fixed(o) for o in outs],
            scratch=[
                pltpu.VMEM((SUB, rows, block_lanes), BF16),
                pltpu.VMEM((rows, width), BF16),
                pltpu.VMEM((rows, width), BF16),
                pltpu.VMEM((rows, width), F32),
            ],
            flops=4 * rows * width * SUB * hidden_width,
            name=name,
        )
        partial, arrived = lax.optimization_barrier((partial, arrived))
        return exchange("gq", partial.reshape(SUB, own, width)), mid, arrived

    projected, (stream, text_blocks) = attention_output(
        attended, vit_weights, "vit_output", (stream, text_blocks)
    )
    partials, mid, arrived = feed_forward(
        projected,
        stream,
        row(vit_norm2),
        vit_weights,
        layer_norm_rows,
        "vit_feed_forward",
        [(1, text_blocks[1]), (3, text_blocks[3])],
    )
    text_parts = [text_blocks[0], *arrived]

    gain_rows = jnp.tile(merge_norm, (share // 4, 1))
    merged = call(merge_norm_body, shape(share, width), (partials, mid, gain_rows), name="merge_norm")
    gathered = gather_four("gq", merged)
    group_slots = group_rows // 4
    outs = shape(gx_count, group_slots, block_lanes)
    projected = call(
        merge_projection_body,
        outs,
        (place, *gathered, mid_weights),
        specs=[SMEM] + [whole(g) for g in gathered] + [block_spec(width, 384, 0)],
        grid=(SUB,),
        out_specs=fixed(outs),
        scratch=[
            pltpu.VMEM((group_rows, width), BF16),
            pltpu.VMEM((group_rows, width), BF16),
            pltpu.VMEM((SUB, group_slots, LANES), BF16),
        ],
        flops=2 * group_rows * width * SUB * LANES,
        name="merge_projection",
    )
    projected, last_block = lax.optimization_barrier((projected, text_blocks[2]))
    text_parts.append(shift_in("gq", last_block, 2))
    all_projected = exchange("gx", projected).reshape(gx_count * group_slots, block_lanes)

    own_index = own_gx * tokens + jnp.arange(tokens, dtype=jnp.int32)
    is_image = jnp.any(positions[None, :] == own_index[:, None], axis=1).astype(F32)
    by_slot = lax.dynamic_index_in_dim(
        positions.reshape(gx_count, SUB, group_slots), own_z, 1, keepdims=False
    )
    placed = call(
        place_body,
        shape(tokens, block_lanes),
        (
            own_index.reshape(tokens, 1),
            is_image.reshape(tokens, 1),
            by_slot.reshape(1, -1),
            all_projected,
            *text_parts,
        ),
        flops=2 * tokens * by_slot.size * block_width,
        name="place_rows",
    )
    own_rows = jnp.sum(
        exchange("gz", placed.reshape(SUB, part, block_lanes)).astype(F32), axis=0
    ).astype(BF16)
    gathered = gather_four("gq", own_rows)

    outs = [shape(SUB, part, 3 * LANES), shape(part, width)]
    triple, embedded = call(
        dec_qkv_body,
        outs,
        (place, *gathered, row(dec_norm1), mid_weights, mid_weights, mid_weights),
        specs=[SMEM]
        + [whole(a) for a in (*gathered, row(dec_norm1))]
        + [block_spec(width, LANES, at) for at in (2, 3, 4)],
        grid=(SUB,),
        out_specs=[pl.BlockSpec((1, part, 3 * LANES), lambda z: (z, 0, 0)), fixed(outs[1])],
        scratch=[pltpu.VMEM((SUB, part, block_lanes), BF16), pltpu.VMEM((part, width), BF16)],
        flops=2 * part * width * SUB * 3 * LANES,
        name="dec_qkv",
    )
    triple = exchange("gz", triple).reshape(tokens, 3 * LANES)
    key_values = triple[:, LANES:]
    near = jnp.stack(
        [key_values]
        + [
            lax.ppermute(
                key_values,
                "gx",
                [(2 * y + c, 2 * ((y + k) % SUB) + c) for y in range(SUB) for c in range(2)],
            )
            for k in range(1, SUB)
        ]
    )
    far = lax.ppermute(near, "gx", [(i, i ^ 1) for i in range(gx_count)])
    bounds = jnp.cumsum(lengths)
    all_index = jnp.arange(gx_count * tokens, dtype=jnp.int32).reshape(gx_count, tokens)
    request = jnp.sum((all_index[:, :, None] >= bounds).astype(jnp.int32), axis=2)
    own_request = jnp.sum((own_index[:, None] >= bounds).astype(jnp.int32), axis=1)
    tables = (place, triple, own_request.reshape(tokens, 1), own_index.reshape(tokens, 1), request)
    sums = [shape(tokens, LANES, dtype=F32), shape(tokens, 1, dtype=F32)]
    weighted, denominator = call(
        near_attention_body,
        sums,
        (*tables, near),
        specs=[SMEM] + [VMEM] * 5,
        flops=2 * tokens * tokens * gx_count * LANES,
        name="near_attention",
    )
    attended = call(
        far_attention_body,
        shape(SUB * SUB, part, LANES),
        (*tables, far, weighted, denominator),
        specs=[SMEM] + [VMEM] * 7,
        scratch=[pltpu.VMEM(sums[0].shape, F32), pltpu.VMEM(sums[1].shape, F32)],
        flops=2 * tokens * tokens * gx_count * LANES,
        name="far_attention",
    )
    projected, _ = attention_output(attended, dec_weights, "dec_output")
    partials, mid, _ = feed_forward(
        projected, embedded, row(dec_norm2), dec_weights, rms_norm_rows, "dec_feed_forward"
    )
    own_tokens = mid.shape[0]
    normed = call(
        dec_final_body, shape(own_tokens, width), (partials, mid, row(next_norm)), name="dec_final"
    )

    gathered = gather_four("gq", normed)
    triple = call(
        next_qkv_body,
        shape(part, 3 * block_lanes),
        (place, *gathered, dec_weights),
        specs=[SMEM] + [whole(g) for g in gathered] + [block_spec(width, 3 * LANES, 2)],
        grid=(SUB,),
        out_specs=pl.BlockSpec((part, 3 * block_lanes), lambda z: (0, 0)),
        scratch=[pltpu.VMEM((part, width), BF16), pltpu.VMEM((SUB, part, 3 * LANES), BF16)],
        flops=2 * part * width * SUB * 3 * LANES,
        name="next_qkv",
    )
    received = exchange("gq", triple.reshape(SUB, own_tokens, 3 * block_lanes))
    finished = call(finish_body, shape(3, own_tokens, width), (received,), name="finish")
    return finished.transpose(1, 0, 2)


def solution(mesh):
    gx_size = mesh.shape["gx"]
    cut = Mesh(mesh.devices.reshape(gx_size, SUB, SUB), ("gx", "gz", "gq"))
    gy = ("gz", "gq")
    flat = P("gx", gy)
    deep = P("gx", None, gy)
    placed = (
        P(("gx", *gy), None),
        P(),
        P("gx"),
        P(),
        P(),
        P(gy, None),
        P(),
        deep,
        flat,
        P(),
        flat,
        flat,
        P(),
        deep,
        P(),
        deep,
        flat,
        P(),
        flat,
        flat,
        P(),
        deep,
    )
    return jax.shard_map(
        per_device,
        mesh=cut,
        in_specs=placed,
        out_specs=P(("gx", *gy), None, None),
        check_vma=False,
    )
```

```python
import functools
import math

import jax
import jax.numpy as jnp
from jax import lax
from jax.experimental import pallas as pl
from jax.experimental.pallas import tpu as pltpu
from jax.sharding import Mesh, PartitionSpec as P

HEAD_DIM = 88
LANES = 128
SUB = 4
NORM_EPS = 1e-06
F32 = jnp.float32
BF16 = jnp.bfloat16
VMEM_LIMIT = 50 * 1024 * 1024


def merge_sources(grid_rows, merge_slots):
    image_count = grid_rows.shape[0]
    merged_count = grid_rows[:, 0] * grid_rows[:, 1]
    merged_end = jnp.cumsum(merged_count)
    merged_start = merged_end - merged_count
    slot_index = jnp.arange(merge_slots, dtype=jnp.int32)
    image_of = jnp.sum((slot_index[:, None] >= merged_end[None, :]).astype(jnp.int32), axis=1)
    is_live = image_of < image_count
    picked = (
        jnp.minimum(image_of, image_count - 1)[:, None]
        == jnp.arange(image_count, dtype=jnp.int32)[None, :]
    ).astype(jnp.int32)
    col_count = jnp.sum(picked * grid_rows[None, :, 1], axis=1)
    first_slot = jnp.sum(picked * merged_start[None, :], axis=1)
    local_slot = slot_index - first_slot
    grid_row = local_slot // col_count
    grid_col = local_slot % col_count
    base_row = 4 * first_slot + 4 * grid_row * col_count + 2 * grid_col
    offsets = jnp.stack(
        [jnp.zeros_like(col_count), jnp.ones_like(col_count), 2 * col_count, 2 * col_count + 1],
        axis=1,
    )
    sources = jnp.where(is_live[:, None], base_row[:, None] + offsets, 0)
    return sources, image_of, is_live


def shift_in(axis, values, step):
    return lax.ppermute(values, axis, [(i, (i + step) % SUB) for i in range(SUB)])


def gather_four(axis, values):
    return [values] + [shift_in(axis, values, k) for k in range(1, SUB)]


def exchange(axis, pieces):
    return lax.all_to_all(pieces, axis, 0, 0)


def collect(axis, values, size):
    return exchange(axis, jnp.broadcast_to(values, (size,) + values.shape))


SMEM = pl.BlockSpec(memory_space=pltpu.SMEM)
VMEM = pl.BlockSpec(memory_space=pltpu.VMEM)


def shape(*dims, dtype=BF16):
    return jax.ShapeDtypeStruct(dims, dtype)


def call(body, outs, args, specs=None, grid=None, out_specs=None, scratch=(), flops=0, name=None):
    if specs is None:
        specs = [VMEM] * len(args)
    if out_specs is None:
        out_specs = jax.tree.map(lambda _: VMEM, outs)
    moved = sum(math.prod(a.shape) * a.dtype.itemsize for a in args)
    kwargs = {} if grid is None else {"grid": grid}
    return pl.pallas_call(
        body,
        out_shape=outs,
        in_specs=specs,
        out_specs=out_specs,
        scratch_shapes=list(scratch),
        cost_estimate=pl.CostEstimate(
            flops=flops, bytes_accessed=moved if flops else 0, transcendentals=0
        ),
        compiler_params=pltpu.CompilerParams(vmem_limit_bytes=VMEM_LIMIT),
        name=name,
        **kwargs,
    )(*args)


def back(own, step):
    return lax.rem(own + (SUB - step), SUB)


def ahead(own, step):
    return lax.rem(own + step, SUB)


def dot(left, right):
    return jnp.dot(left, right, preferred_element_type=F32)


def layer_norm_rows(values, gain):
    centre = values - jnp.mean(values, axis=-1, keepdims=True)
    spread = jnp.mean(centre * centre, axis=-1, keepdims=True)
    return (centre * lax.rsqrt(spread + NORM_EPS) * gain).astype(BF16)


def rms_norm_rows(values, gain):
    square = jnp.mean(values * values, axis=-1, keepdims=True)
    return (values * lax.rsqrt(square + NORM_EPS) * gain).astype(BF16)


def gelu(values):
    return 0.5 * values * (1.0 + lax.erf(values * (2.0**-0.5)))


def pad_heads(values):
    empty = jnp.zeros((values.shape[0], LANES - HEAD_DIM), values.dtype)
    parts = []
    for t in range(3):
        parts += [values[:, t * HEAD_DIM : (t + 1) * HEAD_DIM], empty]
    return jnp.concatenate(parts, axis=1)


def vit_attention_body(r0, r1, r2, r3, weight, gain, source, query_class, key_class, out, triple, merged):
    slots = triple.shape[0]
    step = slots // SUB
    for i, rows in enumerate((r0, r1, r2, r3)):
        normed = layer_norm_rows(rows[...].astype(F32), gain[...])
        triple[i * step : (i + 1) * step, :] = pad_heads(dot(normed, weight[...]).astype(BF16))

    def reorder(i, _):
        part = pl.ds(pl.multiple_of(i * step, step), step)
        chosen = (
            source[part, :] == lax.broadcasted_iota(jnp.int32, (step, slots), 1)
        ).astype(BF16)
        merged[part, :] = dot(chosen, triple[...]).astype(BF16)
        return 0

    lax.fori_loop(0, SUB, reorder, 0)
    for i in range(SUB):
        at = i * step
        scores = lax.dot_general(
            merged[at : at + step, :LANES],
            merged[:, LANES : 2 * LANES],
            (((1,), (1,)), ((), ())),
            preferred_element_type=F32,
        ) * HEAD_DIM ** (-0.5)
        allowed = query_class[at : at + step, :] == key_class[...]
        exp_scores = jnp.where(allowed, jnp.exp(scores), 0.0)
        denominator = jnp.sum(exp_scores, axis=1, keepdims=True)
        weighted = dot(exp_scores.astype(BF16), merged[:, 2 * LANES :])
        result = (weighted / denominator).astype(BF16)
        for q in range(SUB):
            out[i * SUB + q] = result


def pick_rows_body(source, r0, r1, r2, r3, out):
    rows = r0.shape[0]
    total = None
    for i, ref in enumerate((r0, r1, r2, r3)):
        at = lax.broadcasted_iota(jnp.int32, (source.shape[0], rows), 1) + i * rows
        term = dot((source[...] == at).astype(BF16), ref[...])
        total = term if total is None else total + term
    out[...] = total.astype(BF16)


def join_heads(blocks):
    return jnp.concatenate([block[:, :HEAD_DIM] for block in blocks], axis=1)


def out_projection_body(first, heads, weight, out, left, done):
    step = pl.program_id(0)

    @pl.when(step == 0)
    def _():
        left[...] = join_heads([heads[h] for h in range(SUB * SUB)])

    done[step, :, :HEAD_DIM] = dot(left[...], weight[0])[:, first : first + HEAD_DIM].astype(BF16)

    @pl.when(step == SUB - 1)
    def _():
        out[:, : SUB * HEAD_DIM] = join_heads([done[z] for z in range(SUB)])


def hold_blocks(refs, own_q, held):
    for k, ref in enumerate(refs):
        held[back(own_q, k)] = ref[...]


def in_order(held, rows=slice(None)):
    return jnp.concatenate(
        [
            held[q, rows, z * HEAD_DIM : (z + 1) * HEAD_DIM]
            for z in range(SUB)
            for q in range(SUB)
        ],
        axis=1,
    )


def feed_forward_body(norm, place, o0, o1, o2, o3, stream, gain, weight, out, mid_out, held, mid, normed, total):
    own_q = place[2]
    step = pl.program_id(0)
    rows = stream.shape[0]
    share = rows // SUB
    hidden_width = weight.shape[2] // 2

    @pl.when(step == 0)
    def _():
        hold_blocks((o0, o1, o2, o3), own_q, held)

        def prepare(i, _):
            part = pl.ds(pl.multiple_of(i * 2 * share, 2 * share), 2 * share)
            added = in_order(held, part).astype(F32)
            summed = (stream[part, :].astype(F32) + added).astype(BF16)
            mid[part, :] = summed
            normed[part, :] = norm(summed.astype(F32), gain[...])
            return 0

        lax.fori_loop(0, SUB // 2, prepare, 0)

    hidden = gelu(dot(normed[...], weight[0, :, :hidden_width])).astype(BF16)
    down = lax.dot_general(
        hidden,
        weight[0, :, hidden_width:],
        (((1,), (1,)), ((), ())),
        preferred_element_type=F32,
    )

    @pl.when(step == 0)
    def _():
        total[...] = down

    @pl.when((step > 0) & (step < SUB - 1))
    def _():
        total[...] += down

    @pl.when(step == SUB - 1)
    def _():
        out[...] = (total[...] + down).astype(BF16)
        mid_out[...] = mid[pl.ds(pl.multiple_of(own_q * share, share), share), :]


def summed_stream(partials, mid):
    summed = partials[0].astype(F32)
    for i in range(1, SUB):
        summed += partials[i].astype(F32)
    return (mid[...].astype(F32) + summed).astype(BF16).astype(F32)


def merge_norm_body(partials, mid, gain, out):
    rows, width = mid.shape
    final = summed_stream(partials, mid)
    row = lax.broadcasted_iota(jnp.int32, (rows, rows), 0)
    col = lax.broadcasted_iota(jnp.int32, (rows, rows), 1)
    same_group = row // 4 == col // 4

    def group_mean(column):
        across = jnp.sum(jnp.where(same_group, column, 0.0), axis=0, keepdims=True)
        down = jnp.sum(jnp.where(row == col, across, 0.0), axis=1, keepdims=True)
        return down / (4 * width)

    centre = final - group_mean(jnp.sum(final, axis=1, keepdims=True))
    spread = group_mean(jnp.sum(centre * centre, axis=1, keepdims=True))
    out[...] = (centre * lax.rsqrt(spread + NORM_EPS) * gain[...]).astype(BF16)


def merge_projection_body(place, g0, g1, g2, g3, w0, w1, out, rows, left, done):
    own_q = place[2]
    step = pl.program_id(0)
    share = g0.shape[0]
    count = rows.shape[0]
    slots = count // 4

    @pl.when(step == 0)
    def _():
        for k, ref in enumerate((g0, g1, g2, g3)):
            rows[pl.ds(pl.multiple_of(back(own_q, k) * share, share), share), :] = ref[...]
        new_row = lax.broadcasted_iota(jnp.int32, (count, count), 0)
        old_row = lax.broadcasted_iota(jnp.int32, (count, count), 1)
        chosen = ((new_row % slots) * 4 + new_row // slots == old_row).astype(BF16)
        left[...] = dot(chosen, rows[...]).astype(BF16)

    products = jnp.concatenate([dot(left[...], w0[0]), dot(left[...], w1[0])], axis=1)
    total = None
    for patch in range(4):
        at = (patch + 1) * HEAD_DIM
        term = products[patch * slots : (patch + 1) * slots, at : at + HEAD_DIM]
        total = term if total is None else total + term
    done[step, :, :HEAD_DIM] = total.astype(BF16)

    @pl.when(step == SUB - 1)
    def _():
        projected = join_heads([done[z] for z in range(SUB)])
        for g in range(out.shape[0]):
            out[g, :, : SUB * HEAD_DIM] = projected


def text_rows_body(place, ids, table, *rest):
    outs, (total,) = rest[:SUB], rest[SUB:]
    own_q = place[2]
    step = pl.program_id(0)
    last = pl.num_programs(0) - 1
    count = table.shape[0]
    tokens = ids.shape[0]
    share = tokens // SUB
    first = (place[1] * SUB + own_q) * count * pl.num_programs(0) + step * count
    chosen = (ids[...] - first == lax.broadcasted_iota(jnp.int32, (tokens, count), 1)).astype(BF16)
    found = dot(chosen, table[...])

    @pl.when(step == 0)
    def _():
        total[...] = found

    @pl.when(step > 0)
    def _():
        total[...] += found

    @pl.when(step == last)
    def _():
        def hand_out(i, _):
            rows = pl.ds(pl.multiple_of(i * share, share), share)
            for q in range(SUB):
                blocks = [
                    total[rows, at : at + HEAD_DIM]
                    for at in range(q * HEAD_DIM, total.shape[1], SUB * HEAD_DIM)
                ]
                columns = jnp.concatenate(blocks, axis=1).astype(BF16)
                for k in range(SUB):

                    @pl.when(ahead(own_q, k) == q)
                    def _():
                        outs[k][rows, : SUB * HEAD_DIM] = columns

            return 0

        lax.fori_loop(0, SUB, hand_out, 0)


def place_body(seq, is_image, slot_position, projected, t0, t1, t2, t3, out):
    chosen = (seq[...] == slot_position[...]).astype(BF16)
    placed = dot(chosen, projected[...])
    text = t0[...].astype(F32) + t1[...].astype(F32) + t2[...].astype(F32) + t3[...].astype(F32)
    width = SUB * HEAD_DIM
    out[:, :width] = jnp.where(is_image[...] > 0, placed, text)[:, :width].astype(BF16)


def dec_qkv_body(place, g0, g1, g2, g3, gain, weight, out, embedded_out, held, normed):
    @pl.when(pl.program_id(0) == 0)
    def _():
        hold_blocks((g0, g1, g2, g3), place[2], held)
        embedded = in_order(held)
        embedded_out[...] = embedded
        normed[...] = rms_norm_rows(embedded.astype(F32), gain[...])

    out[0] = pad_heads(dot(normed[...], weight[0])[:, : 3 * HEAD_DIM].astype(BF16))


def attend_blocks(own_gx, core, triple, query_request, query_position, request, blocks, weighted, denominator):
    tokens = triple.shape[0]
    part = tokens // 2

    def attend(k, _):
        owner = 2 * lax.rem(lax.div(own_gx, 2) + (SUB - k), SUB) + core

        @pl.when(owner <= own_gx)
        def _():
            key_request = request[pl.ds(owner, 1), :]
            key_position = lax.broadcasted_iota(jnp.int32, (1, tokens), 1) + owner * tokens
            for at in range(0, tokens, part):
                rows = slice(at, at + part)
                scores = lax.dot_general(
                    triple[rows, :LANES],
                    blocks[k, :, :LANES],
                    (((1,), (1,)), ((), ())),
                    preferred_element_type=F32,
                ) * HEAD_DIM ** (-0.5)
                allowed = (key_request == query_request[rows, :]) & (
                    key_position <= query_position[rows, :]
                )
                exp_scores = jnp.where(allowed, jnp.exp(scores), 0.0)
                denominator[rows, :] += jnp.sum(exp_scores, axis=1, keepdims=True)
                weighted[rows, :] += dot(exp_scores.astype(BF16), blocks[k, :, LANES:])

        return 0

    lax.fori_loop(0, SUB, attend, 0)


def near_attention_body(place, triple, query_request, query_position, request, near, weighted, denominator):
    weighted[...] = jnp.zeros_like(weighted)
    denominator[...] = jnp.zeros_like(denominator)
    attend_blocks(
        place[0], lax.rem(place[0], 2), triple, query_request, query_position, request, near, weighted, denominator
    )


def far_attention_body(
    place, triple, query_request, query_position, request, far, near_weighted, near_denominator, out, weighted, denominator
):
    weighted[...] = near_weighted[...]
    denominator[...] = near_denominator[...]
    attend_blocks(
        place[0], lax.rem(place[0] + 1, 2), triple, query_request, query_position, request, far, weighted, denominator
    )
    share = triple.shape[0] // SUB
    for z in range(SUB):
        rows = slice(z * share, (z + 1) * share)
        result = (weighted[rows, :] / denominator[rows, :]).astype(BF16)
        for q in range(SUB):
            out[z * SUB + q] = result


def dec_final_body(partials, mid, gain, out):
    out[...] = rms_norm_rows(summed_stream(partials, mid), gain[...])


def next_qkv_body(place, g0, g1, g2, g3, w0, w1, w2, out, left, done):
    own_q = place[2]
    step = pl.program_id(0)
    share = g0.shape[0]

    @pl.when(step == 0)
    def _():
        for k, ref in enumerate((g0, g1, g2, g3)):
            left[pl.ds(pl.multiple_of(back(own_q, k) * share, share), share), :] = ref[...]

    for i, weight in enumerate((w0, w1, w2)):
        done[step, :, i * LANES : (i + 1) * LANES] = dot(left[...], weight[0]).astype(BF16)

    @pl.when(step == SUB - 1)
    def _():
        out[:, : 3 * SUB * HEAD_DIM] = jnp.concatenate(
            [done[z, :, LANES - 32 : LANES - 32 + 3 * HEAD_DIM] for z in range(SUB)], axis=1
        )


def finish_body(received, out):
    for t in range(3):
        parts = []
        for z in range(SUB):
            at = (3 * z + t) * HEAD_DIM
            parts += [received[q, :, at : at + HEAD_DIM] for q in range(SUB)]
        out[t] = jnp.concatenate(parts, axis=1)


def block_spec(rows, width, at):
    return pl.BlockSpec((1, rows, width), lambda z: (z, 0, at))


def whole(values):
    rank = values.ndim
    return pl.BlockSpec(values.shape, lambda z: (0,) * rank)


def fixed(struct):
    rank = len(struct.shape)
    return pl.BlockSpec(struct.shape, lambda z: (0,) * rank)


def per_device(
    patches,
    grids,
    text_ids,
    positions,
    lengths,
    text_table,
    vit_norm1,
    vit_qkv,
    vit_out,
    vit_norm2,
    vit_fc1,
    vit_fc2,
    merge_norm,
    merge_proj,
    dec_norm1,
    dec_qkv,
    dec_out,
    dec_norm2,
    dec_fc1,
    dec_fc2,
    next_norm,
    next_qkv,
):
    gx_count = lax.axis_size("gx")
    own_gx, own_z, own_q = lax.axis_index("gx"), lax.axis_index("gz"), lax.axis_index("gq")
    place = jnp.stack([own_gx, own_z, own_q]).astype(jnp.int32)
    width = patches.shape[1]
    share = patches.shape[0]
    slots = share * SUB * SUB

    def join_weights(parts, lanes):
        columns = []
        for p in parts:
            columns += [p] if p.ndim == 2 else [p[:, t] for t in range(p.shape[1])]
        used = sum(c.shape[1] for c in columns)
        columns.append(jnp.zeros((columns[0].shape[0], lanes - used), BF16))
        return jnp.concatenate([c for c in columns if c.shape[1]], axis=1)

    def gather_weights(local):
        full = lax.all_gather(local, ("gz", "gx"), axis=0, tiled=True)
        return full.reshape(SUB, width, local.shape[1])

    vit_weights = gather_weights(join_weights([vit_fc1, vit_fc2, vit_out, merge_proj], 1280))

    per_group = grids.shape[0] // gx_count
    own_grids = lax.dynamic_slice_in_dim(grids, own_gx * per_group, per_group, 0)
    merge_slots = positions.shape[0] // gx_count
    sources, image_of, is_live = merge_sources(own_grids, merge_slots)
    holder = sources // share
    block = lax.rem(own_q + SUB - lax.rem(holder, SUB), SUB) * SUB + lax.rem(
        own_z + SUB - holder // SUB, SUB
    )
    source_column = (block * share + lax.rem(sources, share)).reshape(slots, 1)
    query_class = jnp.repeat(jnp.where(is_live, image_of, 0), 4).reshape(slots, 1)
    key_class = jnp.repeat(image_of, 4).reshape(1, slots)

    of_column = jnp.stack(gather_four("gz", patches))
    dec_local = join_weights([dec_fc1, dec_fc2, dec_qkv, dec_out, next_qkv], 1408)
    of_column, dec_local, source_column, query_class, key_class, qkv_parts = (
        lax.optimization_barrier(
            (of_column, dec_local, source_column, query_class, key_class, vit_qkv)
        )
    )
    patches_full = [
        rows.reshape(SUB * share, width) for rows in gather_four("gq", of_column)
    ]
    dec_weights = gather_weights(dec_local)
    own_qkv = jnp.concatenate([qkv_parts[:, t] for t in range(3)], axis=1)
    qkv_weight = lax.all_gather(own_qkv, "gx", axis=0, tiled=True)

    row = lambda gain: gain.reshape(1, -1)
    group_rows = slots // SUB
    attended = call(
        vit_attention_body,
        shape(SUB * SUB, group_rows, LANES),
        (*patches_full, qkv_weight, row(vit_norm1), source_column, query_class, key_class),
        scratch=[
            pltpu.VMEM((slots, 3 * LANES), BF16),
            pltpu.VMEM((slots, 3 * LANES), BF16),
        ],
        flops=2 * slots * (width * 3 * LANES + slots * 5 * LANES),
        name="vit_attention",
    )
    attended, ids = lax.optimization_barrier((attended, text_ids))

    tokens = text_ids.shape[0]
    part = tokens // SUB
    block_width = SUB * HEAD_DIM
    block_lanes = 3 * LANES
    table_step = text_table.shape[0] // 5
    text_blocks = call(
        text_rows_body,
        [shape(tokens, block_lanes)] * SUB,
        (place, ids.reshape(tokens, 1), text_table),
        specs=[
            SMEM,
            pl.BlockSpec((tokens, 1), lambda i: (0, 0)),
            pl.BlockSpec((table_step, width), lambda i: (i, 0)),
        ],
        grid=(5,),
        out_specs=[pl.BlockSpec((tokens, block_lanes), lambda i: (0, 0))] * SUB,
        scratch=[pltpu.VMEM((tokens, width), F32)],
        flops=2 * tokens * text_table.shape[0] * width,
        name="text_rows",
    )
    own_sources = lax.dynamic_slice_in_dim(source_column, own_z * group_rows, group_rows, 0)
    stream = call(
        pick_rows_body,
        shape(group_rows, width),
        (own_sources, *patches_full),
        flops=2 * slots * group_rows * width,
        name="pick_rows",
    )

    def attention_output(attended, weights, at, name, beside=()):
        heads = exchange(("gz", "gq"), attended)
        heads, beside = lax.optimization_barrier((heads, beside))
        rows = heads.shape[1]
        return call(
            functools.partial(out_projection_body, at % LANES),
            shape(rows, block_lanes),
            (heads, weights),
            specs=[whole(heads), block_spec(width, LANES, at // LANES)],
            grid=(SUB,),
            out_specs=pl.BlockSpec((rows, block_lanes), lambda z: (0, 0)),
            scratch=[pltpu.VMEM((rows, width), BF16), pltpu.VMEM((SUB, rows, LANES), BF16)],
            flops=2 * rows * width * SUB * LANES,
            name=name,
        ), beside

    def feed_forward(projected, stream, gain, weights, norm, name, beside=()):
        rows = stream.shape[0]
        own = rows // SUB
        gathered = gather_four("gq", projected)
        gathered, travel = lax.optimization_barrier((gathered, [value for _, value in beside]))
        arrived = [shift_in("gq", value, k) for (k, _), value in zip(beside, travel)]
        hidden_width = vit_fc1.shape[1]
        outs = [shape(rows, width), shape(own, width)]
        partial, mid = call(
            functools.partial(feed_forward_body, norm),
            outs,
            (place, *gathered, stream, gain, weights),
            specs=[SMEM]
            + [whole(g) for g in gathered]
            + [whole(stream), whole(gain), block_spec(width, 2 * hidden_width, 0)],
            grid=(SUB,),
            out_specs=[fixed(o) for o in outs],
            scratch=[
                pltpu.VMEM((SUB, rows, block_lanes), BF16),
                pltpu.VMEM((rows, width), BF16),
                pltpu.VMEM((rows, width), BF16),
                pltpu.VMEM((rows, width), F32),
            ],
            flops=4 * rows * width * SUB * hidden_width,
            name=name,
        )
        partial, arrived = lax.optimization_barrier((partial, arrived))
        return exchange("gq", partial.reshape(SUB, own, width)), mid, arrived

    projected, (stream, text_blocks) = attention_output(
        attended, vit_weights, 768, "vit_output", (stream, text_blocks)
    )
    partials, mid, arrived = feed_forward(
        projected,
        stream,
        row(vit_norm2),
        vit_weights,
        layer_norm_rows,
        "vit_feed_forward",
        [(1, text_blocks[1]), (3, text_blocks[3])],
    )
    text_parts = [text_blocks[0], *arrived]

    gain_rows = jnp.tile(merge_norm, (share // 4, 1))
    merged = call(merge_norm_body, shape(share, width), (partials, mid, gain_rows), name="merge_norm")
    gathered = gather_four("gq", merged)
    group_slots = group_rows // 4
    outs = shape(gx_count, group_slots, block_lanes)
    projected = call(
        merge_projection_body,
        outs,
        (place, *gathered, vit_weights, vit_weights),
        specs=[SMEM]
        + [whole(g) for g in gathered]
        + [block_spec(width, 2 * LANES, 3), block_spec(width, 2 * LANES, 4)],
        grid=(SUB,),
        out_specs=fixed(outs),
        scratch=[
            pltpu.VMEM((group_rows, width), BF16),
            pltpu.VMEM((group_rows, width), BF16),
            pltpu.VMEM((SUB, group_slots, LANES), BF16),
        ],
        flops=2 * group_rows * width * SUB * LANES,
        name="merge_projection",
    )
    projected, last_block = lax.optimization_barrier((projected, text_blocks[2]))
    text_parts.append(shift_in("gq", last_block, 2))
    all_projected = exchange("gx", projected).reshape(gx_count * group_slots, block_lanes)

    own_index = own_gx * tokens + jnp.arange(tokens, dtype=jnp.int32)
    is_image = jnp.any(positions[None, :] == own_index[:, None], axis=1).astype(F32)
    by_slot = lax.dynamic_index_in_dim(
        positions.reshape(gx_count, SUB, group_slots), own_z, 1, keepdims=False
    )
    placed = call(
        place_body,
        shape(tokens, block_lanes),
        (
            own_index.reshape(tokens, 1),
            is_image.reshape(tokens, 1),
            by_slot.reshape(1, -1),
            all_projected,
            *text_parts,
        ),
        flops=2 * tokens * by_slot.size * block_width,
        name="place_rows",
    )
    own_rows = jnp.sum(
        exchange("gz", placed.reshape(SUB, part, block_lanes)).astype(F32), axis=0
    ).astype(BF16)
    gathered = gather_four("gq", own_rows)

    outs = [shape(SUB, part, 3 * LANES), shape(part, width)]
    triple, embedded = call(
        dec_qkv_body,
        outs,
        (place, *gathered, row(dec_norm1), dec_weights),
        specs=[SMEM]
        + [whole(a) for a in (*gathered, row(dec_norm1))]
        + [block_spec(width, 3 * LANES, 2)],
        grid=(SUB,),
        out_specs=[pl.BlockSpec((1, part, 3 * LANES), lambda z: (z, 0, 0)), fixed(outs[1])],
        scratch=[pltpu.VMEM((SUB, part, block_lanes), BF16), pltpu.VMEM((part, width), BF16)],
        flops=2 * part * width * SUB * 3 * LANES,
        name="dec_qkv",
    )
    triple = exchange("gz", triple).reshape(tokens, 3 * LANES)
    key_values = triple[:, LANES:]
    near = jnp.stack(
        [key_values]
        + [
            lax.ppermute(
                key_values,
                "gx",
                [(2 * y + c, 2 * ((y + k) % SUB) + c) for y in range(SUB) for c in range(2)],
            )
            for k in range(1, SUB)
        ]
    )
    far = lax.ppermute(near, "gx", [(i, i ^ 1) for i in range(gx_count)])
    bounds = jnp.cumsum(lengths)
    all_index = jnp.arange(gx_count * tokens, dtype=jnp.int32).reshape(gx_count, tokens)
    request = jnp.sum((all_index[:, :, None] >= bounds).astype(jnp.int32), axis=2)
    own_request = jnp.sum((own_index[:, None] >= bounds).astype(jnp.int32), axis=1)
    tables = (place, triple, own_request.reshape(tokens, 1), own_index.reshape(tokens, 1), request)
    sums = [shape(tokens, LANES, dtype=F32), shape(tokens, 1, dtype=F32)]
    weighted, denominator = call(
        near_attention_body,
        sums,
        (*tables, near),
        specs=[SMEM] + [VMEM] * 5,
        flops=2 * tokens * tokens * gx_count * LANES,
        name="near_attention",
    )
    attended = call(
        far_attention_body,
        shape(SUB * SUB, part, LANES),
        (*tables, far, weighted, denominator),
        specs=[SMEM] + [VMEM] * 7,
        scratch=[pltpu.VMEM(sums[0].shape, F32), pltpu.VMEM(sums[1].shape, F32)],
        flops=2 * tokens * tokens * gx_count * LANES,
        name="far_attention",
    )
    projected, _ = attention_output(attended, dec_weights, 1032, "dec_output")
    partials, mid, _ = feed_forward(
        projected, embedded, row(dec_norm2), dec_weights, rms_norm_rows, "dec_feed_forward"
    )
    own_tokens = mid.shape[0]
    normed = call(
        dec_final_body, shape(own_tokens, width), (partials, mid, row(next_norm)), name="dec_final"
    )

    gathered = gather_four("gq", normed)
    triple = call(
        next_qkv_body,
        shape(part, 3 * block_lanes),
        (place, *gathered, dec_weights, dec_weights, dec_weights),
        specs=[SMEM]
        + [whole(g) for g in gathered]
        + [block_spec(width, LANES, at) for at in (8, 9, 10)],
        grid=(SUB,),
        out_specs=pl.BlockSpec((part, 3 * block_lanes), lambda z: (0, 0)),
        scratch=[pltpu.VMEM((part, width), BF16), pltpu.VMEM((SUB, part, 3 * LANES), BF16)],
        flops=2 * part * width * SUB * 3 * LANES,
        name="next_qkv",
    )
    received = exchange("gq", triple.reshape(SUB, own_tokens, 3 * block_lanes))
    finished = call(finish_body, shape(3, own_tokens, width), (received,), name="finish")
    return finished.transpose(1, 0, 2)


def solution(mesh):
    gx_size = mesh.shape["gx"]
    cut = Mesh(mesh.devices.reshape(gx_size, SUB, SUB), ("gx", "gz", "gq"))
    gy = ("gz", "gq")
    flat = P("gx", gy)
    deep = P("gx", None, gy)
    placed = (
        P(("gx", *gy), None),
        P(),
        P("gx"),
        P(),
        P(),
        P(gy, None),
        P(),
        deep,
        flat,
        P(),
        flat,
        flat,
        P(),
        deep,
        P(),
        deep,
        flat,
        P(),
        flat,
        flat,
        P(),
        deep,
    )
    return jax.shard_map(
        per_device,
        mesh=cut,
        in_specs=placed,
        out_specs=P(("gx", *gy), None, None),
        check_vma=False,
    )
```

```python
import functools
import math

import jax
import jax.numpy as jnp
from jax import lax
from jax.experimental import pallas as pl
from jax.experimental.pallas import tpu as pltpu
from jax.sharding import Mesh, PartitionSpec as P

HEAD_DIM = 88
LANES = 128
SUB = 4
NORM_EPS = 1e-06
F32 = jnp.float32
BF16 = jnp.bfloat16
VMEM_LIMIT = 50 * 1024 * 1024


def merge_sources(grid_rows, merge_slots):
    image_count = grid_rows.shape[0]
    merged_count = grid_rows[:, 0] * grid_rows[:, 1]
    merged_end = jnp.cumsum(merged_count)
    merged_start = merged_end - merged_count
    slot_index = jnp.arange(merge_slots, dtype=jnp.int32)
    image_of = jnp.sum((slot_index[:, None] >= merged_end[None, :]).astype(jnp.int32), axis=1)
    is_live = image_of < image_count
    picked = (
        jnp.minimum(image_of, image_count - 1)[:, None]
        == jnp.arange(image_count, dtype=jnp.int32)[None, :]
    ).astype(jnp.int32)
    col_count = jnp.sum(picked * grid_rows[None, :, 1], axis=1)
    first_slot = jnp.sum(picked * merged_start[None, :], axis=1)
    local_slot = slot_index - first_slot
    grid_row = local_slot // col_count
    grid_col = local_slot % col_count
    base_row = 4 * first_slot + 4 * grid_row * col_count + 2 * grid_col
    offsets = jnp.stack(
        [jnp.zeros_like(col_count), jnp.ones_like(col_count), 2 * col_count, 2 * col_count + 1],
        axis=1,
    )
    sources = jnp.where(is_live[:, None], base_row[:, None] + offsets, 0)
    return sources, image_of, is_live


def shift_in(axis, values, step):
    return lax.ppermute(values, axis, [(i, (i + step) % SUB) for i in range(SUB)])


def gather_four(axis, values):
    return [values] + [shift_in(axis, values, k) for k in range(1, SUB)]


def exchange(axis, pieces):
    return lax.all_to_all(pieces, axis, 0, 0)


def collect(axis, values, size):
    return exchange(axis, jnp.broadcast_to(values, (size,) + values.shape))


SMEM = pl.BlockSpec(memory_space=pltpu.SMEM)
VMEM = pl.BlockSpec(memory_space=pltpu.VMEM)


def shape(*dims, dtype=BF16):
    return jax.ShapeDtypeStruct(dims, dtype)


def call(body, outs, args, specs=None, grid=None, out_specs=None, scratch=(), flops=0, name=None):
    if specs is None:
        specs = [VMEM] * len(args)
    if out_specs is None:
        out_specs = jax.tree.map(lambda _: VMEM, outs)
    moved = sum(math.prod(a.shape) * a.dtype.itemsize for a in args)
    kwargs = {} if grid is None else {"grid": grid}
    return pl.pallas_call(
        body,
        out_shape=outs,
        in_specs=specs,
        out_specs=out_specs,
        scratch_shapes=list(scratch),
        cost_estimate=pl.CostEstimate(
            flops=flops, bytes_accessed=moved if flops else 0, transcendentals=0
        ),
        compiler_params=pltpu.CompilerParams(vmem_limit_bytes=VMEM_LIMIT),
        name=name,
        **kwargs,
    )(*args)


def back(own, step):
    return lax.rem(own + (SUB - step), SUB)


def ahead(own, step):
    return lax.rem(own + step, SUB)


def dot(left, right):
    return jnp.dot(left, right, preferred_element_type=F32)


def layer_norm_rows(values, gain):
    centre = values - jnp.mean(values, axis=-1, keepdims=True)
    spread = jnp.mean(centre * centre, axis=-1, keepdims=True)
    return (centre * lax.rsqrt(spread + NORM_EPS) * gain).astype(BF16)


def rms_norm_rows(values, gain):
    square = jnp.mean(values * values, axis=-1, keepdims=True)
    return (values * lax.rsqrt(square + NORM_EPS) * gain).astype(BF16)


def gelu(values):
    return 0.5 * values * (1.0 + lax.erf(values * (2.0**-0.5)))


def pad_heads(values):
    empty = jnp.zeros((values.shape[0], LANES - HEAD_DIM), values.dtype)
    parts = []
    for t in range(3):
        parts += [values[:, t * HEAD_DIM : (t + 1) * HEAD_DIM], empty]
    return jnp.concatenate(parts, axis=1)


def vit_attention_body(r0, r1, r2, r3, weight, gain, source, query_class, key_class, out, triple, merged):
    slots = triple.shape[0]
    step = slots // SUB
    for i, rows in enumerate((r0, r1, r2, r3)):
        normed = layer_norm_rows(rows[...].astype(F32), gain[...])
        triple[i * step : (i + 1) * step, :] = pad_heads(dot(normed, weight[...]).astype(BF16))

    def reorder(i, _):
        part = pl.ds(pl.multiple_of(i * step, step), step)
        chosen = (
            source[part, :] == lax.broadcasted_iota(jnp.int32, (step, slots), 1)
        ).astype(BF16)
        merged[part, :] = dot(chosen, triple[...]).astype(BF16)
        return 0

    lax.fori_loop(0, SUB, reorder, 0)
    for i in range(SUB):
        at = i * step
        scores = lax.dot_general(
            merged[at : at + step, :LANES],
            merged[:, LANES : 2 * LANES],
            (((1,), (1,)), ((), ())),
            preferred_element_type=F32,
        ) * HEAD_DIM ** (-0.5)
        allowed = query_class[at : at + step, :] == key_class[...]
        exp_scores = jnp.where(allowed, jnp.exp(scores), 0.0)
        denominator = jnp.sum(exp_scores, axis=1, keepdims=True)
        weighted = dot(exp_scores.astype(BF16), merged[:, 2 * LANES :])
        result = (weighted / denominator).astype(BF16)
        for q in range(SUB):
            out[i * SUB + q] = result


def pick_rows_body(source, r0, r1, r2, r3, out):
    rows = r0.shape[0]
    total = None
    for i, ref in enumerate((r0, r1, r2, r3)):
        at = lax.broadcasted_iota(jnp.int32, (source.shape[0], rows), 1) + i * rows
        term = dot((source[...] == at).astype(BF16), ref[...])
        total = term if total is None else total + term
    out[...] = total.astype(BF16)


def join_heads(blocks):
    return jnp.concatenate([block[:, :HEAD_DIM] for block in blocks], axis=1)


def out_projection_body(first, heads, weight, out, left, done):
    step = pl.program_id(0)

    @pl.when(step == 0)
    def _():
        left[...] = join_heads([heads[h] for h in range(SUB * SUB)])

    done[step, :, :HEAD_DIM] = dot(left[...], weight[0])[:, first : first + HEAD_DIM].astype(BF16)

    @pl.when(step == SUB - 1)
    def _():
        out[:, : SUB * HEAD_DIM] = join_heads([done[z] for z in range(SUB)])


def hold_blocks(refs, own_q, held):
    for k, ref in enumerate(refs):
        held[back(own_q, k)] = ref[...]


def in_order(held, rows=slice(None)):
    return jnp.concatenate(
        [
            held[q, rows, z * HEAD_DIM : (z + 1) * HEAD_DIM]
            for z in range(SUB)
            for q in range(SUB)
        ],
        axis=1,
    )


def feed_forward_body(norm, place, o0, o1, o2, o3, stream, gain, weight, out, mid_out, held, mid, normed, total):
    own_q = place[2]
    step = pl.program_id(0)
    rows = stream.shape[0]
    share = rows // SUB
    hidden_width = weight.shape[2] // 2

    @pl.when(step == 0)
    def _():
        hold_blocks((o0, o1, o2, o3), own_q, held)

        def prepare(i, _):
            part = pl.ds(pl.multiple_of(i * 2 * share, 2 * share), 2 * share)
            added = in_order(held, part).astype(F32)
            summed = (stream[part, :].astype(F32) + added).astype(BF16)
            mid[part, :] = summed
            normed[part, :] = norm(summed.astype(F32), gain[...])
            return 0

        lax.fori_loop(0, SUB // 2, prepare, 0)

    hidden = gelu(dot(normed[...], weight[0, :, :hidden_width])).astype(BF16)
    down = lax.dot_general(
        hidden,
        weight[0, :, hidden_width:],
        (((1,), (1,)), ((), ())),
        preferred_element_type=F32,
    )

    @pl.when(step == 0)
    def _():
        total[...] = down

    @pl.when((step > 0) & (step < SUB - 1))
    def _():
        total[...] += down

    @pl.when(step == SUB - 1)
    def _():
        out[...] = (total[...] + down).astype(BF16)
        mid_out[...] = mid[pl.ds(pl.multiple_of(own_q * share, share), share), :]


def summed_stream(partials, mid):
    summed = partials[0].astype(F32)
    for i in range(1, SUB):
        summed += partials[i].astype(F32)
    return (mid[...].astype(F32) + summed).astype(BF16).astype(F32)


def merge_norm_body(partials, mid, gain, out):
    rows, width = mid.shape
    final = summed_stream(partials, mid)
    row = lax.broadcasted_iota(jnp.int32, (rows, rows), 0)
    col = lax.broadcasted_iota(jnp.int32, (rows, rows), 1)
    same_group = row // 4 == col // 4

    def group_mean(column):
        across = jnp.sum(jnp.where(same_group, column, 0.0), axis=0, keepdims=True)
        down = jnp.sum(jnp.where(row == col, across, 0.0), axis=1, keepdims=True)
        return down / (4 * width)

    centre = final - group_mean(jnp.sum(final, axis=1, keepdims=True))
    spread = group_mean(jnp.sum(centre * centre, axis=1, keepdims=True))
    out[...] = (centre * lax.rsqrt(spread + NORM_EPS) * gain[...]).astype(BF16)


def merge_projection_body(place, g0, g1, g2, g3, w0, w1, out, rows, left, done):
    own_q = place[2]
    step = pl.program_id(0)
    share = g0.shape[0]
    count = rows.shape[0]
    slots = count // 4

    @pl.when(step == 0)
    def _():
        for k, ref in enumerate((g0, g1, g2, g3)):
            rows[pl.ds(pl.multiple_of(back(own_q, k) * share, share), share), :] = ref[...]
        new_row = lax.broadcasted_iota(jnp.int32, (count, count), 0)
        old_row = lax.broadcasted_iota(jnp.int32, (count, count), 1)
        chosen = ((new_row % slots) * 4 + new_row // slots == old_row).astype(BF16)
        left[...] = dot(chosen, rows[...]).astype(BF16)

    products = jnp.concatenate([dot(left[...], w0[0]), dot(left[...], w1[0])], axis=1)
    total = None
    for patch in range(4):
        at = (patch + 1) * HEAD_DIM
        term = products[patch * slots : (patch + 1) * slots, at : at + HEAD_DIM]
        total = term if total is None else total + term
    done[step, :, :HEAD_DIM] = total.astype(BF16)

    @pl.when(step == SUB - 1)
    def _():
        projected = join_heads([done[z] for z in range(SUB)])
        for g in range(out.shape[0]):
            out[g, :, : SUB * HEAD_DIM] = projected


def text_rows_body(place, ids, table, *rest):
    outs, (total,) = rest[:SUB], rest[SUB:]
    own_q = place[2]
    step = pl.program_id(0)
    last = pl.num_programs(0) - 1
    count = table.shape[0]
    tokens = ids.shape[0]
    share = tokens // SUB
    first = (place[1] * SUB + own_q) * count * pl.num_programs(0) + step * count
    chosen = (ids[...] - first == lax.broadcasted_iota(jnp.int32, (tokens, count), 1)).astype(BF16)
    found = dot(chosen, table[...])

    @pl.when(step == 0)
    def _():
        total[...] = found

    @pl.when(step > 0)
    def _():
        total[...] += found

    @pl.when(step == last)
    def _():
        def hand_out(i, _):
            rows = pl.ds(pl.multiple_of(i * share, share), share)
            for q in range(SUB):
                blocks = [
                    total[rows, at : at + HEAD_DIM]
                    for at in range(q * HEAD_DIM, total.shape[1], SUB * HEAD_DIM)
                ]
                columns = jnp.concatenate(blocks, axis=1).astype(BF16)
                for k in range(SUB):

                    @pl.when(ahead(own_q, k) == q)
                    def _():
                        outs[k][rows, : SUB * HEAD_DIM] = columns

            return 0

        lax.fori_loop(0, SUB, hand_out, 0)


def place_body(seq, is_image, slot_position, projected, t0, t1, t2, t3, out):
    chosen = (seq[...] == slot_position[...]).astype(BF16)
    placed = dot(chosen, projected[...])
    text = t0[...].astype(F32) + t1[...].astype(F32) + t2[...].astype(F32) + t3[...].astype(F32)
    width = SUB * HEAD_DIM
    out[:, :width] = jnp.where(is_image[...] > 0, placed, text)[:, :width].astype(BF16)


def dec_qkv_body(place, g0, g1, g2, g3, gain, weight, out, embedded_out, held, normed):
    @pl.when(pl.program_id(0) == 0)
    def _():
        hold_blocks((g0, g1, g2, g3), place[2], held)
        embedded = in_order(held)
        embedded_out[...] = embedded
        normed[...] = rms_norm_rows(embedded.astype(F32), gain[...])

    out[0] = pad_heads(dot(normed[...], weight[0])[:, : 3 * HEAD_DIM].astype(BF16))


def attend_blocks(own_gx, core, triple, query_request, query_position, request, blocks, weighted, denominator):
    tokens = triple.shape[0]
    part = tokens // 2

    def attend(k, _):
        owner = 2 * lax.rem(lax.div(own_gx, 2) + (SUB - k), SUB) + core

        @pl.when(owner <= own_gx)
        def _():
            key_request = request[pl.ds(owner, 1), :]
            key_position = lax.broadcasted_iota(jnp.int32, (1, tokens), 1) + owner * tokens
            for at in range(0, tokens, part):
                rows = slice(at, at + part)
                scores = lax.dot_general(
                    triple[rows, :LANES],
                    blocks[k, :, :LANES],
                    (((1,), (1,)), ((), ())),
                    preferred_element_type=F32,
                ) * HEAD_DIM ** (-0.5)
                allowed = (key_request == query_request[rows, :]) & (
                    key_position <= query_position[rows, :]
                )
                exp_scores = jnp.where(allowed, jnp.exp(scores), 0.0)
                denominator[rows, :] += jnp.sum(exp_scores, axis=1, keepdims=True)
                weighted[rows, :] += dot(exp_scores.astype(BF16), blocks[k, :, LANES:])

        return 0

    lax.fori_loop(0, SUB, attend, 0)


def near_attention_body(place, triple, query_request, query_position, request, near, weighted, denominator):
    weighted[...] = jnp.zeros_like(weighted)
    denominator[...] = jnp.zeros_like(denominator)
    attend_blocks(
        place[0], lax.rem(place[0], 2), triple, query_request, query_position, request, near, weighted, denominator
    )


def far_attention_body(
    place, triple, query_request, query_position, request, far, near_weighted, near_denominator, out, weighted, denominator
):
    weighted[...] = near_weighted[...]
    denominator[...] = near_denominator[...]
    attend_blocks(
        place[0], lax.rem(place[0] + 1, 2), triple, query_request, query_position, request, far, weighted, denominator
    )
    share = triple.shape[0] // SUB
    for z in range(SUB):
        rows = slice(z * share, (z + 1) * share)
        result = (weighted[rows, :] / denominator[rows, :]).astype(BF16)
        for q in range(SUB):
            out[z * SUB + q] = result


def finish_body(partials, mid, gain, weight, out, normed, done):
    step = pl.program_id(0)
    count = weight.shape[0]

    @pl.when(step == 0)
    def _():
        normed[...] = rms_norm_rows(summed_stream(partials, mid), gain[...])

    for i in range(count):
        done[step * count + i] = dot(normed[...], weight[i]).astype(BF16)

    @pl.when(step == pl.num_programs(0) - 1)
    def _():
        for t in range(3):
            out[t] = jnp.concatenate(
                [
                    done[h, :, t * HEAD_DIM : (t + 1) * HEAD_DIM]
                    for h in range(done.shape[0])
                ],
                axis=1,
            )


def block_spec(rows, width, at):
    return pl.BlockSpec((1, rows, width), lambda z: (z, 0, at))


def whole(values):
    rank = values.ndim
    return pl.BlockSpec(values.shape, lambda z: (0,) * rank)


def fixed(struct):
    rank = len(struct.shape)
    return pl.BlockSpec(struct.shape, lambda z: (0,) * rank)


def per_device(
    patches,
    grids,
    text_ids,
    positions,
    lengths,
    text_table,
    vit_norm1,
    vit_qkv,
    vit_out,
    vit_norm2,
    vit_fc1,
    vit_fc2,
    merge_norm,
    merge_proj,
    dec_norm1,
    dec_qkv,
    dec_out,
    dec_norm2,
    dec_fc1,
    dec_fc2,
    next_norm,
    next_qkv,
):
    gx_count = lax.axis_size("gx")
    own_gx, own_z, own_q = lax.axis_index("gx"), lax.axis_index("gz"), lax.axis_index("gq")
    place = jnp.stack([own_gx, own_z, own_q]).astype(jnp.int32)
    width = patches.shape[1]
    share = patches.shape[0]
    slots = share * SUB * SUB

    def join_weights(parts, lanes):
        columns = []
        for p in parts:
            columns += [p] if p.ndim == 2 else [p[:, t] for t in range(p.shape[1])]
        used = sum(c.shape[1] for c in columns)
        columns.append(jnp.zeros((columns[0].shape[0], lanes - used), BF16))
        return jnp.concatenate([c for c in columns if c.shape[1]], axis=1)

    def gather_weights(local):
        full = lax.all_gather(local, ("gz", "gx"), axis=0, tiled=True)
        return full.reshape(SUB, width, local.shape[1])

    vit_weights = gather_weights(join_weights([vit_fc1, vit_fc2, vit_out, merge_proj], 1280))

    per_group = grids.shape[0] // gx_count
    own_grids = lax.dynamic_slice_in_dim(grids, own_gx * per_group, per_group, 0)
    merge_slots = positions.shape[0] // gx_count
    sources, image_of, is_live = merge_sources(own_grids, merge_slots)
    holder = sources // share
    block = lax.rem(own_q + SUB - lax.rem(holder, SUB), SUB) * SUB + lax.rem(
        own_z + SUB - holder // SUB, SUB
    )
    source_column = (block * share + lax.rem(sources, share)).reshape(slots, 1)
    query_class = jnp.repeat(jnp.where(is_live, image_of, 0), 4).reshape(slots, 1)
    key_class = jnp.repeat(image_of, 4).reshape(1, slots)

    of_column = jnp.stack(gather_four("gz", patches))
    dec_local = join_weights([dec_fc1, dec_fc2, dec_qkv, dec_out], 1152)
    next_local = join_weights([next_qkv], 3 * HEAD_DIM)
    of_column, dec_local, next_local, source_column, query_class, key_class, qkv_parts = (
        lax.optimization_barrier(
            (of_column, dec_local, next_local, source_column, query_class, key_class, vit_qkv)
        )
    )
    patches_full = [
        rows.reshape(SUB * share, width) for rows in gather_four("gq", of_column)
    ]
    dec_weights = gather_weights(dec_local)
    own_qkv = jnp.concatenate([qkv_parts[:, t] for t in range(3)], axis=1)
    qkv_weight = lax.all_gather(own_qkv, "gx", axis=0, tiled=True)

    row = lambda gain: gain.reshape(1, -1)
    group_rows = slots // SUB
    attended = call(
        vit_attention_body,
        shape(SUB * SUB, group_rows, LANES),
        (*patches_full, qkv_weight, row(vit_norm1), source_column, query_class, key_class),
        scratch=[
            pltpu.VMEM((slots, 3 * LANES), BF16),
            pltpu.VMEM((slots, 3 * LANES), BF16),
        ],
        flops=2 * slots * (width * 3 * LANES + slots * 5 * LANES),
        name="vit_attention",
    )
    attended, ids, next_local = lax.optimization_barrier((attended, text_ids, next_local))
    next_weights = lax.all_gather(next_local, ("gz", "gq", "gx"), axis=0, tiled=True).reshape(
        SUB * SUB, width, 3 * HEAD_DIM
    )

    tokens = text_ids.shape[0]
    part = tokens // SUB
    block_width = SUB * HEAD_DIM
    block_lanes = 3 * LANES
    table_step = text_table.shape[0] // 5
    text_blocks = call(
        text_rows_body,
        [shape(tokens, block_lanes)] * SUB,
        (place, ids.reshape(tokens, 1), text_table),
        specs=[
            SMEM,
            pl.BlockSpec((tokens, 1), lambda i: (0, 0)),
            pl.BlockSpec((table_step, width), lambda i: (i, 0)),
        ],
        grid=(5,),
        out_specs=[pl.BlockSpec((tokens, block_lanes), lambda i: (0, 0))] * SUB,
        scratch=[pltpu.VMEM((tokens, width), F32)],
        flops=2 * tokens * text_table.shape[0] * width,
        name="text_rows",
    )
    own_sources = lax.dynamic_slice_in_dim(source_column, own_z * group_rows, group_rows, 0)
    stream = call(
        pick_rows_body,
        shape(group_rows, width),
        (own_sources, *patches_full),
        flops=2 * slots * group_rows * width,
        name="pick_rows",
    )

    def attention_output(attended, weights, at, name, beside=()):
        heads = exchange(("gz", "gq"), attended)
        heads, beside = lax.optimization_barrier((heads, beside))
        rows = heads.shape[1]
        return call(
            functools.partial(out_projection_body, at % LANES),
            shape(rows, block_lanes),
            (heads, weights),
            specs=[whole(heads), block_spec(width, LANES, at // LANES)],
            grid=(SUB,),
            out_specs=pl.BlockSpec((rows, block_lanes), lambda z: (0, 0)),
            scratch=[pltpu.VMEM((rows, width), BF16), pltpu.VMEM((SUB, rows, LANES), BF16)],
            flops=2 * rows * width * SUB * LANES,
            name=name,
        ), beside

    def feed_forward(projected, stream, gain, weights, norm, name, beside=()):
        rows = stream.shape[0]
        own = rows // SUB
        gathered = gather_four("gq", projected)
        gathered, travel = lax.optimization_barrier((gathered, [value for _, value in beside]))
        arrived = [shift_in("gq", value, k) for (k, _), value in zip(beside, travel)]
        hidden_width = vit_fc1.shape[1]
        outs = [shape(rows, width), shape(own, width)]
        partial, mid = call(
            functools.partial(feed_forward_body, norm),
            outs,
            (place, *gathered, stream, gain, weights),
            specs=[SMEM]
            + [whole(g) for g in gathered]
            + [whole(stream), whole(gain), block_spec(width, 2 * hidden_width, 0)],
            grid=(SUB,),
            out_specs=[fixed(o) for o in outs],
            scratch=[
                pltpu.VMEM((SUB, rows, block_lanes), BF16),
                pltpu.VMEM((rows, width), BF16),
                pltpu.VMEM((rows, width), BF16),
                pltpu.VMEM((rows, width), F32),
            ],
            flops=4 * rows * width * SUB * hidden_width,
            name=name,
        )
        partial, arrived = lax.optimization_barrier((partial, arrived))
        return exchange("gq", partial.reshape(SUB, own, width)), mid, arrived

    projected, (stream, text_blocks) = attention_output(
        attended, vit_weights, 768, "vit_output", (stream, text_blocks)
    )
    partials, mid, arrived = feed_forward(
        projected,
        stream,
        row(vit_norm2),
        vit_weights,
        layer_norm_rows,
        "vit_feed_forward",
        [(1, text_blocks[1]), (3, text_blocks[3])],
    )
    text_parts = [text_blocks[0], *arrived]

    gain_rows = jnp.tile(merge_norm, (share // 4, 1))
    merged = call(merge_norm_body, shape(share, width), (partials, mid, gain_rows), name="merge_norm")
    gathered = gather_four("gq", merged)
    gathered, last_block = lax.optimization_barrier((gathered, text_blocks[2]))
    text_parts.append(shift_in("gq", last_block, 2))
    group_slots = group_rows // 4
    outs = shape(gx_count, group_slots, block_lanes)
    projected = call(
        merge_projection_body,
        outs,
        (place, *gathered, vit_weights, vit_weights),
        specs=[SMEM]
        + [whole(g) for g in gathered]
        + [block_spec(width, 2 * LANES, 3), block_spec(width, 2 * LANES, 4)],
        grid=(SUB,),
        out_specs=fixed(outs),
        scratch=[
            pltpu.VMEM((group_rows, width), BF16),
            pltpu.VMEM((group_rows, width), BF16),
            pltpu.VMEM((SUB, group_slots, LANES), BF16),
        ],
        flops=2 * group_rows * width * SUB * LANES,
        name="merge_projection",
    )
    all_projected = exchange("gx", projected).reshape(gx_count * group_slots, block_lanes)

    own_index = own_gx * tokens + jnp.arange(tokens, dtype=jnp.int32)
    is_image = jnp.any(positions[None, :] == own_index[:, None], axis=1).astype(F32)
    by_slot = lax.dynamic_index_in_dim(
        positions.reshape(gx_count, SUB, group_slots), own_z, 1, keepdims=False
    )
    placed = call(
        place_body,
        shape(tokens, block_lanes),
        (
            own_index.reshape(tokens, 1),
            is_image.reshape(tokens, 1),
            by_slot.reshape(1, -1),
            all_projected,
            *text_parts,
        ),
        flops=2 * tokens * by_slot.size * block_width,
        name="place_rows",
    )
    own_rows = jnp.sum(
        exchange("gz", placed.reshape(SUB, part, block_lanes)).astype(F32), axis=0
    ).astype(BF16)
    gathered = gather_four("gq", own_rows)

    outs = [shape(SUB, part, 3 * LANES), shape(part, width)]
    triple, embedded = call(
        dec_qkv_body,
        outs,
        (place, *gathered, row(dec_norm1), dec_weights),
        specs=[SMEM]
        + [whole(a) for a in (*gathered, row(dec_norm1))]
        + [block_spec(width, 3 * LANES, 2)],
        grid=(SUB,),
        out_specs=[pl.BlockSpec((1, part, 3 * LANES), lambda z: (z, 0, 0)), fixed(outs[1])],
        scratch=[pltpu.VMEM((SUB, part, block_lanes), BF16), pltpu.VMEM((part, width), BF16)],
        flops=2 * part * width * SUB * 3 * LANES,
        name="dec_qkv",
    )
    triple = exchange("gz", triple).reshape(tokens, 3 * LANES)
    key_values = triple[:, LANES:]
    near = jnp.stack(
        [key_values]
        + [
            lax.ppermute(
                key_values,
                "gx",
                [(2 * y + c, 2 * ((y + k) % SUB) + c) for y in range(SUB) for c in range(2)],
            )
            for k in range(1, SUB)
        ]
    )
    far = lax.ppermute(near, "gx", [(i, i ^ 1) for i in range(gx_count)])
    bounds = jnp.cumsum(lengths)
    all_index = jnp.arange(gx_count * tokens, dtype=jnp.int32).reshape(gx_count, tokens)
    request = jnp.sum((all_index[:, :, None] >= bounds).astype(jnp.int32), axis=2)
    own_request = jnp.sum((own_index[:, None] >= bounds).astype(jnp.int32), axis=1)
    tables = (place, triple, own_request.reshape(tokens, 1), own_index.reshape(tokens, 1), request)
    sums = [shape(tokens, LANES, dtype=F32), shape(tokens, 1, dtype=F32)]
    weighted, denominator = call(
        near_attention_body,
        sums,
        (*tables, near),
        specs=[SMEM] + [VMEM] * 5,
        flops=2 * tokens * tokens * gx_count * LANES,
        name="near_attention",
    )
    attended = call(
        far_attention_body,
        shape(SUB * SUB, part, LANES),
        (*tables, far, weighted, denominator),
        specs=[SMEM] + [VMEM] * 7,
        scratch=[pltpu.VMEM(sums[0].shape, F32), pltpu.VMEM(sums[1].shape, F32)],
        flops=2 * tokens * tokens * gx_count * LANES,
        name="far_attention",
    )
    projected, _ = attention_output(attended, dec_weights, 1032, "dec_output")
    partials, mid, _ = feed_forward(
        projected, embedded, row(dec_norm2), dec_weights, rms_norm_rows, "dec_feed_forward"
    )
    own_tokens = mid.shape[0]

    at_once = 2
    finished = call(
        finish_body,
        shape(3, own_tokens, width),
        (partials, mid, row(next_norm), next_weights),
        specs=[whole(partials), whole(mid), pl.BlockSpec((1, width), lambda z: (0, 0))]
        + [pl.BlockSpec((at_once, width, 3 * HEAD_DIM), lambda z: (z, 0, 0))],
        grid=(SUB * SUB // at_once,),
        out_specs=pl.BlockSpec((3, own_tokens, width), lambda z: (0, 0, 0)),
        scratch=[
            pltpu.VMEM((own_tokens, width), BF16),
            pltpu.VMEM((SUB * SUB, own_tokens, 3 * HEAD_DIM), BF16),
        ],
        flops=2 * own_tokens * width * 3 * width,
        name="finish",
    )
    return finished.transpose(1, 0, 2)


def solution(mesh):
    gx_size = mesh.shape["gx"]
    cut = Mesh(mesh.devices.reshape(gx_size, SUB, SUB), ("gx", "gz", "gq"))
    gy = ("gz", "gq")
    flat = P("gx", gy)
    deep = P("gx", None, gy)
    placed = (
        P(("gx", *gy), None),
        P(),
        P("gx"),
        P(),
        P(),
        P(gy, None),
        P(),
        deep,
        flat,
        P(),
        flat,
        flat,
        P(),
        deep,
        P(),
        deep,
        flat,
        P(),
        flat,
        flat,
        P(),
        deep,
    )
    return jax.shard_map(
        per_device,
        mesh=cut,
        in_specs=placed,
        out_specs=P(("gx", *gy), None, None),
        check_vma=False,
    )
```

```python
import functools
import math

import jax
import jax.numpy as jnp
from jax import lax
from jax.experimental import pallas as pl
from jax.experimental.pallas import tpu as pltpu
from jax.sharding import Mesh, PartitionSpec as P

HEAD_DIM = 88
LANES = 128
SUB = 4
NORM_EPS = 1e-06
F32 = jnp.float32
BF16 = jnp.bfloat16
VMEM_LIMIT = 50 * 1024 * 1024


def merge_sources(grid_rows, merge_slots):
    image_count = grid_rows.shape[0]
    merged_count = grid_rows[:, 0] * grid_rows[:, 1]
    merged_end = jnp.cumsum(merged_count)
    merged_start = merged_end - merged_count
    slot_index = jnp.arange(merge_slots, dtype=jnp.int32)
    image_of = jnp.sum((slot_index[:, None] >= merged_end[None, :]).astype(jnp.int32), axis=1)
    is_live = image_of < image_count
    picked = (
        jnp.minimum(image_of, image_count - 1)[:, None]
        == jnp.arange(image_count, dtype=jnp.int32)[None, :]
    ).astype(jnp.int32)
    col_count = jnp.sum(picked * grid_rows[None, :, 1], axis=1)
    first_slot = jnp.sum(picked * merged_start[None, :], axis=1)
    local_slot = slot_index - first_slot
    grid_row = local_slot // col_count
    grid_col = local_slot % col_count
    base_row = 4 * first_slot + 4 * grid_row * col_count + 2 * grid_col
    offsets = jnp.stack(
        [jnp.zeros_like(col_count), jnp.ones_like(col_count), 2 * col_count, 2 * col_count + 1],
        axis=1,
    )
    sources = jnp.where(is_live[:, None], base_row[:, None] + offsets, 0)
    return sources, image_of, is_live


def shift_in(axis, values, step):
    return lax.ppermute(values, axis, [(i, (i + step) % SUB) for i in range(SUB)])


def gather_four(axis, values):
    return [values] + [shift_in(axis, values, k) for k in range(1, SUB)]


def exchange(axis, pieces):
    return lax.all_to_all(pieces, axis, 0, 0)


def collect(axis, values, size):
    return exchange(axis, jnp.broadcast_to(values, (size,) + values.shape))


SMEM = pl.BlockSpec(memory_space=pltpu.SMEM)
VMEM = pl.BlockSpec(memory_space=pltpu.VMEM)


def shape(*dims, dtype=BF16):
    return jax.ShapeDtypeStruct(dims, dtype)


def call(body, outs, args, specs=None, grid=None, out_specs=None, scratch=(), flops=0, name=None):
    if specs is None:
        specs = [VMEM] * len(args)
    if out_specs is None:
        out_specs = jax.tree.map(lambda _: VMEM, outs)
    moved = sum(math.prod(a.shape) * a.dtype.itemsize for a in args)
    kwargs = {} if grid is None else {"grid": grid}
    return pl.pallas_call(
        body,
        out_shape=outs,
        in_specs=specs,
        out_specs=out_specs,
        scratch_shapes=list(scratch),
        cost_estimate=pl.CostEstimate(
            flops=flops, bytes_accessed=moved if flops else 0, transcendentals=0
        ),
        compiler_params=pltpu.CompilerParams(vmem_limit_bytes=VMEM_LIMIT),
        name=name,
        **kwargs,
    )(*args)


def back(own, step):
    return lax.rem(own + (SUB - step), SUB)


def ahead(own, step):
    return lax.rem(own + step, SUB)


def dot(left, right):
    return jnp.dot(left, right, preferred_element_type=F32)


def layer_norm_rows(values, gain):
    centre = values - jnp.mean(values, axis=-1, keepdims=True)
    spread = jnp.mean(centre * centre, axis=-1, keepdims=True)
    return (centre * lax.rsqrt(spread + NORM_EPS) * gain).astype(BF16)


def rms_norm_rows(values, gain):
    square = jnp.mean(values * values, axis=-1, keepdims=True)
    return (values * lax.rsqrt(square + NORM_EPS) * gain).astype(BF16)


def gelu(values):
    return 0.5 * values * (1.0 + lax.erf(values * (2.0**-0.5)))


def pad_heads(values):
    empty = jnp.zeros((values.shape[0], LANES - HEAD_DIM), values.dtype)
    parts = []
    for t in range(3):
        parts += [values[:, t * HEAD_DIM : (t + 1) * HEAD_DIM], empty]
    return jnp.concatenate(parts, axis=1)


def vit_attention_body(r0, r1, r2, r3, weight, gain, source, query_class, key_class, out, triple, merged):
    slots = triple.shape[0]
    step = slots // SUB
    for i, rows in enumerate((r0, r1, r2, r3)):
        normed = layer_norm_rows(rows[...].astype(F32), gain[...])
        triple[i * step : (i + 1) * step, :] = pad_heads(dot(normed, weight[...]).astype(BF16))

    def reorder(i, _):
        part = pl.ds(pl.multiple_of(i * step, step), step)
        chosen = (
            source[part, :] == lax.broadcasted_iota(jnp.int32, (step, slots), 1)
        ).astype(BF16)
        merged[part, :] = dot(chosen, triple[...]).astype(BF16)
        return 0

    lax.fori_loop(0, SUB, reorder, 0)
    for i in range(SUB):
        at = i * step
        scores = lax.dot_general(
            merged[at : at + step, :LANES],
            merged[:, LANES : 2 * LANES],
            (((1,), (1,)), ((), ())),
            preferred_element_type=F32,
        ) * HEAD_DIM ** (-0.5)
        allowed = query_class[at : at + step, :] == key_class[...]
        exp_scores = jnp.where(allowed, jnp.exp(scores), 0.0)
        denominator = jnp.sum(exp_scores, axis=1, keepdims=True)
        weighted = dot(exp_scores.astype(BF16), merged[:, 2 * LANES :])
        result = (weighted / denominator).astype(BF16)
        for q in range(SUB):
            out[i * SUB + q] = result


def pick_rows_body(source, r0, r1, r2, r3, out):
    rows = r0.shape[0]
    total = None
    for i, ref in enumerate((r0, r1, r2, r3)):
        at = lax.broadcasted_iota(jnp.int32, (source.shape[0], rows), 1) + i * rows
        term = dot((source[...] == at).astype(BF16), ref[...])
        total = term if total is None else total + term
    out[...] = total.astype(BF16)


def join_heads(blocks):
    return jnp.concatenate([block[:, :HEAD_DIM] for block in blocks], axis=1)


def out_projection_body(first, heads, weight, out, left, done):
    step = pl.program_id(0)

    @pl.when(step == 0)
    def _():
        left[...] = join_heads([heads[h] for h in range(SUB * SUB)])

    done[step, :, :HEAD_DIM] = dot(left[...], weight[0])[:, first : first + HEAD_DIM].astype(BF16)

    @pl.when(step == SUB - 1)
    def _():
        out[:, : SUB * HEAD_DIM] = join_heads([done[z] for z in range(SUB)])


def hold_blocks(refs, own_q, held):
    for k, ref in enumerate(refs):
        held[back(own_q, k)] = ref[...]


def in_order(held, rows=slice(None)):
    return jnp.concatenate(
        [
            held[q, rows, z * HEAD_DIM : (z + 1) * HEAD_DIM]
            for z in range(SUB)
            for q in range(SUB)
        ],
        axis=1,
    )


def feed_forward_body(norm, place, o0, o1, o2, o3, stream, gain, weight, *rest):
    outs, (mid_out, held, mid, normed, total) = rest[:SUB], rest[SUB:]
    own_q = place[2]
    step = pl.program_id(0)
    rows = stream.shape[0]
    share = rows // SUB
    hidden_width = weight.shape[2] // 2

    @pl.when(step == 0)
    def _():
        hold_blocks((o0, o1, o2, o3), own_q, held)

        def prepare(i, _):
            part = pl.ds(pl.multiple_of(i * 2 * share, 2 * share), 2 * share)
            added = in_order(held, part).astype(F32)
            summed = (stream[part, :].astype(F32) + added).astype(BF16)
            mid[part, :] = summed
            normed[part, :] = norm(summed.astype(F32), gain[...])
            return 0

        lax.fori_loop(0, SUB // 2, prepare, 0)

    hidden = gelu(dot(normed[...], weight[0, :, :hidden_width])).astype(BF16)
    down = lax.dot_general(
        hidden,
        weight[0, :, hidden_width:],
        (((1,), (1,)), ((), ())),
        preferred_element_type=F32,
    )

    @pl.when(step == 0)
    def _():
        total[...] = down

    @pl.when(step > 0)
    def _():
        total[...] += down

    @pl.when(step == SUB - 1)
    def _():
        for k in range(SUB):
            start = pl.multiple_of(ahead(own_q, k) * share, share)
            outs[k][...] = total[pl.ds(start, share), :].astype(BF16)
        mid_out[...] = mid[pl.ds(pl.multiple_of(own_q * share, share), share), :]


def summed_stream(partials, mid):
    summed = partials[0][...].astype(F32)
    for ref in partials[1:]:
        summed += ref[...].astype(F32)
    return (mid[...].astype(F32) + summed).astype(BF16).astype(F32)


def merge_norm_body(p0, p1, p2, p3, mid, gain, out):
    rows, width = mid.shape
    final = summed_stream((p0, p1, p2, p3), mid)
    row = lax.broadcasted_iota(jnp.int32, (rows, rows), 0)
    col = lax.broadcasted_iota(jnp.int32, (rows, rows), 1)
    same_group = row // 4 == col // 4

    def group_mean(column):
        across = jnp.sum(jnp.where(same_group, column, 0.0), axis=0, keepdims=True)
        down = jnp.sum(jnp.where(row == col, across, 0.0), axis=1, keepdims=True)
        return down / (4 * width)

    centre = final - group_mean(jnp.sum(final, axis=1, keepdims=True))
    spread = group_mean(jnp.sum(centre * centre, axis=1, keepdims=True))
    out[...] = (centre * lax.rsqrt(spread + NORM_EPS) * gain[...]).astype(BF16)


def merge_projection_body(place, g0, g1, g2, g3, w0, w1, out, rows, left, done):
    own_q = place[2]
    step = pl.program_id(0)
    share = g0.shape[0]
    count = rows.shape[0]
    slots = count // 4

    @pl.when(step == 0)
    def _():
        for k, ref in enumerate((g0, g1, g2, g3)):
            rows[pl.ds(pl.multiple_of(back(own_q, k) * share, share), share), :] = ref[...]
        new_row = lax.broadcasted_iota(jnp.int32, (count, count), 0)
        old_row = lax.broadcasted_iota(jnp.int32, (count, count), 1)
        chosen = ((new_row % slots) * 4 + new_row // slots == old_row).astype(BF16)
        left[...] = dot(chosen, rows[...]).astype(BF16)

    products = jnp.concatenate([dot(left[...], w0[0]), dot(left[...], w1[0])], axis=1)
    total = None
    for patch in range(4):
        at = (patch + 1) * HEAD_DIM
        term = products[patch * slots : (patch + 1) * slots, at : at + HEAD_DIM]
        total = term if total is None else total + term
    done[step, :, :HEAD_DIM] = total.astype(BF16)

    @pl.when(step == SUB - 1)
    def _():
        projected = join_heads([done[z] for z in range(SUB)])
        for g in range(out.shape[0]):
            out[g, :, : SUB * HEAD_DIM] = projected


def text_rows_body(place, ids, table, *rest):
    outs, (total,) = rest[:SUB], rest[SUB:]
    own_q = place[2]
    step = pl.program_id(0)
    last = pl.num_programs(0) - 1
    count = table.shape[0]
    tokens = ids.shape[0]
    share = tokens // SUB
    first = (place[1] * SUB + own_q) * count * pl.num_programs(0) + step * count
    chosen = (ids[...] - first == lax.broadcasted_iota(jnp.int32, (tokens, count), 1)).astype(BF16)
    found = dot(chosen, table[...])

    @pl.when(step == 0)
    def _():
        total[...] = found

    @pl.when(step > 0)
    def _():
        total[...] += found

    @pl.when(step == last)
    def _():
        def hand_out(i, _):
            rows = pl.ds(pl.multiple_of(i * share, share), share)
            for q in range(SUB):
                blocks = [
                    total[rows, at : at + HEAD_DIM]
                    for at in range(q * HEAD_DIM, total.shape[1], SUB * HEAD_DIM)
                ]
                columns = jnp.concatenate(blocks, axis=1).astype(BF16)
                for k in range(SUB):

                    @pl.when(ahead(own_q, k) == q)
                    def _():
                        outs[k][rows, : SUB * HEAD_DIM] = columns

            return 0

        lax.fori_loop(0, SUB, hand_out, 0)


def place_body(seq, is_image, slot_position, projected, t0, t1, t2, t3, out):
    chosen = (seq[...] == slot_position[...]).astype(BF16)
    placed = dot(chosen, projected[...])
    text = t0[...].astype(F32) + t1[...].astype(F32) + t2[...].astype(F32) + t3[...].astype(F32)
    width = SUB * HEAD_DIM
    out[:, :width] = jnp.where(is_image[...] > 0, placed, text)[:, :width].astype(BF16)


def dec_qkv_body(place, g0, g1, g2, g3, gain, weight, out, embedded_out, held, normed):
    @pl.when(pl.program_id(0) == 0)
    def _():
        hold_blocks((g0, g1, g2, g3), place[2], held)
        embedded = in_order(held)
        embedded_out[...] = embedded
        normed[...] = rms_norm_rows(embedded.astype(F32), gain[...])

    out[0] = pad_heads(dot(normed[...], weight[0])[:, : 3 * HEAD_DIM].astype(BF16))


def attend_blocks(own_gx, core, triple, query_request, query_position, request, blocks, weighted, denominator):
    tokens = triple.shape[0]
    part = tokens // 2

    def attend(k, _):
        owner = 2 * lax.rem(lax.div(own_gx, 2) + (SUB - k), SUB) + core

        @pl.when(owner <= own_gx)
        def _():
            key_request = request[pl.ds(owner, 1), :]
            key_position = lax.broadcasted_iota(jnp.int32, (1, tokens), 1) + owner * tokens
            for at in range(0, tokens, part):
                rows = slice(at, at + part)
                scores = lax.dot_general(
                    triple[rows, :LANES],
                    blocks[k, :, :LANES],
                    (((1,), (1,)), ((), ())),
                    preferred_element_type=F32,
                ) * HEAD_DIM ** (-0.5)
                allowed = (key_request == query_request[rows, :]) & (
                    key_position <= query_position[rows, :]
                )
                exp_scores = jnp.where(allowed, jnp.exp(scores), 0.0)
                denominator[rows, :] += jnp.sum(exp_scores, axis=1, keepdims=True)
                weighted[rows, :] += dot(exp_scores.astype(BF16), blocks[k, :, LANES:])

        return 0

    lax.fori_loop(0, SUB, attend, 0)


def near_attention_body(place, triple, query_request, query_position, request, near, weighted, denominator):
    weighted[...] = jnp.zeros_like(weighted)
    denominator[...] = jnp.zeros_like(denominator)
    attend_blocks(
        place[0], lax.rem(place[0], 2), triple, query_request, query_position, request, near, weighted, denominator
    )


def far_attention_body(
    place, triple, query_request, query_position, request, far, near_weighted, near_denominator, out, weighted, denominator
):
    weighted[...] = near_weighted[...]
    denominator[...] = near_denominator[...]
    attend_blocks(
        place[0], lax.rem(place[0] + 1, 2), triple, query_request, query_position, request, far, weighted, denominator
    )
    share = triple.shape[0] // SUB
    for z in range(SUB):
        rows = slice(z * share, (z + 1) * share)
        result = (weighted[rows, :] / denominator[rows, :]).astype(BF16)
        for q in range(SUB):
            out[z * SUB + q] = result


def finish_body(p0, p1, p2, p3, mid, gain, weight, out, normed, done):
    step = pl.program_id(0)
    count = weight.shape[0]

    @pl.when(step == 0)
    def _():
        normed[...] = rms_norm_rows(summed_stream((p0, p1, p2, p3), mid), gain[...])

    for i in range(count):
        done[step * count + i] = dot(normed[...], weight[i]).astype(BF16)

    @pl.when(step == pl.num_programs(0) - 1)
    def _():
        for t in range(3):
            out[t] = jnp.concatenate(
                [
                    done[h, :, t * HEAD_DIM : (t + 1) * HEAD_DIM]
                    for h in range(done.shape[0])
                ],
                axis=1,
            )


def block_spec(rows, width, at):
    return pl.BlockSpec((1, rows, width), lambda z: (z, 0, at))


def whole(values):
    rank = values.ndim
    return pl.BlockSpec(values.shape, lambda z: (0,) * rank)


def fixed(struct):
    rank = len(struct.shape)
    return pl.BlockSpec(struct.shape, lambda z: (0,) * rank)


def per_device(
    patches,
    grids,
    text_ids,
    positions,
    lengths,
    text_table,
    vit_norm1,
    vit_qkv,
    vit_out,
    vit_norm2,
    vit_fc1,
    vit_fc2,
    merge_norm,
    merge_proj,
    dec_norm1,
    dec_qkv,
    dec_out,
    dec_norm2,
    dec_fc1,
    dec_fc2,
    next_norm,
    next_qkv,
):
    gx_count = lax.axis_size("gx")
    own_gx, own_z, own_q = lax.axis_index("gx"), lax.axis_index("gz"), lax.axis_index("gq")
    place = jnp.stack([own_gx, own_z, own_q]).astype(jnp.int32)
    width = patches.shape[1]
    share = patches.shape[0]
    slots = share * SUB * SUB

    def join_weights(parts, lanes):
        columns = []
        for p in parts:
            columns += [p] if p.ndim == 2 else [p[:, t] for t in range(p.shape[1])]
        used = sum(c.shape[1] for c in columns)
        columns.append(jnp.zeros((columns[0].shape[0], lanes - used), BF16))
        return jnp.concatenate([c for c in columns if c.shape[1]], axis=1)

    def gather_weights(local):
        full = lax.all_gather(local, ("gz", "gx"), axis=0, tiled=True)
        return full.reshape(SUB, width, local.shape[1])

    vit_weights = gather_weights(join_weights([vit_fc1, vit_fc2, vit_out, merge_proj], 1280))

    per_group = grids.shape[0] // gx_count
    own_grids = lax.dynamic_slice_in_dim(grids, own_gx * per_group, per_group, 0)
    merge_slots = positions.shape[0] // gx_count
    sources, image_of, is_live = merge_sources(own_grids, merge_slots)
    holder = sources // share
    block = lax.rem(own_q + SUB - lax.rem(holder, SUB), SUB) * SUB + lax.rem(
        own_z + SUB - holder // SUB, SUB
    )
    source_column = (block * share + lax.rem(sources, share)).reshape(slots, 1)
    query_class = jnp.repeat(jnp.where(is_live, image_of, 0), 4).reshape(slots, 1)
    key_class = jnp.repeat(image_of, 4).reshape(1, slots)

    of_column = jnp.stack(gather_four("gz", patches))
    dec_local = join_weights([dec_fc1, dec_fc2, dec_qkv, dec_out], 1152)
    next_local = join_weights([next_qkv], 3 * HEAD_DIM)
    of_column, dec_local, next_local, source_column, query_class, key_class, qkv_parts = (
        lax.optimization_barrier(
            (of_column, dec_local, next_local, source_column, query_class, key_class, vit_qkv)
        )
    )
    patches_full = [
        rows.reshape(SUB * share, width) for rows in gather_four("gq", of_column)
    ]
    dec_weights = gather_weights(dec_local)
    own_qkv = jnp.concatenate([qkv_parts[:, t] for t in range(3)], axis=1)
    qkv_weight = lax.all_gather(own_qkv, "gx", axis=0, tiled=True)

    row = lambda gain: gain.reshape(1, -1)
    group_rows = slots // SUB
    attended = call(
        vit_attention_body,
        shape(SUB * SUB, group_rows, LANES),
        (*patches_full, qkv_weight, row(vit_norm1), source_column, query_class, key_class),
        scratch=[
            pltpu.VMEM((slots, 3 * LANES), BF16),
            pltpu.VMEM((slots, 3 * LANES), BF16),
        ],
        flops=2 * slots * (width * 3 * LANES + slots * 5 * LANES),
        name="vit_attention",
    )
    attended, ids, next_local = lax.optimization_barrier((attended, text_ids, next_local))
    next_weights = lax.all_gather(next_local, ("gz", "gq", "gx"), axis=0, tiled=True).reshape(
        SUB * SUB, width, 3 * HEAD_DIM
    )

    tokens = text_ids.shape[0]
    part = tokens // SUB
    block_width = SUB * HEAD_DIM
    block_lanes = 3 * LANES
    table_step = text_table.shape[0] // 5
    text_blocks = call(
        text_rows_body,
        [shape(tokens, block_lanes)] * SUB,
        (place, ids.reshape(tokens, 1), text_table),
        specs=[
            SMEM,
            pl.BlockSpec((tokens, 1), lambda i: (0, 0)),
            pl.BlockSpec((table_step, width), lambda i: (i, 0)),
        ],
        grid=(5,),
        out_specs=[pl.BlockSpec((tokens, block_lanes), lambda i: (0, 0))] * SUB,
        scratch=[pltpu.VMEM((tokens, width), F32)],
        flops=2 * tokens * text_table.shape[0] * width,
        name="text_rows",
    )
    own_sources = lax.dynamic_slice_in_dim(source_column, own_z * group_rows, group_rows, 0)
    stream = call(
        pick_rows_body,
        shape(group_rows, width),
        (own_sources, *patches_full),
        flops=2 * slots * group_rows * width,
        name="pick_rows",
    )

    def attention_output(attended, weights, at, name, beside=()):
        heads = exchange(("gz", "gq"), attended)
        heads, beside = lax.optimization_barrier((heads, beside))
        rows = heads.shape[1]
        return call(
            functools.partial(out_projection_body, at % LANES),
            shape(rows, block_lanes),
            (heads, weights),
            specs=[whole(heads), block_spec(width, LANES, at // LANES)],
            grid=(SUB,),
            out_specs=pl.BlockSpec((rows, block_lanes), lambda z: (0, 0)),
            scratch=[pltpu.VMEM((rows, width), BF16), pltpu.VMEM((SUB, rows, LANES), BF16)],
            flops=2 * rows * width * SUB * LANES,
            name=name,
        ), beside

    def feed_forward(projected, stream, gain, weights, norm, name):
        rows = stream.shape[0]
        own = rows // SUB
        gathered = gather_four("gq", projected)
        hidden_width = vit_fc1.shape[1]
        outs = [shape(own, width)] * (SUB + 1)
        *pieces, mid = call(
            functools.partial(feed_forward_body, norm),
            outs,
            (place, *gathered, stream, gain, weights),
            specs=[SMEM]
            + [whole(g) for g in gathered]
            + [whole(stream), whole(gain), block_spec(width, 2 * hidden_width, 0)],
            grid=(SUB,),
            out_specs=[fixed(o) for o in outs],
            scratch=[
                pltpu.VMEM((SUB, rows, block_lanes), BF16),
                pltpu.VMEM((rows, width), BF16),
                pltpu.VMEM((rows, width), BF16),
                pltpu.VMEM((rows, width), F32),
            ],
            flops=4 * rows * width * SUB * hidden_width,
            name=name,
        )
        return [pieces[0]] + [shift_in("gq", pieces[k], k) for k in range(1, SUB)], mid

    text_parts = [text_blocks[0]] + [shift_in("gq", text_blocks[k], k) for k in (1, 3)]
    projected, (stream, text_parts) = attention_output(
        attended, vit_weights, 768, "vit_output", (stream, text_parts)
    )
    partials, mid = feed_forward(
        projected,
        stream,
        row(vit_norm2),
        vit_weights,
        layer_norm_rows,
        "vit_feed_forward",
    )

    gain_rows = jnp.tile(merge_norm, (share // 4, 1))
    merged = call(merge_norm_body, shape(share, width), (*partials, mid, gain_rows), name="merge_norm")
    gathered = gather_four("gq", merged)
    gathered, last_block = lax.optimization_barrier((gathered, text_blocks[2]))
    text_parts.append(shift_in("gq", last_block, 2))
    group_slots = group_rows // 4
    outs = shape(gx_count, group_slots, block_lanes)
    projected = call(
        merge_projection_body,
        outs,
        (place, *gathered, vit_weights, vit_weights),
        specs=[SMEM]
        + [whole(g) for g in gathered]
        + [block_spec(width, 2 * LANES, 3), block_spec(width, 2 * LANES, 4)],
        grid=(SUB,),
        out_specs=fixed(outs),
        scratch=[
            pltpu.VMEM((group_rows, width), BF16),
            pltpu.VMEM((group_rows, width), BF16),
            pltpu.VMEM((SUB, group_slots, LANES), BF16),
        ],
        flops=2 * group_rows * width * SUB * LANES,
        name="merge_projection",
    )
    all_projected = exchange("gx", projected).reshape(gx_count * group_slots, block_lanes)

    own_index = own_gx * tokens + jnp.arange(tokens, dtype=jnp.int32)
    is_image = jnp.any(positions[None, :] == own_index[:, None], axis=1).astype(F32)
    by_slot = lax.dynamic_index_in_dim(
        positions.reshape(gx_count, SUB, group_slots), own_z, 1, keepdims=False
    )
    placed = call(
        place_body,
        shape(tokens, block_lanes),
        (
            own_index.reshape(tokens, 1),
            is_image.reshape(tokens, 1),
            by_slot.reshape(1, -1),
            all_projected,
            *text_parts,
        ),
        flops=2 * tokens * by_slot.size * block_width,
        name="place_rows",
    )
    own_rows = jnp.sum(
        exchange("gz", placed.reshape(SUB, part, block_lanes)).astype(F32), axis=0
    ).astype(BF16)
    gathered = gather_four("gq", own_rows)

    outs = [shape(SUB, part, 3 * LANES), shape(part, width)]
    triple, embedded = call(
        dec_qkv_body,
        outs,
        (place, *gathered, row(dec_norm1), dec_weights),
        specs=[SMEM]
        + [whole(a) for a in (*gathered, row(dec_norm1))]
        + [block_spec(width, 3 * LANES, 2)],
        grid=(SUB,),
        out_specs=[pl.BlockSpec((1, part, 3 * LANES), lambda z: (z, 0, 0)), fixed(outs[1])],
        scratch=[pltpu.VMEM((SUB, part, block_lanes), BF16), pltpu.VMEM((part, width), BF16)],
        flops=2 * part * width * SUB * 3 * LANES,
        name="dec_qkv",
    )
    triple = exchange("gz", triple).reshape(tokens, 3 * LANES)
    key_values = triple[:, LANES:]
    near = jnp.stack(
        [key_values]
        + [
            lax.ppermute(
                key_values,
                "gx",
                [(2 * y + c, 2 * ((y + k) % SUB) + c) for y in range(SUB) for c in range(2)],
            )
            for k in range(1, SUB)
        ]
    )
    far = lax.ppermute(near, "gx", [(i, i ^ 1) for i in range(gx_count)])
    bounds = jnp.cumsum(lengths)
    all_index = jnp.arange(gx_count * tokens, dtype=jnp.int32).reshape(gx_count, tokens)
    request = jnp.sum((all_index[:, :, None] >= bounds).astype(jnp.int32), axis=2)
    own_request = jnp.sum((own_index[:, None] >= bounds).astype(jnp.int32), axis=1)
    tables = (place, triple, own_request.reshape(tokens, 1), own_index.reshape(tokens, 1), request)
    sums = [shape(tokens, LANES, dtype=F32), shape(tokens, 1, dtype=F32)]
    weighted, denominator = call(
        near_attention_body,
        sums,
        (*tables, near),
        specs=[SMEM] + [VMEM] * 5,
        flops=2 * tokens * tokens * gx_count * LANES,
        name="near_attention",
    )
    attended = call(
        far_attention_body,
        shape(SUB * SUB, part, LANES),
        (*tables, far, weighted, denominator),
        specs=[SMEM] + [VMEM] * 7,
        scratch=[pltpu.VMEM(sums[0].shape, F32), pltpu.VMEM(sums[1].shape, F32)],
        flops=2 * tokens * tokens * gx_count * LANES,
        name="far_attention",
    )
    projected, _ = attention_output(attended, dec_weights, 1032, "dec_output")
    partials, mid = feed_forward(
        projected, embedded, row(dec_norm2), dec_weights, rms_norm_rows, "dec_feed_forward"
    )
    own_tokens = mid.shape[0]

    at_once = 2
    finished = call(
        finish_body,
        shape(3, own_tokens, width),
        (*partials, mid, row(next_norm), next_weights),
        specs=[whole(p) for p in (*partials, mid)]
        + [pl.BlockSpec((1, width), lambda z: (0, 0))]
        + [pl.BlockSpec((at_once, width, 3 * HEAD_DIM), lambda z: (z, 0, 0))],
        grid=(SUB * SUB // at_once,),
        out_specs=pl.BlockSpec((3, own_tokens, width), lambda z: (0, 0, 0)),
        scratch=[
            pltpu.VMEM((own_tokens, width), BF16),
            pltpu.VMEM((SUB * SUB, own_tokens, 3 * HEAD_DIM), BF16),
        ],
        flops=2 * own_tokens * width * 3 * width,
        name="finish",
    )
    return finished.transpose(1, 0, 2)


def solution(mesh):
    gx_size = mesh.shape["gx"]
    cut = Mesh(mesh.devices.reshape(gx_size, SUB, SUB), ("gx", "gz", "gq"))
    gy = ("gz", "gq")
    flat = P("gx", gy)
    deep = P("gx", None, gy)
    placed = (
        P(("gx", *gy), None),
        P(),
        P("gx"),
        P(),
        P(),
        P(gy, None),
        P(),
        deep,
        flat,
        P(),
        flat,
        flat,
        P(),
        deep,
        P(),
        deep,
        flat,
        P(),
        flat,
        flat,
        P(),
        deep,
    )
    return jax.shard_map(
        per_device,
        mesh=cut,
        in_specs=placed,
        out_specs=P(("gx", *gy), None, None),
        check_vma=False,
    )
```

```python
import functools
import math

import jax
import jax.numpy as jnp
from jax import lax
from jax.experimental import pallas as pl
from jax.experimental.pallas import tpu as pltpu
from jax.sharding import Mesh, PartitionSpec as P

HEAD_DIM = 88
LANES = 128
SUB = 4
NORM_EPS = 1e-06
F32 = jnp.float32
BF16 = jnp.bfloat16
VMEM_LIMIT = 50 * 1024 * 1024


def merge_sources(grid_rows, merge_slots):
    image_count = grid_rows.shape[0]
    merged_count = grid_rows[:, 0] * grid_rows[:, 1]
    merged_end = jnp.cumsum(merged_count)
    merged_start = merged_end - merged_count
    slot_index = jnp.arange(merge_slots, dtype=jnp.int32)
    image_of = jnp.sum((slot_index[:, None] >= merged_end[None, :]).astype(jnp.int32), axis=1)
    is_live = image_of < image_count
    picked = (
        jnp.minimum(image_of, image_count - 1)[:, None]
        == jnp.arange(image_count, dtype=jnp.int32)[None, :]
    ).astype(jnp.int32)
    col_count = jnp.sum(picked * grid_rows[None, :, 1], axis=1)
    first_slot = jnp.sum(picked * merged_start[None, :], axis=1)
    local_slot = slot_index - first_slot
    grid_row = local_slot // col_count
    grid_col = local_slot % col_count
    base_row = 4 * first_slot + 4 * grid_row * col_count + 2 * grid_col
    offsets = jnp.stack(
        [jnp.zeros_like(col_count), jnp.ones_like(col_count), 2 * col_count, 2 * col_count + 1],
        axis=1,
    )
    sources = jnp.where(is_live[:, None], base_row[:, None] + offsets, 0)
    return sources, image_of, is_live


def shift_in(axis, values, step):
    return lax.ppermute(values, axis, [(i, (i + step) % SUB) for i in range(SUB)])


def gather_four(axis, values):
    return [values] + [shift_in(axis, values, k) for k in range(1, SUB)]


def exchange(axis, pieces):
    return lax.all_to_all(pieces, axis, 0, 0)


def collect(axis, values, size):
    return exchange(axis, jnp.broadcast_to(values, (size,) + values.shape))


SMEM = pl.BlockSpec(memory_space=pltpu.SMEM)
VMEM = pl.BlockSpec(memory_space=pltpu.VMEM)


def shape(*dims, dtype=BF16):
    return jax.ShapeDtypeStruct(dims, dtype)


def call(body, outs, args, specs=None, grid=None, out_specs=None, scratch=(), flops=0, name=None):
    if specs is None:
        specs = [VMEM] * len(args)
    if out_specs is None:
        out_specs = jax.tree.map(lambda _: VMEM, outs)
    moved = sum(math.prod(a.shape) * a.dtype.itemsize for a in args)
    kwargs = {} if grid is None else {"grid": grid}
    return pl.pallas_call(
        body,
        out_shape=outs,
        in_specs=specs,
        out_specs=out_specs,
        scratch_shapes=list(scratch),
        cost_estimate=pl.CostEstimate(
            flops=flops, bytes_accessed=moved if flops else 0, transcendentals=0
        ),
        compiler_params=pltpu.CompilerParams(vmem_limit_bytes=VMEM_LIMIT),
        name=name,
        **kwargs,
    )(*args)


def back(own, step):
    return lax.rem(own + (SUB - step), SUB)


def ahead(own, step):
    return lax.rem(own + step, SUB)


def dot(left, right):
    return jnp.dot(left, right, preferred_element_type=F32)


def layer_norm_rows(values, gain):
    centre = values - jnp.mean(values, axis=-1, keepdims=True)
    spread = jnp.mean(centre * centre, axis=-1, keepdims=True)
    return (centre * lax.rsqrt(spread + NORM_EPS) * gain).astype(BF16)


def rms_norm_rows(values, gain):
    square = jnp.mean(values * values, axis=-1, keepdims=True)
    return (values * lax.rsqrt(square + NORM_EPS) * gain).astype(BF16)


def gelu(values):
    return 0.5 * values * (1.0 + lax.erf(values * (2.0**-0.5)))


def pad_heads(values):
    empty = jnp.zeros((values.shape[0], LANES - HEAD_DIM), values.dtype)
    parts = []
    for t in range(3):
        parts += [values[:, t * HEAD_DIM : (t + 1) * HEAD_DIM], empty]
    return jnp.concatenate(parts, axis=1)


def vit_attention_body(r0, r1, r2, r3, weight, gain, source, query_class, key_class, out, triple, merged):
    slots = triple.shape[0]
    step = slots // SUB
    for i, rows in enumerate((r0, r1, r2, r3)):
        normed = layer_norm_rows(rows[...].astype(F32), gain[...])
        triple[i * step : (i + 1) * step, :] = pad_heads(dot(normed, weight[...]).astype(BF16))

    def reorder(i, _):
        part = pl.ds(pl.multiple_of(i * step, step), step)
        chosen = (
            source[part, :] == lax.broadcasted_iota(jnp.int32, (step, slots), 1)
        ).astype(BF16)
        merged[part, :] = dot(chosen, triple[...]).astype(BF16)
        return 0

    lax.fori_loop(0, SUB, reorder, 0)
    for i in range(SUB):
        at = i * step
        scores = lax.dot_general(
            merged[at : at + step, :LANES],
            merged[:, LANES : 2 * LANES],
            (((1,), (1,)), ((), ())),
            preferred_element_type=F32,
        ) * HEAD_DIM ** (-0.5)
        allowed = query_class[at : at + step, :] == key_class[...]
        exp_scores = jnp.where(allowed, jnp.exp(scores), 0.0)
        denominator = jnp.sum(exp_scores, axis=1, keepdims=True)
        weighted = dot(exp_scores.astype(BF16), merged[:, 2 * LANES :])
        result = (weighted / denominator).astype(BF16)
        for q in range(SUB):
            out[i * SUB + q] = result


def pick_rows_body(source, r0, r1, r2, r3, out):
    rows = r0.shape[0]
    total = None
    for i, ref in enumerate((r0, r1, r2, r3)):
        at = lax.broadcasted_iota(jnp.int32, (source.shape[0], rows), 1) + i * rows
        term = dot((source[...] == at).astype(BF16), ref[...])
        total = term if total is None else total + term
    out[...] = total.astype(BF16)


def join_heads(blocks):
    return jnp.concatenate([block[:, :HEAD_DIM] for block in blocks], axis=1)


def out_projection_body(first, heads, weight, out, left, done):
    step = pl.program_id(0)

    @pl.when(step == 0)
    def _():
        left[...] = join_heads([heads[h] for h in range(SUB * SUB)])

    done[step, :, :HEAD_DIM] = dot(left[...], weight[0])[:, first : first + HEAD_DIM].astype(BF16)

    @pl.when(step == SUB - 1)
    def _():
        out[:, : SUB * HEAD_DIM] = join_heads([done[z] for z in range(SUB)])


def hold_blocks(refs, own_q, held):
    for k, ref in enumerate(refs):
        held[back(own_q, k)] = ref[...]


def in_order(held, rows=slice(None)):
    return jnp.concatenate(
        [
            held[q, rows, z * HEAD_DIM : (z + 1) * HEAD_DIM]
            for z in range(SUB)
            for q in range(SUB)
        ],
        axis=1,
    )


def feed_forward_body(norm, place, o0, o1, o2, o3, stream, gain, weight, *rest):
    outs, (mid_out, held, mid, normed, total) = rest[:SUB], rest[SUB:]
    own_q = place[2]
    step = pl.program_id(0)
    rows = stream.shape[0]
    share = rows // SUB
    hidden_width = weight.shape[2] // 2

    @pl.when(step == 0)
    def _():
        hold_blocks((o0, o1, o2, o3), own_q, held)

        def prepare(i, _):
            part = pl.ds(pl.multiple_of(i * 2 * share, 2 * share), 2 * share)
            added = in_order(held, part).astype(F32)
            summed = (stream[part, :].astype(F32) + added).astype(BF16)
            mid[part, :] = summed
            normed[part, :] = norm(summed.astype(F32), gain[...])
            return 0

        lax.fori_loop(0, SUB // 2, prepare, 0)

    hidden = gelu(dot(normed[...], weight[0, :, :hidden_width])).astype(BF16)
    down = lax.dot_general(
        hidden,
        weight[0, :, hidden_width:],
        (((1,), (1,)), ((), ())),
        preferred_element_type=F32,
    )

    @pl.when(step == 0)
    def _():
        total[...] = down

    @pl.when(step > 0)
    def _():
        total[...] += down

    @pl.when(step == SUB - 1)
    def _():
        for k in range(SUB):
            start = pl.multiple_of(ahead(own_q, k) * share, share)
            outs[k][...] = total[pl.ds(start, share), :].astype(BF16)
        mid_out[...] = mid[pl.ds(pl.multiple_of(own_q * share, share), share), :]


def summed_stream(partials, mid):
    summed = partials[0][...].astype(F32)
    for ref in partials[1:]:
        summed += ref[...].astype(F32)
    return (mid[...].astype(F32) + summed).astype(BF16).astype(F32)


def merge_norm_body(p0, p1, p2, p3, mid, gain, out):
    rows, width = mid.shape
    final = summed_stream((p0, p1, p2, p3), mid)
    row = lax.broadcasted_iota(jnp.int32, (rows, rows), 0)
    col = lax.broadcasted_iota(jnp.int32, (rows, rows), 1)
    same_group = row // 4 == col // 4

    def group_mean(column):
        across = jnp.sum(jnp.where(same_group, column, 0.0), axis=0, keepdims=True)
        down = jnp.sum(jnp.where(row == col, across, 0.0), axis=1, keepdims=True)
        return down / (4 * width)

    centre = final - group_mean(jnp.sum(final, axis=1, keepdims=True))
    spread = group_mean(jnp.sum(centre * centre, axis=1, keepdims=True))
    out[...] = (centre * lax.rsqrt(spread + NORM_EPS) * gain[...]).astype(BF16)


def merge_projection_body(place, g0, g1, g2, g3, w0, w1, out, rows, left, done):
    own_q = place[2]
    step = pl.program_id(0)
    share = g0.shape[0]
    count = rows.shape[0]
    slots = count // 4

    @pl.when(step == 0)
    def _():
        for k, ref in enumerate((g0, g1, g2, g3)):
            rows[pl.ds(pl.multiple_of(back(own_q, k) * share, share), share), :] = ref[...]
        new_row = lax.broadcasted_iota(jnp.int32, (count, count), 0)
        old_row = lax.broadcasted_iota(jnp.int32, (count, count), 1)
        chosen = ((new_row % slots) * 4 + new_row // slots == old_row).astype(BF16)
        left[...] = dot(chosen, rows[...]).astype(BF16)

    products = jnp.concatenate([dot(left[...], w0[0]), dot(left[...], w1[0])], axis=1)
    total = None
    for patch in range(4):
        at = (patch + 1) * HEAD_DIM
        term = products[patch * slots : (patch + 1) * slots, at : at + HEAD_DIM]
        total = term if total is None else total + term
    done[step, :, :HEAD_DIM] = total.astype(BF16)

    @pl.when(step == SUB - 1)
    def _():
        projected = join_heads([done[z] for z in range(SUB)])
        for g in range(out.shape[0]):
            out[g, :, : SUB * HEAD_DIM] = projected


def text_rows_body(place, ids, table, *rest):
    outs, (total,) = rest[:SUB], rest[SUB:]
    own_q = place[2]
    step = pl.program_id(0)
    last = pl.num_programs(0) - 1
    count = table.shape[0]
    tokens = ids.shape[0]
    share = tokens // SUB
    first = (place[1] * SUB + own_q) * count * pl.num_programs(0) + step * count
    chosen = (ids[...] - first == lax.broadcasted_iota(jnp.int32, (tokens, count), 1)).astype(BF16)
    found = dot(chosen, table[...])

    @pl.when(step == 0)
    def _():
        total[...] = found

    @pl.when(step > 0)
    def _():
        total[...] += found

    @pl.when(step == last)
    def _():
        def hand_out(i, _):
            rows = pl.ds(pl.multiple_of(i * share, share), share)
            for q in range(SUB):
                blocks = [
                    total[rows, at : at + HEAD_DIM]
                    for at in range(q * HEAD_DIM, total.shape[1], SUB * HEAD_DIM)
                ]
                columns = jnp.concatenate(blocks, axis=1).astype(BF16)
                for k in range(SUB):

                    @pl.when(ahead(own_q, k) == q)
                    def _():
                        outs[k][rows, : SUB * HEAD_DIM] = columns

            return 0

        lax.fori_loop(0, SUB, hand_out, 0)


def place_body(seq, is_image, slot_position, projected, t0, t1, t2, t3, out):
    chosen = (seq[...] == slot_position[...]).astype(BF16)
    placed = dot(chosen, projected[...])
    text = t0[...].astype(F32) + t1[...].astype(F32) + t2[...].astype(F32) + t3[...].astype(F32)
    width = SUB * HEAD_DIM
    out[:, :width] = jnp.where(is_image[...] > 0, placed, text)[:, :width].astype(BF16)


def dec_qkv_body(place, g0, g1, g2, g3, gain, weight, out, embedded_out, held, normed):
    @pl.when(pl.program_id(0) == 0)
    def _():
        hold_blocks((g0, g1, g2, g3), place[2], held)
        embedded = in_order(held)
        embedded_out[...] = embedded
        normed[...] = rms_norm_rows(embedded.astype(F32), gain[...])

    out[0] = pad_heads(dot(normed[...], weight[0])[:, : 3 * HEAD_DIM].astype(BF16))


def attend_blocks(own_gx, core, triple, query_request, query_position, request, blocks, weighted, denominator):
    tokens = triple.shape[0]
    part = tokens // 2

    def attend(k, _):
        owner = 2 * lax.rem(lax.div(own_gx, 2) + (SUB - k), SUB) + core

        @pl.when(owner <= own_gx)
        def _():
            key_request = request[pl.ds(owner, 1), :]
            key_position = lax.broadcasted_iota(jnp.int32, (1, tokens), 1) + owner * tokens
            for at in range(0, tokens, part):
                rows = slice(at, at + part)
                scores = lax.dot_general(
                    triple[rows, :LANES],
                    blocks[k, :, :LANES],
                    (((1,), (1,)), ((), ())),
                    preferred_element_type=F32,
                ) * HEAD_DIM ** (-0.5)
                allowed = (key_request == query_request[rows, :]) & (
                    key_position <= query_position[rows, :]
                )
                exp_scores = jnp.where(allowed, jnp.exp(scores), 0.0)
                denominator[rows, :] += jnp.sum(exp_scores, axis=1, keepdims=True)
                weighted[rows, :] += dot(exp_scores.astype(BF16), blocks[k, :, LANES:])

        return 0

    lax.fori_loop(0, SUB, attend, 0)


def near_attention_body(place, triple, query_request, query_position, request, near, weighted, denominator):
    weighted[...] = jnp.zeros_like(weighted)
    denominator[...] = jnp.zeros_like(denominator)
    attend_blocks(
        place[0], lax.rem(place[0], 2), triple, query_request, query_position, request, near, weighted, denominator
    )


def far_attention_body(
    place, triple, query_request, query_position, request, far, near_weighted, near_denominator, out, weighted, denominator
):
    weighted[...] = near_weighted[...]
    denominator[...] = near_denominator[...]
    attend_blocks(
        place[0], lax.rem(place[0] + 1, 2), triple, query_request, query_position, request, far, weighted, denominator
    )
    share = triple.shape[0] // SUB
    for z in range(SUB):
        rows = slice(z * share, (z + 1) * share)
        result = (weighted[rows, :] / denominator[rows, :]).astype(BF16)
        for q in range(SUB):
            out[z * SUB + q] = result


def finish_body(half, p0, p1, p2, p3, mid, gain, weight, out, normed, done):
    step = pl.program_id(0)
    count = weight.shape[0]
    tokens = mid.shape[0]

    @pl.when(step == 0)
    def _():
        rows = rms_norm_rows(summed_stream((p0, p1, p2, p3), mid), gain[...])
        for side in range(2):
            starts = range(side * half, rows.shape[1], 2 * half)
            normed[side * tokens : (side + 1) * tokens, :] = jnp.concatenate(
                [rows[:, at : at + half] for at in starts], axis=1
            )

    for i in range(count):
        both = dot(normed[...], weight[i])
        used = both.shape[1] // 2
        done[step * count + i] = (both[:tokens, :used] + both[tokens:, used:]).astype(BF16)

    @pl.when(step == pl.num_programs(0) - 1)
    def _():
        for t in range(3):
            out[t] = jnp.concatenate(
                [
                    done[h, :, t * HEAD_DIM : (t + 1) * HEAD_DIM]
                    for h in range(done.shape[0])
                ],
                axis=1,
            )


def block_spec(rows, width, at):
    return pl.BlockSpec((1, rows, width), lambda z: (z, 0, at))


def whole(values):
    rank = values.ndim
    return pl.BlockSpec(values.shape, lambda z: (0,) * rank)


def fixed(struct):
    rank = len(struct.shape)
    return pl.BlockSpec(struct.shape, lambda z: (0,) * rank)


def per_device(
    patches,
    grids,
    text_ids,
    positions,
    lengths,
    text_table,
    vit_norm1,
    vit_qkv,
    vit_out,
    vit_norm2,
    vit_fc1,
    vit_fc2,
    merge_norm,
    merge_proj,
    dec_norm1,
    dec_qkv,
    dec_out,
    dec_norm2,
    dec_fc1,
    dec_fc2,
    next_norm,
    next_qkv,
):
    gx_count = lax.axis_size("gx")
    own_gx, own_z, own_q = lax.axis_index("gx"), lax.axis_index("gz"), lax.axis_index("gq")
    place = jnp.stack([own_gx, own_z, own_q]).astype(jnp.int32)
    width = patches.shape[1]
    share = patches.shape[0]
    slots = share * SUB * SUB

    def join_weights(parts, lanes):
        columns = []
        for p in parts:
            columns += [p] if p.ndim == 2 else [p[:, t] for t in range(p.shape[1])]
        used = sum(c.shape[1] for c in columns)
        columns.append(jnp.zeros((columns[0].shape[0], lanes - used), BF16))
        return jnp.concatenate([c for c in columns if c.shape[1]], axis=1)

    def gather_weights(local):
        full = lax.all_gather(local, ("gz", "gx"), axis=0, tiled=True)
        return full.reshape(SUB, width, local.shape[1])

    vit_weights = gather_weights(join_weights([vit_fc1, vit_fc2, vit_out, merge_proj], 1280))

    per_group = grids.shape[0] // gx_count
    own_grids = lax.dynamic_slice_in_dim(grids, own_gx * per_group, per_group, 0)
    merge_slots = positions.shape[0] // gx_count
    sources, image_of, is_live = merge_sources(own_grids, merge_slots)
    holder = sources // share
    block = lax.rem(own_q + SUB - lax.rem(holder, SUB), SUB) * SUB + lax.rem(
        own_z + SUB - holder // SUB, SUB
    )
    source_column = (block * share + lax.rem(sources, share)).reshape(slots, 1)
    query_class = jnp.repeat(jnp.where(is_live, image_of, 0), 4).reshape(slots, 1)
    key_class = jnp.repeat(image_of, 4).reshape(1, slots)

    of_column = jnp.stack(gather_four("gz", patches))
    dec_local = join_weights([dec_fc1, dec_fc2, dec_qkv, dec_out], 1152)
    half = next_qkv.shape[0] // 2
    next_local = join_weights([next_qkv[:half], next_qkv[half:]], 6 * HEAD_DIM)
    of_column, dec_local, next_local, source_column, query_class, key_class, qkv_parts = (
        lax.optimization_barrier(
            (of_column, dec_local, next_local, source_column, query_class, key_class, vit_qkv)
        )
    )
    patches_full = [
        rows.reshape(SUB * share, width) for rows in gather_four("gq", of_column)
    ]
    dec_weights = gather_weights(dec_local)
    own_qkv = jnp.concatenate([qkv_parts[:, t] for t in range(3)], axis=1)
    qkv_weight = lax.all_gather(own_qkv, "gx", axis=0, tiled=True)

    row = lambda gain: gain.reshape(1, -1)
    group_rows = slots // SUB
    attended = call(
        vit_attention_body,
        shape(SUB * SUB, group_rows, LANES),
        (*patches_full, qkv_weight, row(vit_norm1), source_column, query_class, key_class),
        scratch=[
            pltpu.VMEM((slots, 3 * LANES), BF16),
            pltpu.VMEM((slots, 3 * LANES), BF16),
        ],
        flops=2 * slots * (width * 3 * LANES + slots * 5 * LANES),
        name="vit_attention",
    )
    attended, ids, next_local = lax.optimization_barrier((attended, text_ids, next_local))
    next_weights = lax.all_gather(next_local, ("gz", "gq", "gx"), axis=0, tiled=True).reshape(
        SUB * SUB, width // 2, 6 * HEAD_DIM
    )

    tokens = text_ids.shape[0]
    part = tokens // SUB
    block_width = SUB * HEAD_DIM
    block_lanes = 3 * LANES
    table_step = text_table.shape[0] // 5
    text_blocks = call(
        text_rows_body,
        [shape(tokens, block_lanes)] * SUB,
        (place, ids.reshape(tokens, 1), text_table),
        specs=[
            SMEM,
            pl.BlockSpec((tokens, 1), lambda i: (0, 0)),
            pl.BlockSpec((table_step, width), lambda i: (i, 0)),
        ],
        grid=(5,),
        out_specs=[pl.BlockSpec((tokens, block_lanes), lambda i: (0, 0))] * SUB,
        scratch=[pltpu.VMEM((tokens, width), F32)],
        flops=2 * tokens * text_table.shape[0] * width,
        name="text_rows",
    )
    own_sources = lax.dynamic_slice_in_dim(source_column, own_z * group_rows, group_rows, 0)
    stream = call(
        pick_rows_body,
        shape(group_rows, width),
        (own_sources, *patches_full),
        flops=2 * slots * group_rows * width,
        name="pick_rows",
    )

    def attention_output(attended, weights, at, name, beside=()):
        heads = exchange(("gz", "gq"), attended)
        heads, beside = lax.optimization_barrier((heads, beside))
        rows = heads.shape[1]
        return call(
            functools.partial(out_projection_body, at % LANES),
            shape(rows, block_lanes),
            (heads, weights),
            specs=[whole(heads), block_spec(width, LANES, at // LANES)],
            grid=(SUB,),
            out_specs=pl.BlockSpec((rows, block_lanes), lambda z: (0, 0)),
            scratch=[pltpu.VMEM((rows, width), BF16), pltpu.VMEM((SUB, rows, LANES), BF16)],
            flops=2 * rows * width * SUB * LANES,
            name=name,
        ), beside

    def feed_forward(projected, stream, gain, weights, norm, name):
        rows = stream.shape[0]
        own = rows // SUB
        gathered = gather_four("gq", projected)
        hidden_width = vit_fc1.shape[1]
        outs = [shape(own, width)] * (SUB + 1)
        *pieces, mid = call(
            functools.partial(feed_forward_body, norm),
            outs,
            (place, *gathered, stream, gain, weights),
            specs=[SMEM]
            + [whole(g) for g in gathered]
            + [whole(stream), whole(gain), block_spec(width, 2 * hidden_width, 0)],
            grid=(SUB,),
            out_specs=[fixed(o) for o in outs],
            scratch=[
                pltpu.VMEM((SUB, rows, block_lanes), BF16),
                pltpu.VMEM((rows, width), BF16),
                pltpu.VMEM((rows, width), BF16),
                pltpu.VMEM((rows, width), F32),
            ],
            flops=4 * rows * width * SUB * hidden_width,
            name=name,
        )
        return [pieces[0]] + [shift_in("gq", pieces[k], k) for k in range(1, SUB)], mid

    text_parts = [text_blocks[0]] + [shift_in("gq", text_blocks[k], k) for k in (1, 3)]
    projected, (stream, text_parts) = attention_output(
        attended, vit_weights, 768, "vit_output", (stream, text_parts)
    )
    partials, mid = feed_forward(
        projected,
        stream,
        row(vit_norm2),
        vit_weights,
        layer_norm_rows,
        "vit_feed_forward",
    )

    gain_rows = jnp.tile(merge_norm, (share // 4, 1))
    merged = call(merge_norm_body, shape(share, width), (*partials, mid, gain_rows), name="merge_norm")
    gathered = gather_four("gq", merged)
    gathered, last_block = lax.optimization_barrier((gathered, text_blocks[2]))
    text_parts.append(shift_in("gq", last_block, 2))
    group_slots = group_rows // 4
    outs = shape(gx_count, group_slots, block_lanes)
    projected = call(
        merge_projection_body,
        outs,
        (place, *gathered, vit_weights, vit_weights),
        specs=[SMEM]
        + [whole(g) for g in gathered]
        + [block_spec(width, 2 * LANES, 3), block_spec(width, 2 * LANES, 4)],
        grid=(SUB,),
        out_specs=fixed(outs),
        scratch=[
            pltpu.VMEM((group_rows, width), BF16),
            pltpu.VMEM((group_rows, width), BF16),
            pltpu.VMEM((SUB, group_slots, LANES), BF16),
        ],
        flops=2 * group_rows * width * SUB * LANES,
        name="merge_projection",
    )
    all_projected = exchange("gx", projected).reshape(gx_count * group_slots, block_lanes)

    own_index = own_gx * tokens + jnp.arange(tokens, dtype=jnp.int32)
    is_image = jnp.any(positions[None, :] == own_index[:, None], axis=1).astype(F32)
    by_slot = lax.dynamic_index_in_dim(
        positions.reshape(gx_count, SUB, group_slots), own_z, 1, keepdims=False
    )
    placed = call(
        place_body,
        shape(tokens, block_lanes),
        (
            own_index.reshape(tokens, 1),
            is_image.reshape(tokens, 1),
            by_slot.reshape(1, -1),
            all_projected,
            *text_parts,
        ),
        flops=2 * tokens * by_slot.size * block_width,
        name="place_rows",
    )
    own_rows = jnp.sum(
        exchange("gz", placed.reshape(SUB, part, block_lanes)).astype(F32), axis=0
    ).astype(BF16)
    gathered = gather_four("gq", own_rows)

    outs = [shape(SUB, part, 3 * LANES), shape(part, width)]
    triple, embedded = call(
        dec_qkv_body,
        outs,
        (place, *gathered, row(dec_norm1), dec_weights),
        specs=[SMEM]
        + [whole(a) for a in (*gathered, row(dec_norm1))]
        + [block_spec(width, 3 * LANES, 2)],
        grid=(SUB,),
        out_specs=[pl.BlockSpec((1, part, 3 * LANES), lambda z: (z, 0, 0)), fixed(outs[1])],
        scratch=[pltpu.VMEM((SUB, part, block_lanes), BF16), pltpu.VMEM((part, width), BF16)],
        flops=2 * part * width * SUB * 3 * LANES,
        name="dec_qkv",
    )
    triple = exchange("gz", triple).reshape(tokens, 3 * LANES)
    key_values = triple[:, LANES:]
    near = jnp.stack(
        [key_values]
        + [
            lax.ppermute(
                key_values,
                "gx",
                [(2 * y + c, 2 * ((y + k) % SUB) + c) for y in range(SUB) for c in range(2)],
            )
            for k in range(1, SUB)
        ]
    )
    far = lax.ppermute(near, "gx", [(i, i ^ 1) for i in range(gx_count)])
    bounds = jnp.cumsum(lengths)
    all_index = jnp.arange(gx_count * tokens, dtype=jnp.int32).reshape(gx_count, tokens)
    request = jnp.sum((all_index[:, :, None] >= bounds).astype(jnp.int32), axis=2)
    own_request = jnp.sum((own_index[:, None] >= bounds).astype(jnp.int32), axis=1)
    tables = (place, triple, own_request.reshape(tokens, 1), own_index.reshape(tokens, 1), request)
    sums = [shape(tokens, LANES, dtype=F32), shape(tokens, 1, dtype=F32)]
    weighted, denominator = call(
        near_attention_body,
        sums,
        (*tables, near),
        specs=[SMEM] + [VMEM] * 5,
        flops=2 * tokens * tokens * gx_count * LANES,
        name="near_attention",
    )
    attended = call(
        far_attention_body,
        shape(SUB * SUB, part, LANES),
        (*tables, far, weighted, denominator),
        specs=[SMEM] + [VMEM] * 7,
        scratch=[pltpu.VMEM(sums[0].shape, F32), pltpu.VMEM(sums[1].shape, F32)],
        flops=2 * tokens * tokens * gx_count * LANES,
        name="far_attention",
    )
    projected, _ = attention_output(attended, dec_weights, 1032, "dec_output")
    partials, mid = feed_forward(
        projected, embedded, row(dec_norm2), dec_weights, rms_norm_rows, "dec_feed_forward"
    )
    own_tokens = mid.shape[0]

    at_once = 2
    finished = call(
        functools.partial(finish_body, half),
        shape(3, own_tokens, width),
        (*partials, mid, row(next_norm), next_weights),
        specs=[whole(p) for p in (*partials, mid)]
        + [pl.BlockSpec((1, width), lambda z: (0, 0))]
        + [pl.BlockSpec((at_once, width // 2, 6 * HEAD_DIM), lambda z: (z, 0, 0))],
        grid=(SUB * SUB // at_once,),
        out_specs=pl.BlockSpec((3, own_tokens, width), lambda z: (0, 0, 0)),
        scratch=[
            pltpu.VMEM((2 * own_tokens, width // 2), BF16),
            pltpu.VMEM((SUB * SUB, own_tokens, 3 * HEAD_DIM), BF16),
        ],
        flops=2 * own_tokens * width * 3 * width,
        name="finish",
    )
    return finished.transpose(1, 0, 2)


def solution(mesh):
    gx_size = mesh.shape["gx"]
    cut = Mesh(mesh.devices.reshape(gx_size, SUB, SUB), ("gx", "gz", "gq"))
    gy = ("gz", "gq")
    flat = P("gx", gy)
    deep = P("gx", None, gy)
    placed = (
        P(("gx", *gy), None),
        P(),
        P("gx"),
        P(),
        P(),
        P(gy, None),
        P(),
        deep,
        flat,
        P(),
        flat,
        flat,
        P(),
        deep,
        P(),
        deep,
        flat,
        P(),
        flat,
        flat,
        P(),
        deep,
    )
    return jax.shard_map(
        per_device,
        mesh=cut,
        in_specs=placed,
        out_specs=P(("gx", *gy), None, None),
        check_vma=False,
    )
```

```python
import functools
import math

import jax
import jax.numpy as jnp
from jax import lax
from jax.experimental import pallas as pl
from jax.experimental.pallas import tpu as pltpu
from jax.sharding import Mesh, PartitionSpec as P

HEAD_DIM = 88
LANES = 128
SUB = 4
NORM_EPS = 1e-06
F32 = jnp.float32
BF16 = jnp.bfloat16
VMEM_LIMIT = 50 * 1024 * 1024


def merge_sources(grid_rows, merge_slots):
    image_count = grid_rows.shape[0]
    merged_count = grid_rows[:, 0] * grid_rows[:, 1]
    merged_end = jnp.cumsum(merged_count)
    merged_start = merged_end - merged_count
    slot_index = jnp.arange(merge_slots, dtype=jnp.int32)
    image_of = jnp.sum((slot_index[:, None] >= merged_end[None, :]).astype(jnp.int32), axis=1)
    is_live = image_of < image_count
    picked = (
        jnp.minimum(image_of, image_count - 1)[:, None]
        == jnp.arange(image_count, dtype=jnp.int32)[None, :]
    ).astype(jnp.int32)
    col_count = jnp.sum(picked * grid_rows[None, :, 1], axis=1)
    first_slot = jnp.sum(picked * merged_start[None, :], axis=1)
    local_slot = slot_index - first_slot
    grid_row = local_slot // col_count
    grid_col = local_slot % col_count
    base_row = 4 * first_slot + 4 * grid_row * col_count + 2 * grid_col
    offsets = jnp.stack(
        [jnp.zeros_like(col_count), jnp.ones_like(col_count), 2 * col_count, 2 * col_count + 1],
        axis=1,
    )
    sources = jnp.where(is_live[:, None], base_row[:, None] + offsets, 0)
    return sources, image_of, is_live


def shift_in(axis, values, step):
    return lax.ppermute(values, axis, [(i, (i + step) % SUB) for i in range(SUB)])


def gather_four(axis, values):
    return [values] + [shift_in(axis, values, k) for k in range(1, SUB)]


def exchange(axis, pieces):
    return lax.all_to_all(pieces, axis, 0, 0)


def collect(axis, values, size):
    return exchange(axis, jnp.broadcast_to(values, (size,) + values.shape))


SMEM = pl.BlockSpec(memory_space=pltpu.SMEM)
VMEM = pl.BlockSpec(memory_space=pltpu.VMEM)


def shape(*dims, dtype=BF16):
    return jax.ShapeDtypeStruct(dims, dtype)


def call(body, outs, args, specs=None, grid=None, out_specs=None, scratch=(), flops=0, name=None):
    if specs is None:
        specs = [VMEM] * len(args)
    if out_specs is None:
        out_specs = jax.tree.map(lambda _: VMEM, outs)
    moved = sum(math.prod(a.shape) * a.dtype.itemsize for a in args)
    kwargs = {} if grid is None else {"grid": grid}
    return pl.pallas_call(
        body,
        out_shape=outs,
        in_specs=specs,
        out_specs=out_specs,
        scratch_shapes=list(scratch),
        cost_estimate=pl.CostEstimate(
            flops=flops, bytes_accessed=moved if flops else 0, transcendentals=0
        ),
        compiler_params=pltpu.CompilerParams(vmem_limit_bytes=VMEM_LIMIT),
        name=name,
        **kwargs,
    )(*args)


def back(own, step):
    return lax.rem(own + (SUB - step), SUB)


def ahead(own, step):
    return lax.rem(own + step, SUB)


def dot(left, right):
    return jnp.dot(left, right, preferred_element_type=F32)


def layer_norm_rows(values, gain):
    centre = values - jnp.mean(values, axis=-1, keepdims=True)
    spread = jnp.mean(centre * centre, axis=-1, keepdims=True)
    return (centre * lax.rsqrt(spread + NORM_EPS) * gain).astype(BF16)


def rms_norm_rows(values, gain):
    square = jnp.mean(values * values, axis=-1, keepdims=True)
    return (values * lax.rsqrt(square + NORM_EPS) * gain).astype(BF16)


def gelu(values):
    return 0.5 * values * (1.0 + lax.erf(values * (2.0**-0.5)))


def pad_heads(values):
    empty = jnp.zeros((values.shape[0], LANES - HEAD_DIM), values.dtype)
    parts = []
    for t in range(3):
        parts += [values[:, t * HEAD_DIM : (t + 1) * HEAD_DIM], empty]
    return jnp.concatenate(parts, axis=1)


def vit_attention_body(r0, r1, r2, r3, weight, gain, source, query_class, key_class, out, triple, merged):
    slots = triple.shape[0]
    step = slots // SUB
    for i, rows in enumerate((r0, r1, r2, r3)):
        normed = layer_norm_rows(rows[...].astype(F32), gain[...])
        triple[i * step : (i + 1) * step, :] = pad_heads(dot(normed, weight[...]).astype(BF16))

    def reorder(i, _):
        part = pl.ds(pl.multiple_of(i * step, step), step)
        chosen = (
            source[part, :] == lax.broadcasted_iota(jnp.int32, (step, slots), 1)
        ).astype(BF16)
        merged[part, :] = dot(chosen, triple[...]).astype(BF16)
        return 0

    lax.fori_loop(0, SUB, reorder, 0)
    for i in range(SUB):
        at = i * step
        scores = lax.dot_general(
            merged[at : at + step, :LANES],
            merged[:, LANES : 2 * LANES],
            (((1,), (1,)), ((), ())),
            preferred_element_type=F32,
        ) * HEAD_DIM ** (-0.5)
        allowed = query_class[at : at + step, :] == key_class[...]
        exp_scores = jnp.where(allowed, jnp.exp(scores), 0.0)
        denominator = jnp.sum(exp_scores, axis=1, keepdims=True)
        weighted = dot(exp_scores.astype(BF16), merged[:, 2 * LANES :])
        result = (weighted / denominator).astype(BF16)
        for q in range(SUB):
            out[i * SUB + q] = result


def pick_rows_body(source, r0, r1, r2, r3, out):
    rows = r0.shape[0]
    total = None
    for i, ref in enumerate((r0, r1, r2, r3)):
        at = lax.broadcasted_iota(jnp.int32, (source.shape[0], rows), 1) + i * rows
        term = dot((source[...] == at).astype(BF16), ref[...])
        total = term if total is None else total + term
    out[...] = total.astype(BF16)


def join_heads(blocks):
    return jnp.concatenate([block[:, :HEAD_DIM] for block in blocks], axis=1)


def out_projection_body(first, heads, weight, out, left, done):
    step = pl.program_id(0)

    @pl.when(step == 0)
    def _():
        left[...] = join_heads([heads[h] for h in range(SUB * SUB)])

    done[step, :, :HEAD_DIM] = dot(left[...], weight[0])[:, first : first + HEAD_DIM].astype(BF16)

    @pl.when(step == SUB - 1)
    def _():
        out[:, : SUB * HEAD_DIM] = join_heads([done[z] for z in range(SUB)])


def hold_blocks(refs, own_q, held):
    for k, ref in enumerate(refs):
        held[back(own_q, k)] = ref[...]


def in_order(held, rows=slice(None)):
    return jnp.concatenate(
        [
            held[q, rows, z * HEAD_DIM : (z + 1) * HEAD_DIM]
            for z in range(SUB)
            for q in range(SUB)
        ],
        axis=1,
    )


def feed_forward_body(norm, place, o0, o1, o2, o3, stream, gain, fc_in, fc_back, *rest):
    outs, (mid_out, held, mid, normed, total) = rest[:SUB], rest[SUB:]
    own_q = place[2]
    step = pl.program_id(0)
    rows = stream.shape[0]
    share = rows // SUB

    @pl.when(step == 0)
    def _():
        hold_blocks((o0, o1, o2, o3), own_q, held)

        def prepare(i, _):
            part = pl.ds(pl.multiple_of(i * 2 * share, 2 * share), 2 * share)
            added = in_order(held, part).astype(F32)
            summed = (stream[part, :].astype(F32) + added).astype(BF16)
            mid[part, :] = summed
            normed[part, :] = norm(summed.astype(F32), gain[...])
            return 0

        lax.fori_loop(0, SUB // 2, prepare, 0)

    hidden = gelu(dot(normed[...], fc_in[0])).astype(BF16)
    down = lax.dot_general(
        hidden,
        fc_back[0],
        (((1,), (1,)), ((), ())),
        preferred_element_type=F32,
    )

    @pl.when(step == 0)
    def _():
        total[...] = down

    @pl.when(step > 0)
    def _():
        total[...] += down

    @pl.when(step == SUB - 1)
    def _():
        for k in range(SUB):
            start = pl.multiple_of(ahead(own_q, k) * share, share)
            outs[k][...] = total[pl.ds(start, share), :].astype(BF16)
        mid_out[...] = mid[pl.ds(pl.multiple_of(own_q * share, share), share), :]


def summed_stream(partials, mid):
    summed = partials[0][...].astype(F32)
    for ref in partials[1:]:
        summed += ref[...].astype(F32)
    return (mid[...].astype(F32) + summed).astype(BF16).astype(F32)


def merge_norm_body(p0, p1, p2, p3, mid, gain, out):
    rows, width = mid.shape
    final = summed_stream((p0, p1, p2, p3), mid)
    row = lax.broadcasted_iota(jnp.int32, (rows, rows), 0)
    col = lax.broadcasted_iota(jnp.int32, (rows, rows), 1)
    same_group = row // 4 == col // 4

    def group_mean(column):
        across = jnp.sum(jnp.where(same_group, column, 0.0), axis=0, keepdims=True)
        down = jnp.sum(jnp.where(row == col, across, 0.0), axis=1, keepdims=True)
        return down / (4 * width)

    centre = final - group_mean(jnp.sum(final, axis=1, keepdims=True))
    spread = group_mean(jnp.sum(centre * centre, axis=1, keepdims=True))
    out[...] = (centre * lax.rsqrt(spread + NORM_EPS) * gain[...]).astype(BF16)


def merge_projection_body(place, g0, g1, g2, g3, w0, w1, out, rows, left, done):
    own_q = place[2]
    step = pl.program_id(0)
    share = g0.shape[0]
    count = rows.shape[0]
    slots = count // 4

    @pl.when(step == 0)
    def _():
        for k, ref in enumerate((g0, g1, g2, g3)):
            rows[pl.ds(pl.multiple_of(back(own_q, k) * share, share), share), :] = ref[...]
        new_row = lax.broadcasted_iota(jnp.int32, (count, count), 0)
        old_row = lax.broadcasted_iota(jnp.int32, (count, count), 1)
        chosen = ((new_row % slots) * 4 + new_row // slots == old_row).astype(BF16)
        left[...] = dot(chosen, rows[...]).astype(BF16)

    products = jnp.concatenate([dot(left[...], w0[0]), dot(left[...], w1[0])], axis=1)
    total = None
    for patch in range(4):
        at = (patch + 1) * HEAD_DIM
        term = products[patch * slots : (patch + 1) * slots, at : at + HEAD_DIM]
        total = term if total is None else total + term
    done[step, :, :HEAD_DIM] = total.astype(BF16)

    @pl.when(step == SUB - 1)
    def _():
        projected = join_heads([done[z] for z in range(SUB)])
        for g in range(out.shape[0]):
            out[g, :, : SUB * HEAD_DIM] = projected


def text_rows_body(place, ids, table, *rest):
    outs, (total,) = rest[:SUB], rest[SUB:]
    own_q = place[2]
    step = pl.program_id(0)
    last = pl.num_programs(0) - 1
    count = table.shape[0]
    tokens = ids.shape[0]
    share = tokens // SUB
    first = (place[1] * SUB + own_q) * count * pl.num_programs(0) + step * count
    chosen = (ids[...] - first == lax.broadcasted_iota(jnp.int32, (tokens, count), 1)).astype(BF16)
    found = dot(chosen, table[...])

    @pl.when(step == 0)
    def _():
        total[...] = found

    @pl.when(step > 0)
    def _():
        total[...] += found

    @pl.when(step == last)
    def _():
        def hand_out(i, _):
            rows = pl.ds(pl.multiple_of(i * share, share), share)
            for q in range(SUB):
                blocks = [
                    total[rows, at : at + HEAD_DIM]
                    for at in range(q * HEAD_DIM, total.shape[1], SUB * HEAD_DIM)
                ]
                columns = jnp.concatenate(blocks, axis=1).astype(BF16)
                for k in range(SUB):

                    @pl.when(ahead(own_q, k) == q)
                    def _():
                        outs[k][rows, : SUB * HEAD_DIM] = columns

            return 0

        lax.fori_loop(0, SUB, hand_out, 0)


def place_body(seq, is_image, slot_position, projected, t0, t1, t2, t3, out):
    chosen = (seq[...] == slot_position[...]).astype(BF16)
    placed = dot(chosen, projected[...])
    text = t0[...].astype(F32) + t1[...].astype(F32) + t2[...].astype(F32) + t3[...].astype(F32)
    width = SUB * HEAD_DIM
    out[:, :width] = jnp.where(is_image[...] > 0, placed, text)[:, :width].astype(BF16)


def dec_qkv_body(place, g0, g1, g2, g3, gain, weight, out, embedded_out, held, normed):
    @pl.when(pl.program_id(0) == 0)
    def _():
        hold_blocks((g0, g1, g2, g3), place[2], held)
        embedded = in_order(held)
        embedded_out[...] = embedded
        normed[...] = rms_norm_rows(embedded.astype(F32), gain[...])

    out[0] = pad_heads(dot(normed[...], weight[0])[:, : 3 * HEAD_DIM].astype(BF16))


def attend_blocks(own_gx, core, triple, query_request, query_position, request, blocks, weighted, denominator):
    tokens = triple.shape[0]
    part = tokens // 2

    def attend(k, _):
        owner = 2 * lax.rem(lax.div(own_gx, 2) + (SUB - k), SUB) + core

        @pl.when(owner <= own_gx)
        def _():
            key_request = request[pl.ds(owner, 1), :]
            key_position = lax.broadcasted_iota(jnp.int32, (1, tokens), 1) + owner * tokens
            for at in range(0, tokens, part):
                rows = slice(at, at + part)
                scores = lax.dot_general(
                    triple[rows, :LANES],
                    blocks[k, :, :LANES],
                    (((1,), (1,)), ((), ())),
                    preferred_element_type=F32,
                ) * HEAD_DIM ** (-0.5)
                allowed = (key_request == query_request[rows, :]) & (
                    key_position <= query_position[rows, :]
                )
                exp_scores = jnp.where(allowed, jnp.exp(scores), 0.0)
                denominator[rows, :] += jnp.sum(exp_scores, axis=1, keepdims=True)
                weighted[rows, :] += dot(exp_scores.astype(BF16), blocks[k, :, LANES:])

        return 0

    lax.fori_loop(0, SUB, attend, 0)


def near_attention_body(place, triple, query_request, query_position, request, near, weighted, denominator):
    weighted[...] = jnp.zeros_like(weighted)
    denominator[...] = jnp.zeros_like(denominator)
    attend_blocks(
        place[0], lax.rem(place[0], 2), triple, query_request, query_position, request, near, weighted, denominator
    )


def far_attention_body(
    place, triple, query_request, query_position, request, far, near_weighted, near_denominator, out, weighted, denominator
):
    weighted[...] = near_weighted[...]
    denominator[...] = near_denominator[...]
    attend_blocks(
        place[0], lax.rem(place[0] + 1, 2), triple, query_request, query_position, request, far, weighted, denominator
    )
    share = triple.shape[0] // SUB
    for z in range(SUB):
        rows = slice(z * share, (z + 1) * share)
        result = (weighted[rows, :] / denominator[rows, :]).astype(BF16)
        for q in range(SUB):
            out[z * SUB + q] = result


def finish_body(half, p0, p1, p2, p3, mid, gain, w0, w1, w2, w3, out, normed, done):
    step = pl.program_id(0)
    weights = (w0, w1, w2, w3)
    count = len(weights)
    tokens = mid.shape[0]

    @pl.when(step == 0)
    def _():
        rows = rms_norm_rows(summed_stream((p0, p1, p2, p3), mid), gain[...])
        for side in range(2):
            starts = range(side * half, rows.shape[1], 2 * half)
            normed[side * tokens : (side + 1) * tokens, :] = jnp.concatenate(
                [rows[:, at : at + half] for at in starts], axis=1
            )

    for i, weight in enumerate(weights):
        both = dot(normed[...], weight[0])
        used = both.shape[1] // 2
        done[step * count + i] = (both[:tokens, :used] + both[tokens:, used:]).astype(BF16)

    @pl.when(step == pl.num_programs(0) - 1)
    def _():
        for t in range(3):
            out[t] = jnp.concatenate(
                [
                    done[h, :, t * HEAD_DIM : (t + 1) * HEAD_DIM]
                    for h in range(done.shape[0])
                ],
                axis=1,
            )


def block_spec(rows, width, at):
    return pl.BlockSpec((1, rows, width), lambda z: (z, 0, at))


def whole(values):
    rank = values.ndim
    return pl.BlockSpec(values.shape, lambda z: (0,) * rank)


def fixed(struct):
    rank = len(struct.shape)
    return pl.BlockSpec(struct.shape, lambda z: (0,) * rank)


def per_device(
    patches,
    grids,
    text_ids,
    positions,
    lengths,
    text_table,
    vit_norm1,
    vit_qkv,
    vit_out,
    vit_norm2,
    vit_fc1,
    vit_fc2,
    merge_norm,
    merge_proj,
    dec_norm1,
    dec_qkv,
    dec_out,
    dec_norm2,
    dec_fc1,
    dec_fc2,
    next_norm,
    next_qkv,
):
    gx_count = lax.axis_size("gx")
    own_gx, own_z, own_q = lax.axis_index("gx"), lax.axis_index("gz"), lax.axis_index("gq")
    place = jnp.stack([own_gx, own_z, own_q]).astype(jnp.int32)
    width = patches.shape[1]
    share = patches.shape[0]
    slots = share * SUB * SUB

    def join_weights(parts, lanes):
        columns = []
        for p in parts:
            columns += [p] if p.ndim == 2 else [p[:, t] for t in range(p.shape[1])]
        used = sum(c.shape[1] for c in columns)
        columns.append(jnp.zeros((columns[0].shape[0], lanes - used), BF16))
        return jnp.concatenate([c for c in columns if c.shape[1]], axis=1)

    def gather_weights(local):
        full = lax.all_gather(local, ("gz", "gx"), axis=0, tiled=True)
        return full.reshape(SUB, width, local.shape[1])

    vit_weights = gather_weights(join_weights([vit_fc1, vit_fc2, vit_out, merge_proj], 1280))

    per_group = grids.shape[0] // gx_count
    own_grids = lax.dynamic_slice_in_dim(grids, own_gx * per_group, per_group, 0)
    merge_slots = positions.shape[0] // gx_count
    sources, image_of, is_live = merge_sources(own_grids, merge_slots)
    holder = sources // share
    block = lax.rem(own_q + SUB - lax.rem(holder, SUB), SUB) * SUB + lax.rem(
        own_z + SUB - holder // SUB, SUB
    )
    source_column = (block * share + lax.rem(sources, share)).reshape(slots, 1)
    query_class = jnp.repeat(jnp.where(is_live, image_of, 0), 4).reshape(slots, 1)
    key_class = jnp.repeat(image_of, 4).reshape(1, slots)

    of_column = jnp.stack(gather_four("gz", patches))
    dec_local = join_weights([dec_fc1, dec_fc2, dec_qkv, dec_out], 1152)
    half = next_qkv.shape[0] // 2
    next_local = join_weights([next_qkv[:half], next_qkv[half:]], 6 * HEAD_DIM)
    of_column, dec_local, next_local, source_column, query_class, key_class, qkv_parts = (
        lax.optimization_barrier(
            (of_column, dec_local, next_local, source_column, query_class, key_class, vit_qkv)
        )
    )
    patches_full = [
        rows.reshape(SUB * share, width) for rows in gather_four("gq", of_column)
    ]
    dec_weights = gather_weights(dec_local)
    own_qkv = jnp.concatenate([qkv_parts[:, t] for t in range(3)], axis=1)
    qkv_weight = lax.all_gather(own_qkv, "gx", axis=0, tiled=True)

    row = lambda gain: gain.reshape(1, -1)
    group_rows = slots // SUB
    attended = call(
        vit_attention_body,
        shape(SUB * SUB, group_rows, LANES),
        (*patches_full, qkv_weight, row(vit_norm1), source_column, query_class, key_class),
        scratch=[
            pltpu.VMEM((slots, 3 * LANES), BF16),
            pltpu.VMEM((slots, 3 * LANES), BF16),
        ],
        flops=2 * slots * (width * 3 * LANES + slots * 5 * LANES),
        name="vit_attention",
    )
    attended, ids, next_local = lax.optimization_barrier((attended, text_ids, next_local))
    next_weights = lax.all_gather(next_local, ("gz", "gq", "gx"), axis=0, tiled=True).reshape(
        SUB * SUB, width // 2, 6 * HEAD_DIM
    )

    tokens = text_ids.shape[0]
    part = tokens // SUB
    block_width = SUB * HEAD_DIM
    block_lanes = 3 * LANES
    table_step = text_table.shape[0] // 5
    text_blocks = call(
        text_rows_body,
        [shape(tokens, block_lanes)] * SUB,
        (place, ids.reshape(tokens, 1), text_table),
        specs=[
            SMEM,
            pl.BlockSpec((tokens, 1), lambda i: (0, 0)),
            pl.BlockSpec((table_step, width), lambda i: (i, 0)),
        ],
        grid=(5,),
        out_specs=[pl.BlockSpec((tokens, block_lanes), lambda i: (0, 0))] * SUB,
        scratch=[pltpu.VMEM((tokens, width), F32)],
        flops=2 * tokens * text_table.shape[0] * width,
        name="text_rows",
    )
    own_sources = lax.dynamic_slice_in_dim(source_column, own_z * group_rows, group_rows, 0)
    stream = call(
        pick_rows_body,
        shape(group_rows, width),
        (own_sources, *patches_full),
        flops=2 * slots * group_rows * width,
        name="pick_rows",
    )

    def attention_output(attended, weights, at, name, beside=()):
        heads = exchange(("gz", "gq"), attended)
        heads, beside = lax.optimization_barrier((heads, beside))
        rows = heads.shape[1]
        return call(
            functools.partial(out_projection_body, at % LANES),
            shape(rows, block_lanes),
            (heads, weights),
            specs=[whole(heads), block_spec(width, LANES, at // LANES)],
            grid=(SUB,),
            out_specs=pl.BlockSpec((rows, block_lanes), lambda z: (0, 0)),
            scratch=[pltpu.VMEM((rows, width), BF16), pltpu.VMEM((SUB, rows, LANES), BF16)],
            flops=2 * rows * width * SUB * LANES,
            name=name,
        ), beside

    def feed_forward(projected, stream, gain, weights, norm, name):
        rows = stream.shape[0]
        own = rows // SUB
        gathered = gather_four("gq", projected)
        hidden_width = vit_fc1.shape[1]
        outs = [shape(own, width)] * (SUB + 1)
        *pieces, mid = call(
            functools.partial(feed_forward_body, norm),
            outs,
            (place, *gathered, stream, gain, weights, weights),
            specs=[SMEM]
            + [whole(g) for g in gathered]
            + [whole(stream), whole(gain)]
            + [block_spec(width, hidden_width, at) for at in (0, 1)],
            grid=(SUB,),
            out_specs=[fixed(o) for o in outs],
            scratch=[
                pltpu.VMEM((SUB, rows, block_lanes), BF16),
                pltpu.VMEM((rows, width), BF16),
                pltpu.VMEM((rows, width), BF16),
                pltpu.VMEM((rows, width), F32),
            ],
            flops=4 * rows * width * SUB * hidden_width,
            name=name,
        )
        return [pieces[0]] + [shift_in("gq", pieces[k], k) for k in range(1, SUB)], mid

    text_parts = [text_blocks[0]] + [shift_in("gq", text_blocks[k], k) for k in (1, 3)]
    projected, (stream, text_parts) = attention_output(
        attended, vit_weights, 768, "vit_output", (stream, text_parts)
    )
    partials, mid = feed_forward(
        projected,
        stream,
        row(vit_norm2),
        vit_weights,
        layer_norm_rows,
        "vit_feed_forward",
    )

    gain_rows = jnp.tile(merge_norm, (share // 4, 1))
    merged = call(merge_norm_body, shape(share, width), (*partials, mid, gain_rows), name="merge_norm")
    gathered = gather_four("gq", merged)
    gathered, last_block = lax.optimization_barrier((gathered, text_blocks[2]))
    text_parts.append(shift_in("gq", last_block, 2))
    group_slots = group_rows // 4
    outs = shape(gx_count, group_slots, block_lanes)
    projected = call(
        merge_projection_body,
        outs,
        (place, *gathered, vit_weights, vit_weights),
        specs=[SMEM]
        + [whole(g) for g in gathered]
        + [block_spec(width, 2 * LANES, 3), block_spec(width, 2 * LANES, 4)],
        grid=(SUB,),
        out_specs=fixed(outs),
        scratch=[
            pltpu.VMEM((group_rows, width), BF16),
            pltpu.VMEM((group_rows, width), BF16),
            pltpu.VMEM((SUB, group_slots, LANES), BF16),
        ],
        flops=2 * group_rows * width * SUB * LANES,
        name="merge_projection",
    )
    all_projected = exchange("gx", projected).reshape(gx_count * group_slots, block_lanes)

    own_index = own_gx * tokens + jnp.arange(tokens, dtype=jnp.int32)
    is_image = jnp.any(positions[None, :] == own_index[:, None], axis=1).astype(F32)
    by_slot = lax.dynamic_index_in_dim(
        positions.reshape(gx_count, SUB, group_slots), own_z, 1, keepdims=False
    )
    placed = call(
        place_body,
        shape(tokens, block_lanes),
        (
            own_index.reshape(tokens, 1),
            is_image.reshape(tokens, 1),
            by_slot.reshape(1, -1),
            all_projected,
            *text_parts,
        ),
        flops=2 * tokens * by_slot.size * block_width,
        name="place_rows",
    )
    own_rows = jnp.sum(
        exchange("gz", placed.reshape(SUB, part, block_lanes)).astype(F32), axis=0
    ).astype(BF16)
    gathered = gather_four("gq", own_rows)

    outs = [shape(SUB, part, 3 * LANES), shape(part, width)]
    triple, embedded = call(
        dec_qkv_body,
        outs,
        (place, *gathered, row(dec_norm1), dec_weights),
        specs=[SMEM]
        + [whole(a) for a in (*gathered, row(dec_norm1))]
        + [block_spec(width, 3 * LANES, 2)],
        grid=(SUB,),
        out_specs=[pl.BlockSpec((1, part, 3 * LANES), lambda z: (z, 0, 0)), fixed(outs[1])],
        scratch=[pltpu.VMEM((SUB, part, block_lanes), BF16), pltpu.VMEM((part, width), BF16)],
        flops=2 * part * width * SUB * 3 * LANES,
        name="dec_qkv",
    )
    triple = exchange("gz", triple).reshape(tokens, 3 * LANES)
    key_values = triple[:, LANES:]
    near = jnp.stack(
        [key_values]
        + [
            lax.ppermute(
                key_values,
                "gx",
                [(2 * y + c, 2 * ((y + k) % SUB) + c) for y in range(SUB) for c in range(2)],
            )
            for k in range(1, SUB)
        ]
    )
    far = lax.ppermute(near, "gx", [(i, i ^ 1) for i in range(gx_count)])
    bounds = jnp.cumsum(lengths)
    all_index = jnp.arange(gx_count * tokens, dtype=jnp.int32).reshape(gx_count, tokens)
    request = jnp.sum((all_index[:, :, None] >= bounds).astype(jnp.int32), axis=2)
    own_request = jnp.sum((own_index[:, None] >= bounds).astype(jnp.int32), axis=1)
    tables = (place, triple, own_request.reshape(tokens, 1), own_index.reshape(tokens, 1), request)
    sums = [shape(tokens, LANES, dtype=F32), shape(tokens, 1, dtype=F32)]
    weighted, denominator = call(
        near_attention_body,
        sums,
        (*tables, near),
        specs=[SMEM] + [VMEM] * 5,
        flops=2 * tokens * tokens * gx_count * LANES,
        name="near_attention",
    )
    attended = call(
        far_attention_body,
        shape(SUB * SUB, part, LANES),
        (*tables, far, weighted, denominator),
        specs=[SMEM] + [VMEM] * 7,
        scratch=[pltpu.VMEM(sums[0].shape, F32), pltpu.VMEM(sums[1].shape, F32)],
        flops=2 * tokens * tokens * gx_count * LANES,
        name="far_attention",
    )
    projected, _ = attention_output(attended, dec_weights, 1032, "dec_output")
    partials, mid = feed_forward(
        projected, embedded, row(dec_norm2), dec_weights, rms_norm_rows, "dec_feed_forward"
    )
    own_tokens = mid.shape[0]

    at_once = 4
    finished = call(
        functools.partial(finish_body, half),
        shape(3, own_tokens, width),
        (*partials, mid, row(next_norm), *[next_weights] * at_once),
        specs=[whole(p) for p in (*partials, mid)]
        + [pl.BlockSpec((1, width), lambda z: (0, 0))]
        + [
            pl.BlockSpec(
                (1, width // 2, 6 * HEAD_DIM), functools.partial(lambda i, z: (at_once * z + i, 0, 0), i)
            )
            for i in range(at_once)
        ],
        grid=(SUB * SUB // at_once,),
        out_specs=pl.BlockSpec((3, own_tokens, width), lambda z: (0, 0, 0)),
        scratch=[
            pltpu.VMEM((2 * own_tokens, width // 2), BF16),
            pltpu.VMEM((SUB * SUB, own_tokens, 3 * HEAD_DIM), BF16),
        ],
        flops=2 * own_tokens * width * 3 * width,
        name="finish",
    )
    return finished.transpose(1, 0, 2)


def solution(mesh):
    gx_size = mesh.shape["gx"]
    cut = Mesh(mesh.devices.reshape(gx_size, SUB, SUB), ("gx", "gz", "gq"))
    gy = ("gz", "gq")
    flat = P("gx", gy)
    deep = P("gx", None, gy)
    placed = (
        P(("gx", *gy), None),
        P(),
        P("gx"),
        P(),
        P(),
        P(gy, None),
        P(),
        deep,
        flat,
        P(),
        flat,
        flat,
        P(),
        deep,
        P(),
        deep,
        flat,
        P(),
        flat,
        flat,
        P(),
        deep,
    )
    return jax.shard_map(
        per_device,
        mesh=cut,
        in_specs=placed,
        out_specs=P(("gx", *gy), None, None),
        check_vma=False,
    )
```

```python
import functools
import math

import jax
import jax.numpy as jnp
from jax import lax
from jax.experimental import pallas as pl
from jax.experimental.pallas import tpu as pltpu
from jax.sharding import Mesh, PartitionSpec as P

HEAD_DIM = 88
LANES = 128
SUB = 4
NORM_EPS = 1e-06
F32 = jnp.float32
BF16 = jnp.bfloat16
VMEM_LIMIT = 50 * 1024 * 1024


def merge_sources(grid_rows, merge_slots):
    image_count = grid_rows.shape[0]
    merged_count = grid_rows[:, 0] * grid_rows[:, 1]
    merged_end = jnp.cumsum(merged_count)
    merged_start = merged_end - merged_count
    slot_index = jnp.arange(merge_slots, dtype=jnp.int32)
    image_of = jnp.sum((slot_index[:, None] >= merged_end[None, :]).astype(jnp.int32), axis=1)
    is_live = image_of < image_count
    picked = (
        jnp.minimum(image_of, image_count - 1)[:, None]
        == jnp.arange(image_count, dtype=jnp.int32)[None, :]
    ).astype(jnp.int32)
    col_count = jnp.sum(picked * grid_rows[None, :, 1], axis=1)
    first_slot = jnp.sum(picked * merged_start[None, :], axis=1)
    local_slot = slot_index - first_slot
    grid_row = local_slot // col_count
    grid_col = local_slot % col_count
    base_row = 4 * first_slot + 4 * grid_row * col_count + 2 * grid_col
    offsets = jnp.stack(
        [jnp.zeros_like(col_count), jnp.ones_like(col_count), 2 * col_count, 2 * col_count + 1],
        axis=1,
    )
    sources = jnp.where(is_live[:, None], base_row[:, None] + offsets, 0)
    return sources, image_of, is_live


def shift_in(axis, values, step):
    return lax.ppermute(values, axis, [(i, (i + step) % SUB) for i in range(SUB)])


def gather_four(axis, values):
    return [values] + [shift_in(axis, values, k) for k in range(1, SUB)]


def exchange(axis, pieces):
    return lax.all_to_all(pieces, axis, 0, 0)


def collect(axis, values, size):
    return exchange(axis, jnp.broadcast_to(values, (size,) + values.shape))


SMEM = pl.BlockSpec(memory_space=pltpu.SMEM)
VMEM = pl.BlockSpec(memory_space=pltpu.VMEM)


def shape(*dims, dtype=BF16):
    return jax.ShapeDtypeStruct(dims, dtype)


def call(body, outs, args, specs=None, grid=None, out_specs=None, scratch=(), flops=0, name=None):
    if specs is None:
        specs = [VMEM] * len(args)
    if out_specs is None:
        out_specs = jax.tree.map(lambda _: VMEM, outs)
    moved = sum(math.prod(a.shape) * a.dtype.itemsize for a in args)
    kwargs = {} if grid is None else {"grid": grid}
    return pl.pallas_call(
        body,
        out_shape=outs,
        in_specs=specs,
        out_specs=out_specs,
        scratch_shapes=list(scratch),
        cost_estimate=pl.CostEstimate(
            flops=flops, bytes_accessed=moved if flops else 0, transcendentals=0
        ),
        compiler_params=pltpu.CompilerParams(vmem_limit_bytes=VMEM_LIMIT),
        name=name,
        **kwargs,
    )(*args)


def back(own, step):
    return lax.rem(own + (SUB - step), SUB)


def ahead(own, step):
    return lax.rem(own + step, SUB)


def dot(left, right):
    return jnp.dot(left, right, preferred_element_type=F32)


def layer_norm_rows(values, gain):
    centre = values - jnp.mean(values, axis=-1, keepdims=True)
    spread = jnp.mean(centre * centre, axis=-1, keepdims=True)
    return (centre * lax.rsqrt(spread + NORM_EPS) * gain).astype(BF16)


def rms_norm_rows(values, gain):
    square = jnp.mean(values * values, axis=-1, keepdims=True)
    return (values * lax.rsqrt(square + NORM_EPS) * gain).astype(BF16)


def gelu(values):
    return 0.5 * values * (1.0 + lax.erf(values * (2.0**-0.5)))


def pad_heads(values):
    empty = jnp.zeros((values.shape[0], LANES - HEAD_DIM), values.dtype)
    parts = []
    for t in range(3):
        parts += [values[:, t * HEAD_DIM : (t + 1) * HEAD_DIM], empty]
    return jnp.concatenate(parts, axis=1)


def vit_attention_body(r0, r1, r2, r3, weight, gain, source, query_class, key_class, out, triple, merged):
    slots = triple.shape[0]
    step = slots // SUB
    for i, rows in enumerate((r0, r1, r2, r3)):
        normed = layer_norm_rows(rows[...].astype(F32), gain[...])
        triple[i * step : (i + 1) * step, :] = pad_heads(dot(normed, weight[...]).astype(BF16))

    def reorder(i, _):
        part = pl.ds(pl.multiple_of(i * step, step), step)
        chosen = (
            source[part, :] == lax.broadcasted_iota(jnp.int32, (step, slots), 1)
        ).astype(BF16)
        merged[part, :] = dot(chosen, triple[...]).astype(BF16)
        return 0

    lax.fori_loop(0, SUB, reorder, 0)
    for i in range(SUB):
        at = i * step
        scores = lax.dot_general(
            merged[at : at + step, :LANES],
            merged[:, LANES : 2 * LANES],
            (((1,), (1,)), ((), ())),
            preferred_element_type=F32,
        ) * HEAD_DIM ** (-0.5)
        allowed = query_class[at : at + step, :] == key_class[...]
        exp_scores = jnp.where(allowed, jnp.exp(scores), 0.0)
        denominator = jnp.sum(exp_scores, axis=1, keepdims=True)
        weighted = dot(exp_scores.astype(BF16), merged[:, 2 * LANES :])
        result = (weighted / denominator).astype(BF16)
        for q in range(SUB):
            out[i * SUB + q] = result


def pick_rows_body(source, r0, r1, r2, r3, out):
    rows = r0.shape[0]
    total = None
    for i, ref in enumerate((r0, r1, r2, r3)):
        at = lax.broadcasted_iota(jnp.int32, (source.shape[0], rows), 1) + i * rows
        term = dot((source[...] == at).astype(BF16), ref[...])
        total = term if total is None else total + term
    out[...] = total.astype(BF16)


def join_heads(blocks):
    return jnp.concatenate([block[:, :HEAD_DIM] for block in blocks], axis=1)


def out_projection_body(first, heads, w0, w1, w2, w3, out):
    left = join_heads([heads[h] for h in range(SUB * SUB)])
    done = [
        dot(left, weight[0])[:, first : first + HEAD_DIM].astype(BF16) for weight in (w0, w1, w2, w3)
    ]
    out[:, : SUB * HEAD_DIM] = jnp.concatenate(done, axis=1)


def hold_blocks(refs, own_q, held):
    for k, ref in enumerate(refs):
        held[back(own_q, k)] = ref[...]


def in_order(held, rows=slice(None)):
    return jnp.concatenate(
        [
            held[q, rows, z * HEAD_DIM : (z + 1) * HEAD_DIM]
            for z in range(SUB)
            for q in range(SUB)
        ],
        axis=1,
    )


def feed_forward_body(norm, place, o0, o1, o2, o3, stream, gain, fc_in, fc_back, *rest):
    outs, (mid_out, held, mid, normed, total) = rest[:SUB], rest[SUB:]
    own_q = place[2]
    step = pl.program_id(0)
    rows = stream.shape[0]
    share = rows // SUB

    @pl.when(step == 0)
    def _():
        hold_blocks((o0, o1, o2, o3), own_q, held)

        def prepare(i, _):
            part = pl.ds(pl.multiple_of(i * 2 * share, 2 * share), 2 * share)
            added = in_order(held, part).astype(F32)
            summed = (stream[part, :].astype(F32) + added).astype(BF16)
            mid[part, :] = summed
            normed[part, :] = norm(summed.astype(F32), gain[...])
            return 0

        lax.fori_loop(0, SUB // 2, prepare, 0)

    hidden = gelu(dot(normed[...], fc_in[0])).astype(BF16)
    down = lax.dot_general(
        hidden,
        fc_back[0],
        (((1,), (1,)), ((), ())),
        preferred_element_type=F32,
    )

    @pl.when(step == 0)
    def _():
        total[...] = down

    @pl.when(step > 0)
    def _():
        total[...] += down

    @pl.when(step == SUB - 1)
    def _():
        for k in range(SUB):
            start = pl.multiple_of(ahead(own_q, k) * share, share)
            outs[k][...] = total[pl.ds(start, share), :].astype(BF16)
        mid_out[...] = mid[pl.ds(pl.multiple_of(own_q * share, share), share), :]


def summed_stream(partials, mid):
    summed = partials[0][...].astype(F32)
    for ref in partials[1:]:
        summed += ref[...].astype(F32)
    return (mid[...].astype(F32) + summed).astype(BF16).astype(F32)


def merge_norm_body(p0, p1, p2, p3, mid, gain, out):
    rows, width = mid.shape
    final = summed_stream((p0, p1, p2, p3), mid)
    row = lax.broadcasted_iota(jnp.int32, (rows, rows), 0)
    col = lax.broadcasted_iota(jnp.int32, (rows, rows), 1)
    same_group = row // 4 == col // 4

    def group_mean(column):
        across = jnp.sum(jnp.where(same_group, column, 0.0), axis=0, keepdims=True)
        down = jnp.sum(jnp.where(row == col, across, 0.0), axis=1, keepdims=True)
        return down / (4 * width)

    centre = final - group_mean(jnp.sum(final, axis=1, keepdims=True))
    spread = group_mean(jnp.sum(centre * centre, axis=1, keepdims=True))
    out[...] = (centre * lax.rsqrt(spread + NORM_EPS) * gain[...]).astype(BF16)


def merge_projection_body(place, g0, g1, g2, g3, w0, w1, out, rows, left, done):
    own_q = place[2]
    step = pl.program_id(0)
    share = g0.shape[0]
    count = rows.shape[0]
    slots = count // 4

    @pl.when(step == 0)
    def _():
        for k, ref in enumerate((g0, g1, g2, g3)):
            rows[pl.ds(pl.multiple_of(back(own_q, k) * share, share), share), :] = ref[...]
        new_row = lax.broadcasted_iota(jnp.int32, (count, count), 0)
        old_row = lax.broadcasted_iota(jnp.int32, (count, count), 1)
        chosen = ((new_row % slots) * 4 + new_row // slots == old_row).astype(BF16)
        left[...] = dot(chosen, rows[...]).astype(BF16)

    products = jnp.concatenate([dot(left[...], w0[0]), dot(left[...], w1[0])], axis=1)
    total = None
    for patch in range(4):
        at = (patch + 1) * HEAD_DIM
        term = products[patch * slots : (patch + 1) * slots, at : at + HEAD_DIM]
        total = term if total is None else total + term
    done[step, :, :HEAD_DIM] = total.astype(BF16)

    @pl.when(step == SUB - 1)
    def _():
        projected = join_heads([done[z] for z in range(SUB)])
        for g in range(out.shape[0]):
            out[g, :, : SUB * HEAD_DIM] = projected


def text_rows_body(place, ids, table, *rest):
    outs, (total,) = rest[:SUB], rest[SUB:]
    own_q = place[2]
    step = pl.program_id(0)
    last = pl.num_programs(0) - 1
    count = table.shape[0]
    tokens = ids.shape[0]
    share = tokens // SUB
    first = (place[1] * SUB + own_q) * count * pl.num_programs(0) + step * count
    chosen = (ids[...] - first == lax.broadcasted_iota(jnp.int32, (tokens, count), 1)).astype(BF16)
    found = dot(chosen, table[...])

    @pl.when(step == 0)
    def _():
        total[...] = found

    @pl.when(step > 0)
    def _():
        total[...] += found

    @pl.when(step == last)
    def _():
        def hand_out(i, _):
            rows = pl.ds(pl.multiple_of(i * share, share), share)
            for q in range(SUB):
                blocks = [
                    total[rows, at : at + HEAD_DIM]
                    for at in range(q * HEAD_DIM, total.shape[1], SUB * HEAD_DIM)
                ]
                columns = jnp.concatenate(blocks, axis=1).astype(BF16)
                for k in range(SUB):

                    @pl.when(ahead(own_q, k) == q)
                    def _():
                        outs[k][rows, : SUB * HEAD_DIM] = columns

            return 0

        lax.fori_loop(0, SUB, hand_out, 0)


def place_body(seq, is_image, slot_position, projected, t0, t1, t2, t3, out):
    chosen = (seq[...] == slot_position[...]).astype(BF16)
    placed = dot(chosen, projected[...])
    text = t0[...].astype(F32) + t1[...].astype(F32) + t2[...].astype(F32) + t3[...].astype(F32)
    width = SUB * HEAD_DIM
    out[:, :width] = jnp.where(is_image[...] > 0, placed, text)[:, :width].astype(BF16)


def dec_qkv_body(place, g0, g1, g2, g3, gain, weight, out, embedded_out, held, normed):
    @pl.when(pl.program_id(0) == 0)
    def _():
        hold_blocks((g0, g1, g2, g3), place[2], held)
        embedded = in_order(held)
        embedded_out[...] = embedded
        normed[...] = rms_norm_rows(embedded.astype(F32), gain[...])

    out[0] = pad_heads(dot(normed[...], weight[0])[:, : 3 * HEAD_DIM].astype(BF16))


def attend_blocks(own_gx, core, triple, query_request, query_position, request, blocks, weighted, denominator):
    tokens = triple.shape[0]
    part = tokens // 2

    def attend(k, _):
        owner = 2 * lax.rem(lax.div(own_gx, 2) + (SUB - k), SUB) + core

        @pl.when(owner <= own_gx)
        def _():
            key_request = request[pl.ds(owner, 1), :]
            key_position = lax.broadcasted_iota(jnp.int32, (1, tokens), 1) + owner * tokens
            for at in range(0, tokens, part):
                rows = slice(at, at + part)
                scores = lax.dot_general(
                    triple[rows, :LANES],
                    blocks[k, :, :LANES],
                    (((1,), (1,)), ((), ())),
                    preferred_element_type=F32,
                ) * HEAD_DIM ** (-0.5)
                allowed = (key_request == query_request[rows, :]) & (
                    key_position <= query_position[rows, :]
                )
                exp_scores = jnp.where(allowed, jnp.exp(scores), 0.0)
                denominator[rows, :] += jnp.sum(exp_scores, axis=1, keepdims=True)
                weighted[rows, :] += dot(exp_scores.astype(BF16), blocks[k, :, LANES:])

        return 0

    lax.fori_loop(0, SUB, attend, 0)


def near_attention_body(place, triple, query_request, query_position, request, near, weighted, denominator):
    weighted[...] = jnp.zeros_like(weighted)
    denominator[...] = jnp.zeros_like(denominator)
    attend_blocks(
        place[0], lax.rem(place[0], 2), triple, query_request, query_position, request, near, weighted, denominator
    )


def far_attention_body(
    place, triple, query_request, query_position, request, far, near_weighted, near_denominator, out, weighted, denominator
):
    weighted[...] = near_weighted[...]
    denominator[...] = near_denominator[...]
    attend_blocks(
        place[0], lax.rem(place[0] + 1, 2), triple, query_request, query_position, request, far, weighted, denominator
    )
    share = triple.shape[0] // SUB
    for z in range(SUB):
        rows = slice(z * share, (z + 1) * share)
        result = (weighted[rows, :] / denominator[rows, :]).astype(BF16)
        for q in range(SUB):
            out[z * SUB + q] = result


def finish_body(half, p0, p1, p2, p3, mid, gain, w0, w1, w2, w3, out, normed, done):
    step = pl.program_id(0)
    weights = (w0, w1, w2, w3)
    count = len(weights)
    tokens = mid.shape[0]

    @pl.when(step == 0)
    def _():
        rows = rms_norm_rows(summed_stream((p0, p1, p2, p3), mid), gain[...])
        for side in range(2):
            starts = range(side * half, rows.shape[1], 2 * half)
            normed[side * tokens : (side + 1) * tokens, :] = jnp.concatenate(
                [rows[:, at : at + half] for at in starts], axis=1
            )

    for i, weight in enumerate(weights):
        both = dot(normed[...], weight[0])
        used = both.shape[1] // 2
        done[step * count + i] = (both[:tokens, :used] + both[tokens:, used:]).astype(BF16)

    @pl.when(step == pl.num_programs(0) - 1)
    def _():
        for t in range(3):
            out[t] = jnp.concatenate(
                [
                    done[h, :, t * HEAD_DIM : (t + 1) * HEAD_DIM]
                    for h in range(done.shape[0])
                ],
                axis=1,
            )


def block_spec(rows, width, at):
    return pl.BlockSpec((1, rows, width), lambda z: (z, 0, at))


def whole(values):
    rank = values.ndim
    return pl.BlockSpec(values.shape, lambda z: (0,) * rank)


def fixed(struct):
    rank = len(struct.shape)
    return pl.BlockSpec(struct.shape, lambda z: (0,) * rank)


def per_device(
    patches,
    grids,
    text_ids,
    positions,
    lengths,
    text_table,
    vit_norm1,
    vit_qkv,
    vit_out,
    vit_norm2,
    vit_fc1,
    vit_fc2,
    merge_norm,
    merge_proj,
    dec_norm1,
    dec_qkv,
    dec_out,
    dec_norm2,
    dec_fc1,
    dec_fc2,
    next_norm,
    next_qkv,
):
    gx_count = lax.axis_size("gx")
    own_gx, own_z, own_q = lax.axis_index("gx"), lax.axis_index("gz"), lax.axis_index("gq")
    place = jnp.stack([own_gx, own_z, own_q]).astype(jnp.int32)
    width = patches.shape[1]
    share = patches.shape[0]
    slots = share * SUB * SUB

    def join_weights(parts, lanes):
        columns = []
        for p in parts:
            columns += [p] if p.ndim == 2 else [p[:, t] for t in range(p.shape[1])]
        used = sum(c.shape[1] for c in columns)
        columns.append(jnp.zeros((columns[0].shape[0], lanes - used), BF16))
        return jnp.concatenate([c for c in columns if c.shape[1]], axis=1)

    def gather_weights(local):
        full = lax.all_gather(local, ("gz", "gx"), axis=0, tiled=True)
        return full.reshape(SUB, width, local.shape[1])

    vit_weights = gather_weights(join_weights([vit_fc1, vit_fc2, vit_out, merge_proj], 1280))

    per_group = grids.shape[0] // gx_count
    own_grids = lax.dynamic_slice_in_dim(grids, own_gx * per_group, per_group, 0)
    merge_slots = positions.shape[0] // gx_count
    sources, image_of, is_live = merge_sources(own_grids, merge_slots)
    holder = sources // share
    block = lax.rem(own_q + SUB - lax.rem(holder, SUB), SUB) * SUB + lax.rem(
        own_z + SUB - holder // SUB, SUB
    )
    source_column = (block * share + lax.rem(sources, share)).reshape(slots, 1)
    query_class = jnp.repeat(jnp.where(is_live, image_of, 0), 4).reshape(slots, 1)
    key_class = jnp.repeat(image_of, 4).reshape(1, slots)

    of_column = jnp.stack(gather_four("gz", patches))
    dec_local = join_weights([dec_fc1, dec_fc2, dec_qkv, dec_out], 1152)
    half = next_qkv.shape[0] // 2
    next_local = join_weights([next_qkv[:half], next_qkv[half:]], 6 * HEAD_DIM)
    of_column, dec_local, next_local, source_column, query_class, key_class, qkv_parts = (
        lax.optimization_barrier(
            (of_column, dec_local, next_local, source_column, query_class, key_class, vit_qkv)
        )
    )
    patches_full = [
        rows.reshape(SUB * share, width) for rows in gather_four("gq", of_column)
    ]
    dec_weights = gather_weights(dec_local)
    own_qkv = jnp.concatenate([qkv_parts[:, t] for t in range(3)], axis=1)
    qkv_weight = lax.all_gather(own_qkv, "gx", axis=0, tiled=True)

    row = lambda gain: gain.reshape(1, -1)
    group_rows = slots // SUB
    attended = call(
        vit_attention_body,
        shape(SUB * SUB, group_rows, LANES),
        (*patches_full, qkv_weight, row(vit_norm1), source_column, query_class, key_class),
        scratch=[
            pltpu.VMEM((slots, 3 * LANES), BF16),
            pltpu.VMEM((slots, 3 * LANES), BF16),
        ],
        flops=2 * slots * (width * 3 * LANES + slots * 5 * LANES),
        name="vit_attention",
    )
    attended, ids, next_local = lax.optimization_barrier((attended, text_ids, next_local))
    next_weights = lax.all_gather(next_local, ("gz", "gq", "gx"), axis=0, tiled=True).reshape(
        SUB * SUB, width // 2, 6 * HEAD_DIM
    )

    tokens = text_ids.shape[0]
    part = tokens // SUB
    block_width = SUB * HEAD_DIM
    block_lanes = 3 * LANES
    table_step = text_table.shape[0] // 5
    text_blocks = call(
        text_rows_body,
        [shape(tokens, block_lanes)] * SUB,
        (place, ids.reshape(tokens, 1), text_table),
        specs=[
            SMEM,
            pl.BlockSpec((tokens, 1), lambda i: (0, 0)),
            pl.BlockSpec((table_step, width), lambda i: (i, 0)),
        ],
        grid=(5,),
        out_specs=[pl.BlockSpec((tokens, block_lanes), lambda i: (0, 0))] * SUB,
        scratch=[pltpu.VMEM((tokens, width), F32)],
        flops=2 * tokens * text_table.shape[0] * width,
        name="text_rows",
    )
    own_sources = lax.dynamic_slice_in_dim(source_column, own_z * group_rows, group_rows, 0)
    stream = call(
        pick_rows_body,
        shape(group_rows, width),
        (own_sources, *patches_full),
        flops=2 * slots * group_rows * width,
        name="pick_rows",
    )

    def attention_output(attended, weights, at, name, beside=()):
        heads = exchange(("gz", "gq"), attended)
        heads, beside = lax.optimization_barrier((heads, beside))
        rows = heads.shape[1]
        return call(
            functools.partial(out_projection_body, at % LANES),
            shape(rows, block_lanes),
            (heads, *[weights] * SUB),
            specs=[whole(heads)]
            + [
                pl.BlockSpec(
                    (1, width, LANES), functools.partial(lambda i, z: (i, 0, at // LANES), i)
                )
                for i in range(SUB)
            ],
            grid=(1,),
            out_specs=pl.BlockSpec((rows, block_lanes), lambda z: (0, 0)),
            flops=2 * rows * width * SUB * LANES,
            name=name,
        ), beside

    def feed_forward(projected, stream, gain, weights, norm, name):
        rows = stream.shape[0]
        own = rows // SUB
        gathered = gather_four("gq", projected)
        hidden_width = vit_fc1.shape[1]
        outs = [shape(own, width)] * (SUB + 1)
        *pieces, mid = call(
            functools.partial(feed_forward_body, norm),
            outs,
            (place, *gathered, stream, gain, weights, weights),
            specs=[SMEM]
            + [whole(g) for g in gathered]
            + [whole(stream), whole(gain)]
            + [block_spec(width, hidden_width, at) for at in (0, 1)],
            grid=(SUB,),
            out_specs=[fixed(o) for o in outs],
            scratch=[
                pltpu.VMEM((SUB, rows, block_lanes), BF16),
                pltpu.VMEM((rows, width), BF16),
                pltpu.VMEM((rows, width), BF16),
                pltpu.VMEM((rows, width), F32),
            ],
            flops=4 * rows * width * SUB * hidden_width,
            name=name,
        )
        return [pieces[0]] + [shift_in("gq", pieces[k], k) for k in range(1, SUB)], mid

    text_parts = [text_blocks[0]] + [shift_in("gq", text_blocks[k], k) for k in (1, 3)]
    projected, (stream, text_parts) = attention_output(
        attended, vit_weights, 768, "vit_output", (stream, text_parts)
    )
    partials, mid = feed_forward(
        projected,
        stream,
        row(vit_norm2),
        vit_weights,
        layer_norm_rows,
        "vit_feed_forward",
    )

    gain_rows = jnp.tile(merge_norm, (share // 4, 1))
    merged = call(merge_norm_body, shape(share, width), (*partials, mid, gain_rows), name="merge_norm")
    gathered = gather_four("gq", merged)
    gathered, last_block = lax.optimization_barrier((gathered, text_blocks[2]))
    text_parts.append(shift_in("gq", last_block, 2))
    group_slots = group_rows // 4
    outs = shape(gx_count, group_slots, block_lanes)
    projected = call(
        merge_projection_body,
        outs,
        (place, *gathered, vit_weights, vit_weights),
        specs=[SMEM]
        + [whole(g) for g in gathered]
        + [block_spec(width, 2 * LANES, 3), block_spec(width, 2 * LANES, 4)],
        grid=(SUB,),
        out_specs=fixed(outs),
        scratch=[
            pltpu.VMEM((group_rows, width), BF16),
            pltpu.VMEM((group_rows, width), BF16),
            pltpu.VMEM((SUB, group_slots, LANES), BF16),
        ],
        flops=2 * group_rows * width * SUB * LANES,
        name="merge_projection",
    )
    all_projected = exchange("gx", projected).reshape(gx_count * group_slots, block_lanes)

    own_index = own_gx * tokens + jnp.arange(tokens, dtype=jnp.int32)
    is_image = jnp.any(positions[None, :] == own_index[:, None], axis=1).astype(F32)
    by_slot = lax.dynamic_index_in_dim(
        positions.reshape(gx_count, SUB, group_slots), own_z, 1, keepdims=False
    )
    placed = call(
        place_body,
        shape(tokens, block_lanes),
        (
            own_index.reshape(tokens, 1),
            is_image.reshape(tokens, 1),
            by_slot.reshape(1, -1),
            all_projected,
            *text_parts,
        ),
        flops=2 * tokens * by_slot.size * block_width,
        name="place_rows",
    )
    own_rows = jnp.sum(
        exchange("gz", placed.reshape(SUB, part, block_lanes)).astype(F32), axis=0
    ).astype(BF16)
    gathered = gather_four("gq", own_rows)

    outs = [shape(SUB, part, 3 * LANES), shape(part, width)]
    triple, embedded = call(
        dec_qkv_body,
        outs,
        (place, *gathered, row(dec_norm1), dec_weights),
        specs=[SMEM]
        + [whole(a) for a in (*gathered, row(dec_norm1))]
        + [block_spec(width, 3 * LANES, 2)],
        grid=(SUB,),
        out_specs=[pl.BlockSpec((1, part, 3 * LANES), lambda z: (z, 0, 0)), fixed(outs[1])],
        scratch=[pltpu.VMEM((SUB, part, block_lanes), BF16), pltpu.VMEM((part, width), BF16)],
        flops=2 * part * width * SUB * 3 * LANES,
        name="dec_qkv",
    )
    triple = exchange("gz", triple).reshape(tokens, 3 * LANES)
    key_values = triple[:, LANES:]
    near = jnp.stack(
        [key_values]
        + [
            lax.ppermute(
                key_values,
                "gx",
                [(2 * y + c, 2 * ((y + k) % SUB) + c) for y in range(SUB) for c in range(2)],
            )
            for k in range(1, SUB)
        ]
    )
    far = lax.ppermute(near, "gx", [(i, i ^ 1) for i in range(gx_count)])
    bounds = jnp.cumsum(lengths)
    all_index = jnp.arange(gx_count * tokens, dtype=jnp.int32).reshape(gx_count, tokens)
    request = jnp.sum((all_index[:, :, None] >= bounds).astype(jnp.int32), axis=2)
    own_request = jnp.sum((own_index[:, None] >= bounds).astype(jnp.int32), axis=1)
    tables = (place, triple, own_request.reshape(tokens, 1), own_index.reshape(tokens, 1), request)
    sums = [shape(tokens, LANES, dtype=F32), shape(tokens, 1, dtype=F32)]
    weighted, denominator = call(
        near_attention_body,
        sums,
        (*tables, near),
        specs=[SMEM] + [VMEM] * 5,
        flops=2 * tokens * tokens * gx_count * LANES,
        name="near_attention",
    )
    attended = call(
        far_attention_body,
        shape(SUB * SUB, part, LANES),
        (*tables, far, weighted, denominator),
        specs=[SMEM] + [VMEM] * 7,
        scratch=[pltpu.VMEM(sums[0].shape, F32), pltpu.VMEM(sums[1].shape, F32)],
        flops=2 * tokens * tokens * gx_count * LANES,
        name="far_attention",
    )
    projected, _ = attention_output(attended, dec_weights, 1032, "dec_output")
    partials, mid = feed_forward(
        projected, embedded, row(dec_norm2), dec_weights, rms_norm_rows, "dec_feed_forward"
    )
    own_tokens = mid.shape[0]

    at_once = 4
    finished = call(
        functools.partial(finish_body, half),
        shape(3, own_tokens, width),
        (*partials, mid, row(next_norm), *[next_weights] * at_once),
        specs=[whole(p) for p in (*partials, mid)]
        + [pl.BlockSpec((1, width), lambda z: (0, 0))]
        + [
            pl.BlockSpec(
                (1, width // 2, 6 * HEAD_DIM), functools.partial(lambda i, z: (at_once * z + i, 0, 0), i)
            )
            for i in range(at_once)
        ],
        grid=(SUB * SUB // at_once,),
        out_specs=pl.BlockSpec((3, own_tokens, width), lambda z: (0, 0, 0)),
        scratch=[
            pltpu.VMEM((2 * own_tokens, width // 2), BF16),
            pltpu.VMEM((SUB * SUB, own_tokens, 3 * HEAD_DIM), BF16),
        ],
        flops=2 * own_tokens * width * 3 * width,
        name="finish",
    )
    return finished.transpose(1, 0, 2)


def solution(mesh):
    gx_size = mesh.shape["gx"]
    cut = Mesh(mesh.devices.reshape(gx_size, SUB, SUB), ("gx", "gz", "gq"))
    gy = ("gz", "gq")
    flat = P("gx", gy)
    deep = P("gx", None, gy)
    placed = (
        P(("gx", *gy), None),
        P(),
        P("gx"),
        P(),
        P(),
        P(gy, None),
        P(),
        deep,
        flat,
        P(),
        flat,
        flat,
        P(),
        deep,
        P(),
        deep,
        flat,
        P(),
        flat,
        flat,
        P(),
        deep,
    )
    return jax.shard_map(
        per_device,
        mesh=cut,
        in_specs=placed,
        out_specs=P(("gx", *gy), None, None),
        check_vma=False,
    )
```
